128 devices in a mesh: tbl: 16 (over z, y), row: 8 (over x, core).
Axes of the slice: x: 4, y: 4, z: 4, core: 2. Of those that a mesh axis runs over, the one named last changes fastest.
Arguments:
- slab: bfloat16 [8192, 256], P(('tbl', 'row')), may hold values from -1.1953125 to 1.1953125
- counts: int32 [16384, 8192], P(None, ('tbl', 'row')), may hold values 0 or 1
- cross_down: bfloat16 [4096, 512], replicated, may hold values from -0.09375 to 0.09375
- cross_up: bfloat16 [512, 4096], replicated, may hold values from -0.25 to 0.25
- cross_bias: float32 [4096], replicated, may hold values from -3 to 3
- out_weight: float32 [4096], replicated, may hold values from -0.09375 to 0.09375
- labels: int32 [16384], P(('tbl', 'row')), may hold values 0 or 1
Outputs:
- grad_slab: float32 [8192, 256], P(('tbl', 'row'))
- grad_down: bfloat16 [4096, 512], P(('tbl', 'row'))
- grad_up: bfloat16 [512, 4096], P(None, ('tbl', 'row'))
- grad_bias: float32 [4096], P(('tbl', 'row'))
- grad_out: float32 [4096], P(('tbl', 'row'))
The draws below stay inside these ranges and needn't reach their ends.
All inputs are finite; a program needn't handle non-finite values. No bound on the sum of `counts` or of `labels` on one device may be relied on, other than what follows from the above.
Results may differ from the reference program's by a relative error of at most 0.022.
Values may be sent and summed in bfloat16 or wider, within the bound.
No kernel may reach another device: no remote copies, remote signals or barrier semaphores. Data moves between devices by JAX's collectives and lax.ppermute only.
A program may use at most 128 MiB of HBM per device.

```python
import jax
import jax.numpy as jnp
from jax import lax

EMBED = 256
TABLES = 16
RANK = 512
ROWS_DEV = 64
CROSS = 4096
BATCH = 16384
TOTAL_ROWS = 8192
N_TBL = 16
N_ROW = 8


def set_ends(drawn, own_key, smallest, largest):
    index_at = [jax.random.randint(jax.random.fold_in(own_key, axis), (), 0, length) for axis, length in enumerate(drawn.shape)]
    widest = drawn.shape.index(max(drawn.shape))
    next_to = index_at[:widest] + [(index_at[widest] + 1) % drawn.shape[widest]] + index_at[widest + 1:]
    return drawn.at[tuple(index_at)].set(smallest).at[tuple(next_to)].set(largest)


def steps_of(own_key, extent, cuts, smallest, top_value):
    loudness, own = 1.0, jax.random.fold_in(own_key, 6)
    for position, blocks in cuts:
        draws = jnp.exp(jax.random.uniform(jax.random.fold_in(own, position), (blocks,), jnp.float32, smallest / len(cuts), top_value / len(cuts)))
        loudness = loudness * jnp.repeat(draws, extent[position] // blocks).reshape([-1 if axis == position else 1 for axis in range(len(extent))])
    return loudness


def normal_values(stream_key, dims, deviation, limit, shards=(), held_as=jnp.bfloat16):
    result = deviation * jax.random.normal(stream_key, dims, jnp.float32)
    if shards:
        result = result * steps_of(stream_key, dims, shards, -0.22, 0.18)
    return jnp.clip(result, -limit, limit).astype(held_as)


def setup_inputs(seed: int = 0) -> dict:
    streams_of = jax.random.split(jax.random.key(seed), 8)
    slab = normal_values(streams_of[0], (TOTAL_ROWS, EMBED), 0.18, 1.1953125, ((0, 128),))
    counts = set_ends((jax.random.randint(streams_of[1], (BATCH, TOTAL_ROWS), 0, 32) < 1).astype(jnp.int32), jax.random.fold_in(streams_of[1], 1), 0, 1)
    cross_down = normal_values(streams_of[2], (CROSS, RANK), CROSS ** -0.5, 0.09375)
    cross_up = normal_values(streams_of[3], (RANK, CROSS), RANK ** -0.5, 0.25)
    cross_bias = normal_values(streams_of[4], (CROSS,), 0.5, 3.0, (), jnp.float32)
    out_weight = normal_values(streams_of[5], (CROSS,), CROSS ** -0.5, 0.09375, (), jnp.float32)
    labels = set_ends((jax.random.randint(streams_of[6], (BATCH,), 0, 2) < 1).astype(jnp.int32), jax.random.fold_in(streams_of[6], 1), 0, 1)
    return {"slab": slab, "counts": counts, "cross_down": cross_down, "cross_up": cross_up, "cross_bias": cross_bias, "out_weight": out_weight, "labels": labels}


def reference(slab, counts, cross_down, cross_up, cross_bias, out_weight, labels):
    per_group = TABLES // N_TBL
    row_span = N_ROW // per_group
    group_rows = ROWS_DEV * N_ROW
    owner_table = ((jnp.arange(N_ROW, dtype=jnp.int32) // row_span)[:, None] == jnp.arange(per_group, dtype=jnp.int32)[None, :]).astype(jnp.float32)

    def pool_group(group):
        start_row = (group * group_rows).astype(jnp.int32)
        counted = lax.dynamic_slice_in_dim(counts, start_row, group_rows, 1).astype(jnp.float32).reshape(BATCH, N_ROW, ROWS_DEV)
        slab_rows = lax.dynamic_slice_in_dim(slab, start_row, group_rows, 0).astype(jnp.float32).reshape(N_ROW, ROWS_DEV, EMBED)
        partial_value = jnp.einsum("bkr,kre->kbe", counted, slab_rows).astype(jnp.bfloat16)
        partial_value = lax.optimization_barrier(partial_value).astype(jnp.float32)
        return jnp.einsum("kbe,kt->bte", partial_value, owner_table).reshape(BATCH, per_group * EMBED)

    stacked = lax.map(pool_group, jnp.arange(N_TBL, dtype=jnp.int32))
    pooled = stacked.transpose(1, 0, 2).reshape(BATCH, CROSS).astype(jnp.bfloat16)
    pooled_full = pooled.astype(jnp.float32)
    squeezed = jnp.dot(pooled, cross_down, preferred_element_type=jnp.float32).astype(jnp.bfloat16)
    cross_gain = jnp.dot(squeezed, cross_up, preferred_element_type=jnp.float32) + cross_bias
    crossed = pooled_full * cross_gain + pooled_full
    logits = jnp.sum(crossed * out_weight, axis=1)
    grad_logits = jax.nn.sigmoid(logits) - labels.astype(jnp.float32)
    grad_out = jnp.sum(crossed * grad_logits[:, None], axis=0)
    grad_crossed = grad_logits[:, None] * out_weight
    grad_gain = grad_crossed * pooled_full
    grad_bias = jnp.sum(grad_gain, axis=0)
    gain_half = grad_gain.astype(jnp.bfloat16)
    grad_up = jnp.dot(squeezed.T, gain_half, preferred_element_type=jnp.float32).astype(jnp.bfloat16)
    grad_squeezed = jnp.dot(gain_half, cross_up.T, preferred_element_type=jnp.float32).astype(jnp.bfloat16)
    grad_down = jnp.dot(pooled.T, grad_squeezed, preferred_element_type=jnp.float32).astype(jnp.bfloat16)
    grad_pooled = (grad_crossed * (cross_gain + 1.0) + jnp.dot(grad_squeezed, cross_down.T, preferred_element_type=jnp.float32)).astype(jnp.bfloat16)

    def back_group(group):
        start_row = (group * group_rows).astype(jnp.int32)
        counted = lax.dynamic_slice_in_dim(counts, start_row, group_rows, 1).astype(jnp.float32).reshape(BATCH, N_ROW, ROWS_DEV)
        columns = lax.dynamic_slice_in_dim(grad_pooled, (group * per_group * EMBED).astype(jnp.int32), per_group * EMBED, 1).astype(jnp.float32).reshape(BATCH, per_group, EMBED)
        selected = jnp.einsum("bte,kt->kbe", columns, owner_table)
        return jnp.einsum("bkr,kbe->kre", counted, selected).reshape(group_rows, EMBED)

    grad_slab = lax.map(back_group, jnp.arange(N_TBL, dtype=jnp.int32)).reshape(TOTAL_ROWS, EMBED)
    return grad_slab, grad_down, grad_up, grad_bias, grad_out
```

```python
import jax
import jax.numpy as jnp
from jax import lax
from jax.experimental import pallas as pl
from jax.experimental.pallas import tpu as pltpu
from jax.sharding import Mesh
from jax.sharding import PartitionSpec as P


ALL = ("z", "y", "x", "c")
PLANE = ("y", "x", "c")
NZ, NY, NX, NC = 4, 4, 4, 2
NK = NX * NC
PEERS = NY * NK
OWN = 128
ROWS = 64
EMBED = 256
RANK = 512
COLS = 1024
SAMPLES = NZ * OWN
EXT = 16
PACK = 416
F32 = jnp.float32
BF16 = jnp.bfloat16


def dot(a, b, da, db):
    return lax.dot_general(a, b, (((da,), (db,)), ((), ())), preferred_element_type=F32)


def flat(z, y, x, c):
    return (((z % NZ) * NY + y % NY) * NX + x % NX) * NC + c % NC


def shift(value, dz=0, dy=0, dx=0, dc=0):
    pairs = [
        (flat(z, y, x, c), flat(z + dz, y + dy, x + dx, c + dc))
        for z in range(NZ)
        for y in range(NY)
        for x in range(NX)
        for c in range(NC)
    ]
    return lax.ppermute(value, ALL, pairs)


def pack_counts(z, counts_t, slab):
    def body(z_ref, b0, b1, b2, b3, slab_ref, out):
        for k in range(NK):
            for i, block in enumerate((b0, b1, b2, b3)):
                out[k, :, i * OWN : (i + 1) * OWN] = (
                    block[:, k * OWN : (k + 1) * OWN].astype(F32).astype(BF16)
                )
            out[k, :, SAMPLES:] = slab_ref[...]

    def block_of(i):
        return pl.BlockSpec((ROWS, NK * OWN), lambda y, z: (0, lax.rem(z[0] + i, NZ) * NY + y))

    return pl.pallas_call(
        body,
        grid_spec=pltpu.PrefetchScalarGridSpec(
            num_scalar_prefetch=1,
            grid=(NY,),
            in_specs=[block_of(i) for i in range(NZ)]
            + [pl.BlockSpec((ROWS, EMBED), lambda y, z: (0, 0))],
            out_specs=pl.BlockSpec((NK, ROWS, SAMPLES + EMBED), lambda y, z: (y, 0, 0)),
        ),
        out_shape=jax.ShapeDtypeStruct((PEERS, ROWS, SAMPLES + EMBED), BF16),
        name="pack_counts",
    )(z, counts_t, counts_t, counts_t, counts_t, slab)


def head_rows(w, bias):
    v = w * (1.0 + bias)
    high = v.astype(BF16).astype(F32)
    low = v - high
    at = lax.broadcasted_iota(jnp.int32, (EXT, COLS), 0)
    return jnp.where(at < 2, high, jnp.where(at == 2, low, 0.0)).astype(BF16)


def forward(z, arrived, down, up, w, bias):
    def body(z_ref, in_ref, down_ref, up_ref, w_ref, bias_ref, pooled_ref, *outs):
        for y in range(NY):
            rows = slice(y * 512, (y + 1) * 512)
            pooled_ref[y * EMBED : (y + 1) * EMBED, :] = dot(
                in_ref[rows, SAMPLES:], in_ref[rows, :SAMPLES], 0, 0
            ).astype(BF16)
        pooled = pooled_ref[...]
        w = w_ref[...]
        scaled_up = (up_ref[...].astype(F32) * w).astype(BF16)
        top = dot(down_ref[...], pooled, 0, 0).astype(BF16)
        bottom = dot(scaled_up, pooled, 1, 0).astype(BF16)
        head = dot(head_rows(w, bias_ref[...]), pooled, 1, 0)
        sums = head[0:1] + head[2:3]
        high = sums.astype(BF16).astype(F32)
        at = lax.broadcasted_iota(jnp.int32, (EXT, SAMPLES), 0)
        ext = jnp.where(at == 0, high, jnp.where(at == 1, sums - high, 0.0)).astype(BF16)
        for i, out in enumerate(outs):
            cols = slice(i * OWN, (i + 1) * OWN)
            out[0:RANK, :] = top[:, cols]
            out[RANK : 2 * RANK, :] = bottom[:, cols]
            out[2 * RANK :, :] = ext[:, cols]

    return pl.pallas_call(
        body,
        grid_spec=pltpu.PrefetchScalarGridSpec(
            num_scalar_prefetch=1,
            grid=(1,),
            in_specs=[
                pl.BlockSpec((PEERS * ROWS, SAMPLES + EMBED), lambda i, z: (0, 0)),
                pl.BlockSpec((COLS, RANK), lambda i, z: (z[0], 0)),
                pl.BlockSpec((RANK, COLS), lambda i, z: (0, z[0])),
                pl.BlockSpec((1, COLS), lambda i, z: (0, z[0])),
                pl.BlockSpec((1, COLS), lambda i, z: (0, z[0])),
            ],
            out_specs=[pl.BlockSpec((COLS, SAMPLES), lambda i, z: (0, 0))]
            + [pl.BlockSpec((2 * RANK + EXT, OWN), lambda i, z: (0, 0))] * NZ,
        ),
        out_shape=[jax.ShapeDtypeStruct((COLS, SAMPLES), BF16)]
        + [jax.ShapeDtypeStruct((2 * RANK + EXT, OWN), BF16)] * NZ,
        name="forward",
    )(z, arrived, down, up, w, bias)


def own_samples(parts, labels):
    def body(p0, p1, p2, p3, labels_ref, out):
        def total(rows):
            return sum((p[rows, :].astype(F32) for p in (p1, p2, p3)), p0[rows, :].astype(F32))

        squeezed = total(slice(0, RANK)).astype(BF16).astype(F32)
        other = total(slice(RANK, 2 * RANK))
        ext = total(slice(2 * RANK, 2 * RANK + EXT))
        logits = ext[0:1] + ext[1:2] + jnp.sum(squeezed * other, axis=0, keepdims=True)
        g = jax.nn.sigmoid(logits) - labels_ref[...].astype(F32)
        out[0:RANK, :] = (g * other).astype(BF16)
        out[RANK : 2 * RANK, :] = (g * squeezed).astype(BF16)
        high = g.astype(BF16).astype(F32)
        at = lax.broadcasted_iota(jnp.int32, (EXT, OWN), 0)
        rows = jnp.where((at == 0) | (at == 2), high, jnp.where(at == 1, g - high, 0.0))
        out[2 * RANK :, :] = rows.astype(BF16)

    return pl.pallas_call(
        body,
        out_shape=jax.ShapeDtypeStruct((2 * RANK + EXT, OWN), BF16),
        name="own_samples",
    )(*parts, labels)


def backward(place, blocks, pooled, arrived, down, up, w, bias):
    def body(place_ref, b0, b1, b2, b3, pooled_ref, in_ref, down_ref, up_ref, w_ref, bias_ref, mine, other):
        low_core = place_ref[1] == 0
        g = jnp.concatenate([b[...] for b in (b0, b1, b2, b3)], axis=1)
        w = w_ref[...]
        scaled_up = (up_ref[...].astype(F32) * w).astype(BF16)
        grad_pooled = (
            dot(down_ref[...], g[0:RANK], 1, 0)
            + dot(scaled_up, g[RANK : 2 * RANK], 0, 0)
            + dot(head_rows(w, bias_ref[...]), g[2 * RANK :], 0, 0)
        ).astype(BF16)

        def put(y, rows, value):
            pair = value.reshape(NX, NC, *value.shape[1:])
            even, odd = pair[:, 0], pair[:, 1]
            mine[y * NX : (y + 1) * NX, rows, :] = jnp.where(low_core, even, odd).astype(BF16)
            other[y * NX : (y + 1) * NX, rows, :] = jnp.where(low_core, odd, even).astype(BF16)

        for y in range(NY):
            of_table = slice(y * EMBED, (y + 1) * EMBED)
            slab = dot(in_ref[y * 512 : (y + 1) * 512, :SAMPLES], grad_pooled[of_table], 1, 1)
            for j in range(2):
                put(y, slice(j * ROWS, (j + 1) * ROWS), slab[:, j * 128 : (j + 1) * 128].reshape(NK, ROWS, 128))
            own = pooled_ref[of_table, :]
            both = dot(own, g[0 : 2 * RANK], 1, 1)
            for j in range(8):
                at = 128 + j * 32
                put(y, slice(at, at + 32), both[:, j * 128 : (j + 1) * 128].reshape(NK, 32, 128))
            sums = dot(own, jnp.concatenate([g[2 * RANK :], jnp.zeros((128 - EXT, SAMPLES), BF16)], axis=0), 1, 1)
            put(y, slice(384, 416), sums.reshape(NK, 32, 128))

    return pl.pallas_call(
        body,
        grid_spec=pltpu.PrefetchScalarGridSpec(
            num_scalar_prefetch=1,
            grid=(1,),
            in_specs=[pl.BlockSpec((2 * RANK + EXT, OWN), lambda i, z: (0, 0))] * NZ
            + [
                pl.BlockSpec((COLS, SAMPLES), lambda i, z: (0, 0)),
                pl.BlockSpec((PEERS * ROWS, SAMPLES + EMBED), lambda i, z: (0, 0)),
                pl.BlockSpec((COLS, RANK), lambda i, z: (z[0], 0)),
                pl.BlockSpec((RANK, COLS), lambda i, z: (0, z[0])),
                pl.BlockSpec((1, COLS), lambda i, z: (0, z[0])),
                pl.BlockSpec((1, COLS), lambda i, z: (0, z[0])),
            ],
            out_specs=[pl.BlockSpec((NY * NX, PACK, 128), lambda i, z: (0, 0, 0))] * 2,
        ),
        out_shape=[jax.ShapeDtypeStruct((NY * NX, PACK, 128), BF16)] * 2,
        name="backward",
    )(place, *blocks, pooled, arrived, down, up, w, bias)


def local(slab, counts, cross_down, cross_up, cross_bias, out_weight, labels):
    iz, iy, ix, ic = (lax.axis_index(a) for a in ALL)
    place = jnp.stack([iz, ic]).astype(jnp.int32)
    w_row = out_weight.reshape(1, -1)
    bias_row = cross_bias.reshape(1, -1)
    first = (((iz * NY + iy) * NX + ix) * NC + ic) * 32
    w_own = lax.dynamic_slice_in_dim(out_weight, first, 32)
    bias_own = lax.dynamic_slice_in_dim(cross_bias, first, 32)
    up_own = lax.dynamic_slice_in_dim(cross_up, first, 32, 1).T

    sent = pack_counts(place, counts.T, slab)
    arrived = lax.all_to_all(sent, PLANE, 0, 0, tiled=True).reshape(PEERS * ROWS, SAMPLES + EMBED)
    pooled, *chunks = forward(place, arrived, cross_down, cross_up, w_row, bias_row)
    parts = [chunks[0]] + [shift(chunks[i], dz=i) for i in range(1, NZ)]
    mine = own_samples(parts, labels.reshape(1, OWN))
    blocks = [mine] + [shift(mine, dz=-i) for i in range(1, NZ)]
    kept, given = backward(place, blocks, pooled, arrived, cross_down, cross_up, w_row, bias_row)
    paired = (kept.astype(F32) + shift(given, dc=1).astype(F32)).astype(BF16)
    shares = lax.all_to_all(paired, ("y", "x"), 0, 0, tiled=True)
    total = jnp.sum(shares.astype(F32), axis=0)
    grad_slab = jnp.concatenate([total[0:64], total[64:128]], axis=1)
    both = jnp.concatenate([total[128 + j * 32 : 160 + j * 32] for j in range(8)], axis=1)
    grad_down = both[:, :RANK].astype(BF16)
    product = both[:, RANK:]
    grad_up = (product * w_own[:, None]).astype(BF16).T
    sums = total[384:416, 0] + total[384:416, 1]
    grad_bias = w_own * sums
    grad_out = (1.0 + bias_own) * sums + jnp.sum(product * up_own.astype(F32), axis=1)
    return grad_slab, grad_down, grad_up, grad_bias, grad_out


def solution(mesh):
    torus = Mesh(mesh.devices.reshape(NZ, NY, NX, NC), ALL)
    return jax.shard_map(
        local,
        mesh=torus,
        in_specs=(P(ALL, None), P(None, ALL), P(), P(), P(), P(), P(ALL)),
        out_specs=(P(ALL, None), P(ALL, None), P(None, ALL), P(ALL), P(ALL)),
        check_vma=False,
    )
```

```python
import jax
import jax.numpy as jnp
from jax import lax
from jax.experimental import pallas as pl
from jax.experimental.pallas import tpu as pltpu
from jax.sharding import Mesh
from jax.sharding import PartitionSpec as P


ALL = ("z", "y", "x", "c")
PLANE = ("y", "x", "c")
NZ, NY, NX, NC = 4, 4, 4, 2
NK = NX * NC
PEERS = NY * NK
OWN = 128
ROWS = 64
EMBED = 256
RANK = 512
COLS = 1024
SAMPLES = NZ * OWN
EXT = 16
PACK = 416
PART = PACK // 2
HALF = EMBED // 2
F32 = jnp.float32
BF16 = jnp.bfloat16


def dot(a, b, da, db):
    return lax.dot_general(a, b, (((da,), (db,)), ((), ())), preferred_element_type=F32)


def flat(z, y, x, c):
    return (((z % NZ) * NY + y % NY) * NX + x % NX) * NC + c % NC


def shift(value, dz=0, dy=0, dx=0, dc=0):
    pairs = [
        (flat(z, y, x, c), flat(z + dz, y + dy, x + dx, c + dc))
        for z in range(NZ)
        for y in range(NY)
        for x in range(NX)
        for c in range(NC)
    ]
    return lax.ppermute(value, ALL, pairs)


def pack_counts(z, counts_t, slab):
    def body(z_ref, b0, b1, b2, b3, slab_ref, out):
        for k in range(NK):
            for i, block in enumerate((b0, b1, b2, b3)):
                out[k, :, i * OWN : (i + 1) * OWN] = (
                    block[:, k * OWN : (k + 1) * OWN].astype(F32).astype(BF16)
                )
            half = k % NC
            out[k, :, SAMPLES:] = slab_ref[:, half * HALF : (half + 1) * HALF]

    def block_of(i):
        return pl.BlockSpec((ROWS, NK * OWN), lambda y, z: (0, lax.rem(z[0] + i, NZ) * NY + y))

    return pl.pallas_call(
        body,
        grid_spec=pltpu.PrefetchScalarGridSpec(
            num_scalar_prefetch=1,
            grid=(NY,),
            in_specs=[block_of(i) for i in range(NZ)]
            + [pl.BlockSpec((ROWS, EMBED), lambda y, z: (0, 0))],
            out_specs=pl.BlockSpec((NK, ROWS, SAMPLES + HALF), lambda y, z: (y, 0, 0)),
        ),
        out_shape=jax.ShapeDtypeStruct((PEERS, ROWS, SAMPLES + HALF), BF16),
        name="pack_counts",
    )(z, counts_t, counts_t, counts_t, counts_t, slab)


def head_rows(w, bias):
    v = w * (1.0 + bias)
    high = v.astype(BF16).astype(F32)
    low = v - high
    at = lax.broadcasted_iota(jnp.int32, (EXT, COLS), 0)
    return jnp.where(at < 2, high, jnp.where(at == 2, low, 0.0)).astype(BF16)


def forward(place, arrived, other, down, up, w, bias):
    def body(place_ref, in_ref, other_ref, down_ref, up_ref, w_ref, bias_ref, pooled_ref, *outs):
        low_core = place_ref[3] == 0
        for y in range(NY):
            rows = slice(y * 512, (y + 1) * 512)
            own, partner = in_ref[rows, SAMPLES:], other_ref[rows, :]
            slab = jnp.concatenate(
                [jnp.where(low_core, own, partner), jnp.where(low_core, partner, own)], axis=1
            )
            pooled_ref[y * EMBED : (y + 1) * EMBED, :] = dot(
                slab, in_ref[rows, :SAMPLES], 0, 0
            ).astype(BF16)
        pooled = pooled_ref[...]
        w = w_ref[...]
        scaled_up = (up_ref[...].astype(F32) * w).astype(BF16)
        top = dot(down_ref[...], pooled, 0, 0).astype(BF16)
        bottom = dot(scaled_up, pooled, 1, 0).astype(BF16)
        head = dot(head_rows(w, bias_ref[...]), pooled, 1, 0)
        sums = head[0:1] + head[2:3]
        high = sums.astype(BF16).astype(F32)
        at = lax.broadcasted_iota(jnp.int32, (EXT, SAMPLES), 0)
        ext = jnp.where(at == 0, high, jnp.where(at == 1, sums - high, 0.0)).astype(BF16)
        for i, out in enumerate(outs):
            cols = slice(i * OWN, (i + 1) * OWN)
            out[0:RANK, :] = top[:, cols]
            out[RANK : 2 * RANK, :] = bottom[:, cols]
            out[2 * RANK :, :] = ext[:, cols]

    return pl.pallas_call(
        body,
        grid_spec=pltpu.PrefetchScalarGridSpec(
            num_scalar_prefetch=1,
            grid=(1,),
            in_specs=[
                pl.BlockSpec((PEERS * ROWS, SAMPLES + HALF), lambda i, z: (0, 0)),
                pl.BlockSpec((PEERS * ROWS, HALF), lambda i, z: (0, 0)),
                pl.BlockSpec((COLS, RANK), lambda i, z: (z[0], 0)),
                pl.BlockSpec((RANK, COLS), lambda i, z: (0, z[0])),
                pl.BlockSpec((1, COLS), lambda i, z: (0, z[0])),
                pl.BlockSpec((1, COLS), lambda i, z: (0, z[0])),
            ],
            out_specs=[pl.BlockSpec((COLS, SAMPLES), lambda i, z: (0, 0))]
            + [pl.BlockSpec((2 * RANK + EXT, OWN), lambda i, z: (0, 0))] * NZ,
        ),
        out_shape=[jax.ShapeDtypeStruct((COLS, SAMPLES), BF16)]
        + [jax.ShapeDtypeStruct((2 * RANK + EXT, OWN), BF16)] * NZ,
        name="forward",
    )(place, arrived, other, down, up, w, bias)


def own_samples(parts, labels):
    def body(p0, p1, p2, p3, labels_ref, out):
        def total(rows):
            return sum((p[rows, :].astype(F32) for p in (p1, p2, p3)), p0[rows, :].astype(F32))

        squeezed = total(slice(0, RANK)).astype(BF16).astype(F32)
        other = total(slice(RANK, 2 * RANK))
        ext = total(slice(2 * RANK, 2 * RANK + EXT))
        logits = ext[0:1] + ext[1:2] + jnp.sum(squeezed * other, axis=0, keepdims=True)
        g = jax.nn.sigmoid(logits) - labels_ref[...].astype(F32)
        out[0:RANK, :] = (g * other).astype(BF16)
        out[RANK : 2 * RANK, :] = (g * squeezed).astype(BF16)
        high = g.astype(BF16).astype(F32)
        at = lax.broadcasted_iota(jnp.int32, (EXT, OWN), 0)
        rows = jnp.where((at == 0) | (at == 2), high, jnp.where(at == 1, g - high, 0.0))
        out[2 * RANK :, :] = rows.astype(BF16)

    return pl.pallas_call(
        body,
        out_shape=jax.ShapeDtypeStruct((2 * RANK + EXT, OWN), BF16),
        name="own_samples",
    )(*parts, labels)


def backward(place, blocks, pooled, arrived, down, up, w, bias):
    def body(place_ref, b0, b1, b2, b3, pooled_ref, in_ref, down_ref, up_ref, w_ref, bias_ref, mine, other):
        low_core = place_ref[3] == 0
        g = jnp.concatenate([b[...] for b in (b0, b1, b2, b3)], axis=1)
        w = w_ref[...]
        scaled_up = (up_ref[...].astype(F32) * w).astype(BF16)
        grad_pooled = (
            dot(down_ref[...], g[0:RANK], 1, 0)
            + dot(scaled_up, g[RANK : 2 * RANK], 0, 0)
            + dot(head_rows(w, bias_ref[...]), g[2 * RANK :], 0, 0)
        ).astype(BF16)

        def put(y, rows, value):
            pair = value.reshape(NX, NC, *value.shape[1:])
            even, odd = pair[:, 0], pair[:, 1]
            mine[y * NX : (y + 1) * NX, rows, :] = jnp.where(low_core, even, odd).astype(BF16)
            other[y * NX : (y + 1) * NX, rows, :] = jnp.where(low_core, odd, even).astype(BF16)

        for y in range(NY):
            of_table = slice(y * EMBED, (y + 1) * EMBED)
            slab = dot(in_ref[y * 512 : (y + 1) * 512, :], grad_pooled[of_table], 1, 1)
            for j in range(2):
                put(y, slice(j * ROWS, (j + 1) * ROWS), slab[:, j * 128 : (j + 1) * 128].reshape(NK, ROWS, 128))
            own = pooled_ref[of_table, :]
            both = dot(own, g[0 : 2 * RANK], 1, 1)
            for j in range(8):
                at = 128 + j * 32
                put(y, slice(at, at + 32), both[:, j * 128 : (j + 1) * 128].reshape(NK, 32, 128))
            sums = dot(own, jnp.concatenate([g[2 * RANK :], jnp.zeros((128 - EXT, SAMPLES), BF16)], axis=0), 1, 1)
            put(y, slice(384, 416), sums.reshape(NK, 32, 128))

    return pl.pallas_call(
        body,
        grid_spec=pltpu.PrefetchScalarGridSpec(
            num_scalar_prefetch=1,
            grid=(1,),
            in_specs=[pl.BlockSpec((2 * RANK + EXT, OWN), lambda i, z: (0, 0))] * NZ
            + [
                pl.BlockSpec((COLS, SAMPLES), lambda i, z: (0, 0)),
                pl.BlockSpec((PEERS * ROWS, SAMPLES), lambda i, z: (0, 0)),
                pl.BlockSpec((COLS, RANK), lambda i, z: (z[0], 0)),
                pl.BlockSpec((RANK, COLS), lambda i, z: (0, z[0])),
                pl.BlockSpec((1, COLS), lambda i, z: (0, z[0])),
                pl.BlockSpec((1, COLS), lambda i, z: (0, z[0])),
            ],
            out_specs=[pl.BlockSpec((NY * NX, PACK, 128), lambda i, z: (0, 0, 0))] * 2,
        ),
        out_shape=[jax.ShapeDtypeStruct((NY * NX, PACK, 128), BF16)] * 2,
        name="backward",
    )(place, *blocks, pooled, arrived, down, up, w, bias)


def pair_sums(place, mine, partner):
    def body(place_ref, mine_ref, partner_ref, *outs):
        for d in range(4):
            to_x = lax.rem(place_ref[2] + d, NX)
            to_y = lax.rem(place_ref[1] + d, NY)
            for i in range(4):
                first = (i * NX + to_x, slice(0, PART))
                outs[d][i] = (mine_ref[first].astype(F32) + partner_ref[first].astype(F32)).astype(BF16)
                second = (to_y * NX + i, slice(PART, PACK))
                outs[4 + d][i] = (mine_ref[second].astype(F32) + partner_ref[second].astype(F32)).astype(BF16)

    whole = pl.BlockSpec((NY * NX, PACK, 128), lambda i, z: (0, 0, 0))
    return pl.pallas_call(
        body,
        grid_spec=pltpu.PrefetchScalarGridSpec(
            num_scalar_prefetch=1,
            grid=(1,),
            in_specs=[whole] * 2,
            out_specs=[pl.BlockSpec((4, PART, 128), lambda i, z: (0, 0, 0))] * 8,
        ),
        out_shape=[jax.ShapeDtypeStruct((4, PART, 128), BF16)] * 8,
        name="pair_sums",
    )(place, mine, partner)


def line_sums(place, over_x, over_y):
    def body(place_ref, *refs):
        ins, outs = refs[:8], refs[8:]
        for d in range(4):
            for side, at in ((0, lax.rem(place_ref[1] + d, NY)), (4, lax.rem(place_ref[2] + d, NX))):
                a, b, c, e = (ins[side + i][at].astype(F32) for i in range(4))
                outs[side + d][...] = ((a + b) + (c + e)).astype(BF16)

    return pl.pallas_call(
        body,
        grid_spec=pltpu.PrefetchScalarGridSpec(
            num_scalar_prefetch=1,
            grid=(1,),
            in_specs=[pl.BlockSpec((4, PART, 128), lambda i, z: (0, 0, 0))] * 8,
            out_specs=[pl.BlockSpec((PART, 128), lambda i, z: (0, 0))] * 8,
        ),
        out_shape=[jax.ShapeDtypeStruct((PART, 128), BF16)] * 8,
        name="line_sums",
    )(place, *over_x, *over_y)


def finish(place, firsts, seconds, up, w, bias):
    def body(place_ref, *refs):
        ins = refs[:8]
        up_ref, w_ref, bias_ref, slab_out, down_out, up_out, bias_out, out_out = refs[8:]

        def total(parts):
            a, b, c, e = (p[...].astype(F32) for p in parts)
            return (a + b) + (c + e)

        packed = jnp.concatenate([total(ins[:4]), total(ins[4:])], axis=0)
        slab_out[:, :128] = packed[0:ROWS]
        slab_out[:, 128:] = packed[ROWS : 2 * ROWS]
        both = [packed[128 + j * 32 : 160 + j * 32] for j in range(8)]
        for j in range(4):
            down_out[:, j * 128 : (j + 1) * 128] = both[j].astype(BF16)
        product = jnp.concatenate(both[4:], axis=1)
        offset = lax.rem(place_ref[2] * NC + place_ref[3], 4) * 32
        lane = lax.broadcasted_iota(jnp.int32, (32, 128), 1)
        row = lax.broadcasted_iota(jnp.int32, (32, 128), 0)
        own = lane == row + offset
        w_own = jnp.sum(jnp.where(own, w_ref[...], 0.0), axis=1, keepdims=True)
        bias_own = jnp.sum(jnp.where(own, bias_ref[...], 0.0), axis=1, keepdims=True)
        up_own = dot(jnp.where(own, 1.0, 0.0).astype(BF16), up_ref[...], 1, 1)
        up_out[...] = (product * w_own).astype(BF16)
        sums = jnp.sum(jnp.where(lane < 2, packed[384:416], 0.0), axis=1, keepdims=True)
        out = (1.0 + bias_own) * sums + jnp.sum(product * up_own, axis=1, keepdims=True)
        bias_out[...] = jnp.sum(jnp.where(lane == row, w_own * sums, 0.0), axis=0, keepdims=True)[:, :32]
        out_out[...] = jnp.sum(jnp.where(lane == row, out, 0.0), axis=0, keepdims=True)[:, :32]

    def strip(i, p):
        return (0, (p[0] * NY + p[1]) * 2 + lax.div(p[2] * NC + p[3], 4))

    def plain(i, p):
        return (0, 0)

    return pl.pallas_call(
        body,
        grid_spec=pltpu.PrefetchScalarGridSpec(
            num_scalar_prefetch=1,
            grid=(1,),
            in_specs=[pl.BlockSpec((PART, 128), plain)] * 8
            + [pl.BlockSpec((RANK, 128), strip), pl.BlockSpec((1, 128), strip), pl.BlockSpec((1, 128), strip)],
            out_specs=[
                pl.BlockSpec((ROWS, EMBED), plain),
                pl.BlockSpec((32, RANK), plain),
                pl.BlockSpec((32, RANK), plain),
                pl.BlockSpec((1, 32), plain),
                pl.BlockSpec((1, 32), plain),
            ],
        ),
        out_shape=[
            jax.ShapeDtypeStruct((ROWS, EMBED), F32),
            jax.ShapeDtypeStruct((32, RANK), BF16),
            jax.ShapeDtypeStruct((32, RANK), BF16),
            jax.ShapeDtypeStruct((1, 32), F32),
            jax.ShapeDtypeStruct((1, 32), F32),
        ],
        name="finish",
    )(place, *firsts, *seconds, up, w, bias)


def local(slab, counts, cross_down, cross_up, cross_bias, out_weight, labels):
    place = jnp.stack([lax.axis_index(a) for a in ALL]).astype(jnp.int32)
    w_row = out_weight.reshape(1, -1)
    bias_row = cross_bias.reshape(1, -1)

    sent = pack_counts(place, counts.T, slab)
    arrived = lax.all_to_all(sent, PLANE, 0, 0, tiled=True).reshape(PEERS * ROWS, SAMPLES + HALF)
    other = shift(arrived[:, SAMPLES:], dc=1)
    pooled, *chunks = forward(place, arrived, other, cross_down, cross_up, w_row, bias_row)
    parts = [chunks[0]] + [shift(chunks[i], dz=i) for i in range(1, NZ)]
    mine = own_samples(parts, labels.reshape(1, OWN))
    blocks = [mine] + [shift(mine, dz=-i) for i in range(1, NZ)]
    kept, given = backward(place, blocks, pooled, arrived, cross_down, cross_up, w_row, bias_row)
    halves = pair_sums(place, kept, shift(given, dc=1))
    over_x = [halves[0]] + [shift(halves[d], dx=d) for d in range(1, 4)]
    over_y = [halves[4]] + [shift(halves[4 + d], dy=d) for d in range(1, 4)]
    lines = line_sums(place, over_x, over_y)
    firsts = [lines[0]] + [shift(lines[d], dy=d) for d in range(1, 4)]
    seconds = [lines[4]] + [shift(lines[4 + d], dx=d) for d in range(1, 4)]
    grad_slab, grad_down, grad_up, grad_bias, grad_out = finish(
        place, firsts, seconds, cross_up, out_weight.reshape(1, -1), bias_row
    )
    return grad_slab, grad_down, grad_up.T, grad_bias.reshape(32), grad_out.reshape(32)


def solution(mesh):
    torus = Mesh(mesh.devices.reshape(NZ, NY, NX, NC), ALL)
    return jax.shard_map(
        local,
        mesh=torus,
        in_specs=(P(ALL, None), P(None, ALL), P(), P(), P(), P(), P(ALL)),
        out_specs=(P(ALL, None), P(ALL, None), P(None, ALL), P(ALL), P(ALL)),
        check_vma=False,
    )
```

```python
import jax
import jax.numpy as jnp
from jax import lax
from jax.experimental import pallas as pl
from jax.experimental.pallas import tpu as pltpu
from jax.sharding import Mesh
from jax.sharding import PartitionSpec as P


ALL = ("z", "y", "x", "c")
PLANE = ("y", "x", "c")
NZ, NY, NX, NC = 4, 4, 4, 2
NK = NX * NC
PEERS = NY * NK
OWN = 128
ROWS = 64
EMBED = 256
RANK = 512
COLS = 1024
SAMPLES = NZ * OWN
EXT = 16
PACK = 416
HALF = EMBED // 2
F32 = jnp.float32
BF16 = jnp.bfloat16


def dot(a, b, da, db):
    return lax.dot_general(a, b, (((da,), (db,)), ((), ())), preferred_element_type=F32)


def flat(z, y, x, c):
    return (((z % NZ) * NY + y % NY) * NX + x % NX) * NC + c % NC


def shift(value, dz=0, dy=0, dx=0, dc=0):
    pairs = [
        (flat(z, y, x, c), flat(z + dz, y + dy, x + dx, c + dc))
        for z in range(NZ)
        for y in range(NY)
        for x in range(NX)
        for c in range(NC)
    ]
    return lax.ppermute(value, ALL, pairs)


def near(value):
    return pltpu.with_memory_space_constraint(value, pltpu.VMEM)


def call(body, name, outs, args, specs=None, scratch=(), mib=24, cost=None):
    return pl.pallas_call(
        body,
        in_specs=specs or [pl.BlockSpec(memory_space=pltpu.VMEM)] * len(args),
        out_specs=[pl.BlockSpec(memory_space=pltpu.VMEM)] * len(outs),
        out_shape=outs,
        scratch_shapes=list(scratch),
        compiler_params=pltpu.CompilerParams(vmem_limit_bytes=mib << 20),
        cost_estimate=cost,
        name=name,
    )(*args)


IN_SMEM = pl.BlockSpec(memory_space=pltpu.SMEM)
IN_VMEM = pl.BlockSpec(memory_space=pltpu.VMEM)
IN_HBM = pl.BlockSpec(memory_space=pltpu.HBM)


def pack_counts(place, counts_t, slab):
    strip = NK * OWN

    def body(place_ref, counts_ref, slab_ref, out, held, sems):
        def copy(y, i):
            start = pl.multiple_of(lax.rem(place_ref[0] + i, NZ) * (NY * strip) + y * strip, strip)
            return pltpu.make_async_copy(
                counts_ref.at[:, pl.ds(start, strip)], held.at[y, i], sems.at[y, i]
            )

        for y in range(NY):
            for i in range(NZ):
                copy(y, i).start()
        for k in range(PEERS):
            half = k % NC
            out[k, :, SAMPLES:] = slab_ref[:, half * HALF : (half + 1) * HALF]
        for y in range(NY):
            for i in range(NZ):
                copy(y, i).wait()
                for k in range(NK):
                    out[y * NK + k, :, i * OWN : (i + 1) * OWN] = (
                        held[y, i, :, k * OWN : (k + 1) * OWN].astype(F32).astype(BF16)
                    )

    return call(
        body,
        "pack_counts",
        [pltpu.VMEM((PEERS, ROWS, SAMPLES + HALF), BF16)],
        (place, pltpu.with_memory_space_constraint(counts_t, pltpu.HBM), slab),
        [IN_SMEM, IN_HBM, IN_VMEM],
        [pltpu.VMEM((NY, NZ, ROWS, strip), jnp.int32), pltpu.SemaphoreType.DMA((NY, NZ))],
    )[0]


def prepare(place, down, up, w, bias):
    def body(place_ref, down_ref, up_ref, w_ref, bias_ref, rows_out, cols_out, own_out, up_out, down_s, up_s, w_s, bias_s, sems):
        start = pl.multiple_of(place_ref[0] * COLS, COLS)
        copies = [
            pltpu.make_async_copy(down_ref.at[pl.ds(start, COLS), :], down_s, sems.at[0]),
            pltpu.make_async_copy(up_ref.at[:, pl.ds(start, COLS)], up_s, sems.at[1]),
            pltpu.make_async_copy(w_ref.at[:, pl.ds(start, COLS)], w_s, sems.at[2]),
            pltpu.make_async_copy(bias_ref.at[:, pl.ds(start, COLS)], bias_s, sems.at[3]),
        ]
        for copy in copies:
            copy.start()
        for copy in copies:
            copy.wait()
        w = w_s[...]
        scaled_up = (up_s[...].astype(F32) * w).astype(BF16)
        rows_out[0:RANK, :] = down_s[...].T
        rows_out[RANK : 2 * RANK, :] = scaled_up
        v = w * (1.0 + bias_s[...])
        high = v.astype(BF16).astype(F32)
        at = lax.broadcasted_iota(jnp.int32, (EXT, COLS), 0)
        rows_out[2 * RANK :, :] = jnp.where(at < 2, high, jnp.where(at == 2, v - high, 0.0)).astype(BF16)
        cols_out[:, 0:RANK] = down_s[...]
        cols_out[:, RANK:] = scaled_up.T
        k = place_ref[2] * NC + place_ref[3]
        strip = pl.multiple_of((place_ref[1] * 2 + lax.div(k, 4)) * 128, 128)
        offset = lax.rem(k, 4) * 32
        lane = lax.broadcasted_iota(jnp.int32, (32, 128), 1)
        row = lax.broadcasted_iota(jnp.int32, (32, 128), 0)
        own = lane == row + offset
        w_own = jnp.sum(jnp.where(own, w_s[:, pl.ds(strip, 128)], 0.0), axis=1, keepdims=True)
        bias_own = jnp.sum(jnp.where(own, bias_s[:, pl.ds(strip, 128)], 0.0), axis=1, keepdims=True)
        own_out[...] = jnp.where(lane == 0, w_own, bias_own)
        up_out[...] = dot(jnp.where(own, 1.0, 0.0).astype(BF16), up_s[:, pl.ds(strip, 128)], 1, 1)

    return call(
        body,
        "prepare",
        [
            pltpu.VMEM((2 * RANK + EXT, COLS), BF16),
            pltpu.VMEM((COLS, 2 * RANK), BF16),
            pltpu.VMEM((32, 128), F32),
            pltpu.VMEM((32, RANK), F32),
        ],
        (place, *(pltpu.with_memory_space_constraint(v, pltpu.HBM) for v in (down, up, w, bias))),
        [IN_SMEM] + [IN_HBM] * 4,
        [
            pltpu.VMEM((COLS, RANK), BF16),
            pltpu.VMEM((RANK, COLS), BF16),
            pltpu.VMEM((1, COLS), F32),
            pltpu.VMEM((1, COLS), F32),
            pltpu.SemaphoreType.DMA((4,)),
        ],
        cost=pl.CostEstimate(flops=1 << 30, bytes_accessed=6 << 20, transcendentals=0),
    )


def forward(place, arrived, other, rows):
    def body(place_ref, in_ref, other_ref, rows_ref, pooled_ref, *outs):
        low_core = place_ref[3] == 0
        for y in range(NY):
            at = slice(y * 512, (y + 1) * 512)
            own, partner = in_ref[at, SAMPLES:], other_ref[at, :]
            slab = jnp.concatenate(
                [jnp.where(low_core, own, partner), jnp.where(low_core, partner, own)], axis=1
            )
            pooled_ref[y * EMBED : (y + 1) * EMBED, :] = dot(slab, in_ref[at, :SAMPLES], 0, 0).astype(BF16)
        pooled = pooled_ref[...]
        for part in range(4):
            at = slice(part * 256, (part + 1) * 256)
            product = dot(rows_ref[at, :], pooled, 1, 0).astype(BF16)
            for i, out in enumerate(outs):
                out[at, :] = product[:, i * OWN : (i + 1) * OWN]
        head = dot(rows_ref[2 * RANK :, :], pooled, 1, 0)
        sums = head[0:1] + head[2:3]
        high = sums.astype(BF16).astype(F32)
        at = lax.broadcasted_iota(jnp.int32, (EXT, SAMPLES), 0)
        ext = jnp.where(at == 0, high, jnp.where(at == 1, sums - high, 0.0)).astype(BF16)
        for i, out in enumerate(outs):
            out[2 * RANK :, :] = ext[:, i * OWN : (i + 1) * OWN]

    return call(
        body,
        "forward",
        [pltpu.VMEM((COLS, SAMPLES), BF16)] + [pltpu.VMEM((2 * RANK + EXT, OWN), BF16)] * NZ,
        (place, near(arrived), near(other), near(rows)),
        [IN_SMEM] + [IN_VMEM] * 3,
    )


def own_samples(parts, labels):
    def body(p0, p1, p2, p3, labels_ref, out):
        def total(rows):
            a, b, c, d = (p[rows, :].astype(F32) for p in (p0, p1, p2, p3))
            return (a + b) + (c + d)

        squeezed = total(slice(0, RANK)).astype(BF16).astype(F32)
        other = total(slice(RANK, 2 * RANK))
        ext = total(slice(2 * RANK, 2 * RANK + EXT))
        logits = ext[0:1] + ext[1:2] + jnp.sum(squeezed * other, axis=0, keepdims=True)
        g = jax.nn.sigmoid(logits) - labels_ref[...].astype(F32)
        out[0:RANK, :] = (g * other).astype(BF16)
        out[RANK : 2 * RANK, :] = (g * squeezed).astype(BF16)
        high = g.astype(BF16).astype(F32)
        at = lax.broadcasted_iota(jnp.int32, (EXT, OWN), 0)
        rows = jnp.where((at == 0) | (at == 2), high, jnp.where(at == 1, g - high, 0.0))
        out[2 * RANK :, :] = rows.astype(BF16)

    return call(
        body,
        "own_samples",
        [pltpu.VMEM((2 * RANK + EXT, OWN), BF16)],
        (*(near(p) for p in parts), labels),
    )[0]


def backward(place, blocks, pooled, arrived, rows, cols):
    def body(place_ref, b0, b1, b2, b3, pooled_ref, in_ref, rows_ref, cols_ref, mine, other):
        low_core = place_ref[3] == 0

        def put(targets, at, value):
            pair = value.astype(BF16).reshape(-1, NC, *value.shape[1:])
            even, odd = pair[:, 0], pair[:, 1]
            mine[targets, at, :] = jnp.where(low_core, even, odd)
            other[targets, at, :] = jnp.where(low_core, odd, even)

        g = jnp.concatenate([b[...] for b in (b0, b1, b2, b3)], axis=1)
        everyone = slice(0, NY * NX)
        for j in range(4):
            both = dot(pooled_ref[...], g[j * 256 : (j + 1) * 256], 1, 1)
            for h in range(2):
                at = 128 + (2 * j + h) * 32
                put(everyone, slice(at, at + 32), both[:, h * 128 : (h + 1) * 128].reshape(PEERS, 32, 128))
        ext = g[2 * RANK :]
        padded = jnp.concatenate([ext, jnp.zeros((128 - EXT, SAMPLES), BF16)], axis=0)
        put(everyone, slice(384, 416), dot(pooled_ref[...], padded, 1, 1).reshape(PEERS, 32, 128))
        for y in range(NY):
            table = slice(y * EMBED, (y + 1) * EMBED)
            grad_pooled = (
                dot(cols_ref[table, :], g[: 2 * RANK], 1, 0)
                + dot(rows_ref[2 * RANK :, table], ext, 0, 0)
            ).astype(BF16)
            slab = dot(in_ref[y * 512 : (y + 1) * 512, :SAMPLES], grad_pooled, 1, 1)
            for j in range(2):
                put(
                    slice(y * NX, (y + 1) * NX),
                    slice(j * ROWS, (j + 1) * ROWS),
                    slab[:, j * 128 : (j + 1) * 128].reshape(NK, ROWS, 128),
                )

    return call(
        body,
        "backward",
        [pltpu.VMEM((NY * NX, PACK, 128), BF16)] * 2,
        (place, *(near(b) for b in blocks), near(pooled), near(arrived), near(rows), near(cols)),
        [IN_SMEM] + [IN_VMEM] * 8,
    )


def pair_sums(mine, partner):
    def body(a, b, out):
        out[...] = (a[...].astype(F32) + b[...].astype(F32)).astype(BF16)

    return call(
        body, "pair_sums", [pltpu.VMEM((NY * NX, PACK, 128), BF16)], (near(mine), near(partner))
    )[0]


def finish(shares, own, up_own):
    def body(in_ref, own_ref, up_ref, slab_out, down_out, up_out, bias_out, out_out):
        def total(at):
            held = in_ref[0, at, :].astype(F32)
            for i in range(1, NY * NX):
                held = held + in_ref[i, at, :].astype(F32)
            return held

        slab_out[:, :128] = total(slice(0, ROWS))
        slab_out[:, 128:] = total(slice(ROWS, 2 * ROWS))
        both = [total(slice(128 + j * 32, 160 + j * 32)) for j in range(8)]
        for j in range(4):
            down_out[:, j * 128 : (j + 1) * 128] = both[j].astype(BF16)
        product = jnp.concatenate(both[4:], axis=1)
        w_own, bias_own = own_ref[:, 0:1], own_ref[:, 1:2]
        up_out[...] = (product * w_own).astype(BF16)
        lane = lax.broadcasted_iota(jnp.int32, (32, 128), 1)
        row = lax.broadcasted_iota(jnp.int32, (32, 128), 0)
        sums = jnp.sum(jnp.where(lane < 2, total(slice(384, 416)), 0.0), axis=1, keepdims=True)
        out = (1.0 + bias_own) * sums + jnp.sum(product * up_ref[...], axis=1, keepdims=True)
        bias_out[...] = jnp.sum(jnp.where(lane == row, w_own * sums, 0.0), axis=0, keepdims=True)[:, :32]
        out_out[...] = jnp.sum(jnp.where(lane == row, out, 0.0), axis=0, keepdims=True)[:, :32]

    return call(
        body,
        "finish",
        [
            jax.ShapeDtypeStruct((ROWS, EMBED), F32),
            jax.ShapeDtypeStruct((32, RANK), BF16),
            jax.ShapeDtypeStruct((32, RANK), BF16),
            jax.ShapeDtypeStruct((1, 32), F32),
            jax.ShapeDtypeStruct((1, 32), F32),
        ],
        (near(shares), near(own), near(up_own)),
    )


def local(slab, counts, cross_down, cross_up, cross_bias, out_weight, labels):
    place = jnp.stack([lax.axis_index(a) for a in ALL]).astype(jnp.int32)
    sent = pack_counts(place, counts.T, slab)
    arrived = lax.all_to_all(sent, PLANE, 0, 0, tiled=True).reshape(PEERS * ROWS, SAMPLES + HALF)
    rows, cols, own, up_own = prepare(
        place, cross_down, cross_up, out_weight.reshape(1, -1), cross_bias.reshape(1, -1)
    )
    other = shift(arrived[:, SAMPLES:], dc=1)
    pooled, *chunks = forward(place, arrived, other, rows)
    parts = [chunks[0]] + [shift(chunks[i], dz=i) for i in range(1, NZ)]
    mine = own_samples(parts, labels.reshape(1, OWN))
    blocks = [mine] + [shift(mine, dz=-i) for i in range(1, NZ)]
    kept, given = backward(place, blocks, pooled, arrived, rows, cols)
    paired = pair_sums(kept, shift(given, dc=1))
    shares = lax.all_to_all(paired, ("y", "x"), 0, 0, tiled=True)
    grad_slab, grad_down, grad_up, grad_bias, grad_out = finish(shares, own, up_own)
    return grad_slab, grad_down, grad_up.T, grad_bias.reshape(32), grad_out.reshape(32)


def solution(mesh):
    torus = Mesh(mesh.devices.reshape(NZ, NY, NX, NC), ALL)
    return jax.shard_map(
        local,
        mesh=torus,
        in_specs=(P(ALL, None), P(None, ALL), P(), P(), P(), P(), P(ALL)),
        out_specs=(P(ALL, None), P(ALL, None), P(None, ALL), P(ALL), P(ALL)),
        check_vma=False,
    )
```

```python
import jax
import jax.numpy as jnp
from jax import lax
from jax.experimental import pallas as pl
from jax.experimental.pallas import tpu as pltpu
from jax.sharding import Mesh
from jax.sharding import PartitionSpec as P


ALL = ("z", "y", "x", "c")
PLANE = ("y", "x", "c")
NZ, NY, NX, NC = 4, 4, 4, 2
NK = NX * NC
PEERS = NY * NK
OWN = 128
ROWS = 64
EMBED = 256
RANK = 512
COLS = 1024
SAMPLES = NZ * OWN
EXT = 16
PACK = 400
HALF = EMBED // 2
FAR = SAMPLES - OWN
F32 = jnp.float32
BF16 = jnp.bfloat16


def dot(a, b, da, db):
    return lax.dot_general(a, b, (((da,), (db,)), ((), ())), preferred_element_type=F32)


def flat(z, y, x, c):
    return (((z % NZ) * NY + y % NY) * NX + x % NX) * NC + c % NC


def shift(value, dz=0, dy=0, dx=0, dc=0):
    pairs = [
        (flat(z, y, x, c), flat(z + dz, y + dy, x + dx, c + dc))
        for z in range(NZ)
        for y in range(NY)
        for x in range(NX)
        for c in range(NC)
    ]
    return lax.ppermute(value, ALL, pairs)


def near(value):
    return pltpu.with_memory_space_constraint(value, pltpu.VMEM)


def far(value):
    return pltpu.with_memory_space_constraint(value, pltpu.HBM)


def call(body, outs, args, specs=None, scratch=(), mib=24, cost=None):
    return pl.pallas_call(
        body,
        in_specs=specs or [pl.BlockSpec(memory_space=pltpu.VMEM)] * len(args),
        out_specs=[pl.BlockSpec(memory_space=pltpu.VMEM)] * len(outs),
        out_shape=outs,
        scratch_shapes=list(scratch),
        compiler_params=pltpu.CompilerParams(vmem_limit_bytes=mib << 20),
        cost_estimate=cost,
    )(*args)


IN_SMEM = pl.BlockSpec(memory_space=pltpu.SMEM)
IN_VMEM = pl.BlockSpec(memory_space=pltpu.VMEM)
IN_HBM = pl.BlockSpec(memory_space=pltpu.HBM)


def strips(place_ref, counts_ref, held, sems, blocks):
    strip = NK * OWN

    def copy(y, n, i):
        start = pl.multiple_of(lax.rem(place_ref[0] + i, NZ) * (NY * strip) + y * strip, strip)
        return pltpu.make_async_copy(counts_ref.at[:, pl.ds(start, strip)], held.at[y, n], sems.at[y, n])

    return [(y, n, copy(y, n, i)) for y in range(NY) for n, i in enumerate(blocks)]


def strip_scratch(blocks):
    return [pltpu.VMEM((NY, blocks, ROWS, NK * OWN), jnp.int32), pltpu.SemaphoreType.DMA((NY, blocks))]


def unpack(strip_list, held, out):
    for y, n, copy in strip_list:
        copy.wait()
        for k in range(NK):
            out[y * NK + k, :, n * OWN : (n + 1) * OWN] = (
                held[y, n, :, k * OWN : (k + 1) * OWN].astype(F32).astype(BF16)
            )


def pack_counts(place, counts_t, slab):
    def body(place_ref, counts_ref, slab_ref, out, held, slab_s, sems, slab_sem):
        slab_copy = pltpu.make_async_copy(slab_ref, slab_s, slab_sem)
        slab_copy.start()
        copies = strips(place_ref, counts_ref, held, sems, range(1, NZ))
        for _, _, copy in copies:
            copy.start()
        slab_copy.wait()
        for k in range(PEERS):
            half = k % NC
            out[k, :, FAR:] = slab_s[:, half * HALF : (half + 1) * HALF]
        unpack(copies, held, out)

    held, sems = strip_scratch(NZ - 1)
    return call(
        body,
        [pltpu.VMEM((PEERS, ROWS, FAR + HALF), BF16)],
        (place, far(counts_t), far(slab)),
        [IN_SMEM, IN_HBM, IN_HBM],
        [held, pltpu.VMEM((ROWS, EMBED), BF16), sems, pltpu.SemaphoreType.DMA],
    )[0]


def prepare(place, down, up, w, bias):
    def body(place_ref, down_ref, up_ref, w_ref, bias_ref, rows_out, cols_out, own_out, up_out, down_s, up_s, w_s, bias_s, sems):
        start = pl.multiple_of(place_ref[0] * COLS, COLS)
        copies = [
            pltpu.make_async_copy(down_ref.at[pl.ds(start, COLS), :], down_s, sems.at[0]),
            pltpu.make_async_copy(up_ref.at[:, pl.ds(start, COLS)], up_s, sems.at[1]),
            pltpu.make_async_copy(w_ref.at[:, pl.ds(start, COLS)], w_s, sems.at[2]),
            pltpu.make_async_copy(bias_ref.at[:, pl.ds(start, COLS)], bias_s, sems.at[3]),
        ]
        for copy in copies:
            copy.start()
        for copy in copies:
            copy.wait()
        w = w_s[...]
        scaled_up = (up_s[...].astype(F32) * w).astype(BF16)
        rows_out[0:RANK, :] = down_s[...].T
        rows_out[RANK : 2 * RANK, :] = scaled_up
        v = w * (1.0 + bias_s[...])
        high = v.astype(BF16).astype(F32)
        at = lax.broadcasted_iota(jnp.int32, (EXT, COLS), 0)
        rows_out[2 * RANK :, :] = jnp.where(at < 2, high, jnp.where(at == 2, v - high, 0.0)).astype(BF16)
        cols_out[:, 0:RANK] = down_s[...]
        cols_out[:, RANK:] = scaled_up.T
        k = place_ref[2] * NC + place_ref[3]
        strip = pl.multiple_of((place_ref[1] * 2 + lax.div(k, 4)) * 128, 128)
        offset = lax.rem(k, 4) * 32
        lane = lax.broadcasted_iota(jnp.int32, (32, 128), 1)
        row = lax.broadcasted_iota(jnp.int32, (32, 128), 0)
        own = lane == row + offset
        w_own = jnp.sum(jnp.where(own, w_s[:, pl.ds(strip, 128)], 0.0), axis=1, keepdims=True)
        bias_own = jnp.sum(jnp.where(own, bias_s[:, pl.ds(strip, 128)], 0.0), axis=1, keepdims=True)
        place_own = (row + offset).astype(F32)
        own_out[...] = jnp.where(lane == 0, w_own, jnp.where(lane == 1, bias_own, place_own))
        up_out[...] = dot(jnp.where(own, 1.0, 0.0).astype(BF16), up_s[:, pl.ds(strip, 128)], 1, 1)

    return call(
        body,
        [
            pltpu.VMEM((2 * RANK + EXT, COLS), BF16),
            pltpu.VMEM((COLS, 2 * RANK), BF16),
            pltpu.VMEM((32, 128), F32),
            pltpu.VMEM((32, RANK), F32),
        ],
        (place, *(far(v) for v in (down, up, w, bias))),
        [IN_SMEM] + [IN_HBM] * 4,
        [
            pltpu.VMEM((COLS, RANK), BF16),
            pltpu.VMEM((RANK, COLS), BF16),
            pltpu.VMEM((1, COLS), F32),
            pltpu.VMEM((1, COLS), F32),
            pltpu.SemaphoreType.DMA((4,)),
        ],
        cost=pl.CostEstimate(flops=1 << 30, bytes_accessed=6 << 20, transcendentals=0),
    )


def head_of(rows_ref, pooled):
    head = dot(rows_ref[2 * RANK :, :], pooled, 1, 0)
    sums = head[0:1] + head[2:3]
    high = sums.astype(BF16).astype(F32)
    at = lax.broadcasted_iota(jnp.int32, (EXT, pooled.shape[1]), 0)
    return jnp.where(at == 0, high, jnp.where(at == 1, sums - high, 0.0)).astype(BF16)


def forward_far(place, arrived, other, rows, counts_t):
    def body(place_ref, in_ref, other_ref, rows_ref, counts_ref, pooled_ref, slab_out, sent, c1, c2, c3, held, sems):
        copies = strips(place_ref, counts_ref, held, sems, range(1))
        for _, _, copy in copies:
            copy.start()
        low_core = place_ref[3] == 0
        for y in range(NY):
            at = slice(y * 512, (y + 1) * 512)
            own, partner = in_ref[at, FAR:].T, other_ref[at, :].T
            slab = jnp.concatenate(
                [jnp.where(low_core, own, partner), jnp.where(low_core, partner, own)], axis=0
            )
            table = slice(y * EMBED, (y + 1) * EMBED)
            slab_out[table, :] = slab
            pooled_ref[table, :] = dot(slab, in_ref[at, :FAR], 1, 0).astype(BF16)
        pooled = pooled_ref[...]
        for part in range(4):
            at = slice(part * 256, (part + 1) * 256)
            product = dot(rows_ref[at, :], pooled, 1, 0).astype(BF16)
            for i, out in enumerate((c1, c2, c3)):
                out[at, :] = product[:, i * OWN : (i + 1) * OWN]
        ext = head_of(rows_ref, pooled)
        for i, out in enumerate((c1, c2, c3)):
            out[2 * RANK :, :] = ext[:, i * OWN : (i + 1) * OWN]
        unpack(copies, held, sent)

    return call(
        body,
        [
            pltpu.VMEM((COLS, FAR), BF16),
            pltpu.VMEM((COLS, 512), BF16),
            pltpu.VMEM((PEERS, ROWS, OWN), BF16),
        ]
        + [pltpu.VMEM((2 * RANK + EXT, OWN), BF16)] * (NZ - 1),
        (place, near(arrived), near(other), near(rows), far(counts_t)),
        [IN_SMEM] + [IN_VMEM] * 3 + [IN_HBM],
        strip_scratch(1),
        cost=pl.CostEstimate(flops=3 << 30, bytes_accessed=4 << 20, transcendentals=0),
    )


def forward_own(arrived, slab, rows):
    def body(in_ref, slab_ref, rows_ref, pooled_ref, out):
        for y in range(NY):
            table = slice(y * EMBED, (y + 1) * EMBED)
            pooled_ref[table, :] = dot(slab_ref[table, :], in_ref[y * 512 : (y + 1) * 512, :], 1, 0).astype(BF16)
        pooled = pooled_ref[...]
        out[0 : 2 * RANK, :] = dot(rows_ref[0 : 2 * RANK, :], pooled, 1, 0).astype(BF16)
        out[2 * RANK :, :] = head_of(rows_ref, pooled)

    return call(
        body,
        [pltpu.VMEM((COLS, OWN), BF16), pltpu.VMEM((2 * RANK + EXT, OWN), BF16)],
        (near(arrived), near(slab), near(rows)),
        cost=pl.CostEstimate(flops=1 << 30, bytes_accessed=1 << 20, transcendentals=0),
    )


def own_samples(parts, labels):
    def body(p0, p1, p2, p3, labels_ref, out):
        def total(rows):
            a, b, c, d = (p[rows, :].astype(F32) for p in (p0, p1, p2, p3))
            return (a + b) + (c + d)

        squeezed = total(slice(0, RANK)).astype(BF16).astype(F32)
        other = total(slice(RANK, 2 * RANK))
        ext = total(slice(2 * RANK, 2 * RANK + EXT))
        logits = ext[0:1] + ext[1:2] + jnp.sum(squeezed * other, axis=0, keepdims=True)
        g = jax.nn.sigmoid(logits) - labels_ref[...].astype(F32)
        out[0:RANK, :] = (g * other).astype(BF16)
        out[RANK : 2 * RANK, :] = (g * squeezed).astype(BF16)
        high = g.astype(BF16).astype(F32)
        at = lax.broadcasted_iota(jnp.int32, (EXT, OWN), 0)
        rows = jnp.where((at == 0) | (at == 2), high, jnp.where(at == 1, g - high, 0.0))
        out[2 * RANK :, :] = rows.astype(BF16)

    return call(body, [pltpu.VMEM((2 * RANK + EXT, OWN), BF16)], (*(near(p) for p in parts), labels))[0]


def weight_sums(pooled, g, both_of, sums_of):
    for j in range(4):
        both_of(j, dot(pooled, g[j * 256 : (j + 1) * 256], 1, 1))
    sums_of(dot(g[2 * RANK :], pooled, 1, 1))


def slab_sums(y, counts, g, rows_ref, cols_ref):
    table = slice(y * EMBED, (y + 1) * EMBED)
    grad_pooled = (
        dot(cols_ref[table, :], g[: 2 * RANK], 1, 0) + dot(rows_ref[2 * RANK :, table], g[2 * RANK :], 0, 0)
    ).astype(BF16)
    return dot(counts, grad_pooled, 1, 1)


def backward_first(block0, block3, pooled0, pooled_far, arrived0, arrived, rows, cols):
    def body(b0, b3, pooled0_ref, pooled_ref, in0_ref, in_ref, rows_ref, cols_ref, both_out, sums_out, slab_out):
        g = jnp.concatenate([b0[...], b3[...]], axis=1)
        pooled = jnp.concatenate([pooled0_ref[...], pooled_ref[:, 2 * OWN :]], axis=1)

        def both_of(j, value):
            both_out[:, j * 256 : (j + 1) * 256] = value

        def sums_of(value):
            sums_out[...] = value

        weight_sums(pooled, g, both_of, sums_of)
        for y in range(NY):
            at = slice(y * 512, (y + 1) * 512)
            counts = jnp.concatenate([in0_ref[at, :], in_ref[at, 2 * OWN : FAR]], axis=1)
            slab_out[at, :] = slab_sums(y, counts, g, rows_ref, cols_ref)

    return call(
        body,
        [
            pltpu.VMEM((COLS, 2 * RANK), F32),
            pltpu.VMEM((EXT, COLS), F32),
            pltpu.VMEM((PEERS * ROWS, EMBED), F32),
        ],
        tuple(near(v) for v in (block0, block3, pooled0, pooled_far, arrived0, arrived, rows, cols)),
        cost=pl.CostEstimate(flops=2 << 30, bytes_accessed=6 << 20, transcendentals=0),
    )


def put(low_core, mine, other, targets, at, value):
    pair = value.astype(BF16).reshape(-1, NC, *value.shape[1:])
    even, odd = pair[:, 0], pair[:, 1]
    mine[targets, at, :] = jnp.where(low_core, even, odd)
    other[targets, at, :] = jnp.where(low_core, odd, even)


EVERYONE = slice(0, NY * NX)


def backward_weights(place, block1, block2, pooled_far, both, sums):
    def body(place_ref, b1, b2, pooled_ref, both_ref, sums_ref, mine, other):
        low_core = place_ref[3] == 0
        g = jnp.concatenate([b1[...], b2[...]], axis=1)

        def both_of(j, value):
            for h in range(2):
                at = (2 * j + h) * 128
                held = both_ref[:, at : at + 128] + value[:, h * 128 : (h + 1) * 128]
                to = slice((2 * j + h) * 32, (2 * j + h + 1) * 32)
                put(low_core, mine, other, EVERYONE, to, held.reshape(PEERS, 32, 128))

        def sums_of(value):
            held = (value + sums_ref[...]).astype(BF16)
            for strip in range(8):
                row = held[:, strip * 128 : (strip + 1) * 128]
                for i in range(2):
                    mine[strip * 2 + i, 256:, :] = row
                    other[strip * 2 + i, 256:, :] = row

        weight_sums(pooled_ref[:, : 2 * OWN], g, both_of, sums_of)

    return call(
        body,
        [pltpu.VMEM((NY * NX, 272, 128), BF16)] * 2,
        (place, *(near(v) for v in (block1, block2, pooled_far, both, sums))),
        [IN_SMEM] + [IN_VMEM] * 5,
        cost=pl.CostEstimate(flops=1 << 30, bytes_accessed=4 << 20, transcendentals=0),
    )


def backward_slab(place, block1, block2, arrived, rows, cols, slab_first):
    def body(place_ref, b1, b2, in_ref, rows_ref, cols_ref, first_ref, mine, other):
        low_core = place_ref[3] == 0
        g = jnp.concatenate([b1[...], b2[...]], axis=1)
        for y in range(NY):
            at = slice(y * 512, (y + 1) * 512)
            slab = first_ref[at, :] + slab_sums(y, in_ref[at, : 2 * OWN], g, rows_ref, cols_ref)
            for j in range(2):
                put(
                    low_core,
                    mine,
                    other,
                    slice(y * NX, (y + 1) * NX),
                    slice(j * ROWS, (j + 1) * ROWS),
                    slab[:, j * 128 : (j + 1) * 128].reshape(NK, ROWS, 128),
                )

    return call(
        body,
        [pltpu.VMEM((NY * NX, 2 * ROWS, 128), BF16)] * 2,
        (place, *(near(v) for v in (block1, block2, arrived, rows, cols, slab_first))),
        [IN_SMEM] + [IN_VMEM] * 6,
        cost=pl.CostEstimate(flops=1 << 30, bytes_accessed=4 << 20, transcendentals=0),
    )


def pair_sums(slab, slab_partner, weights, weights_partner):
    def body(a, b, c, d, out):
        out[:, : 2 * ROWS, :] = (a[...].astype(F32) + b[...].astype(F32)).astype(BF16)
        out[:, 2 * ROWS :, :] = (c[...].astype(F32) + d[...].astype(F32)).astype(BF16)

    return call(
        body,
        [pltpu.VMEM((NY * NX, PACK, 128), BF16)],
        tuple(near(v) for v in (slab, slab_partner, weights, weights_partner)),
    )[0]


def finish(shares, own, up_own):
    def body(in_ref, own_ref, up_ref, slab_out, down_out, up_out, bias_out, out_out):
        def total(at):
            held = in_ref[0, at, :].astype(F32)
            for i in range(1, NY * NX):
                held = held + in_ref[i, at, :].astype(F32)
            return held

        slab_out[:, :128] = total(slice(0, ROWS))
        slab_out[:, 128:] = total(slice(ROWS, 2 * ROWS))
        both = [total(slice(128 + j * 32, 160 + j * 32)) for j in range(8)]
        for j in range(4):
            down_out[:, j * 128 : (j + 1) * 128] = both[j].astype(BF16)
        product = jnp.concatenate(both[4:], axis=1)
        w_own, bias_own = own_ref[:, 0:1], own_ref[:, 1:2]
        up_out[...] = (product * w_own).astype(BF16)
        lane = lax.broadcasted_iota(jnp.int32, (32, 128), 1)
        row = lax.broadcasted_iota(jnp.int32, (32, 128), 0)
        last = total(slice(384, 400))
        own = lane.astype(F32) == own_ref[:, 2:3]
        sums = jnp.sum(jnp.where(own, last[0:1] + last[1:2], 0.0), axis=1, keepdims=True)
        out = (1.0 + bias_own) * sums + jnp.sum(product * up_ref[...], axis=1, keepdims=True)
        bias_out[...] = jnp.sum(jnp.where(lane == row, w_own * sums, 0.0), axis=0, keepdims=True)[:, :32]
        out_out[...] = jnp.sum(jnp.where(lane == row, out, 0.0), axis=0, keepdims=True)[:, :32]

    return call(
        body,
        [
            jax.ShapeDtypeStruct((ROWS, EMBED), F32),
            jax.ShapeDtypeStruct((32, RANK), BF16),
            jax.ShapeDtypeStruct((32, RANK), BF16),
            jax.ShapeDtypeStruct((1, 32), F32),
            jax.ShapeDtypeStruct((1, 32), F32),
        ],
        (near(shares), near(own), near(up_own)),
    )


def local(slab, counts, cross_down, cross_up, cross_bias, out_weight, labels):
    place = jnp.stack([lax.axis_index(a) for a in ALL]).astype(jnp.int32)
    counts_t = counts.T
    rows, cols, own, up_own = prepare(
        place, cross_down, cross_up, out_weight.reshape(1, -1), cross_bias.reshape(1, -1)
    )
    sent = pack_counts(place, counts_t, slab)
    arrived = lax.all_to_all(sent, PLANE, 0, 0, tiled=True).reshape(PEERS * ROWS, FAR + HALF)
    other = shift(arrived[:, FAR:], dc=1)
    pooled, slab_t, sent0, *chunks = forward_far(place, arrived, other, rows, counts_t)
    parts = []
    for i in range(1, NZ):
        parts.append(shift(chunks[i - 1], dz=i))
    arrived0 = lax.all_to_all(sent0, PLANE, 0, 0, tiled=True).reshape(PEERS * ROWS, OWN)
    pooled0, chunk0 = forward_own(arrived0, slab_t, rows)
    block0 = own_samples([chunk0] + parts, labels.reshape(1, OWN))
    block1, block2, block3 = (shift(block0, dz=-i) for i in range(1, NZ))
    both, sums, slab_first = backward_first(block0, block3, pooled0, pooled, arrived0, arrived, rows, cols)
    weights, given = backward_weights(place, block1, block2, pooled, both, sums)
    weights_partner = shift(given, dc=1)
    slabs, given = backward_slab(place, block1, block2, arrived, rows, cols, slab_first)
    paired = pair_sums(slabs, shift(given, dc=1), weights, weights_partner)
    shares = lax.all_to_all(paired, ("y", "x"), 0, 0, tiled=True)
    grad_slab, grad_down, grad_up, grad_bias, grad_out = finish(shares, own, up_own)
    return grad_slab, grad_down, grad_up.T, grad_bias.reshape(32), grad_out.reshape(32)


def solution(mesh):
    torus = Mesh(mesh.devices.reshape(NZ, NY, NX, NC), ALL)
    return jax.shard_map(
        local,
        mesh=torus,
        in_specs=(P(ALL, None), P(None, ALL), P(), P(), P(), P(), P(ALL)),
        out_specs=(P(ALL, None), P(ALL, None), P(None, ALL), P(ALL), P(ALL)),
        check_vma=False,
    )
```

```python
import jax
import jax.numpy as jnp
from jax import lax
from jax.experimental import pallas as pl
from jax.experimental.pallas import tpu as pltpu
from jax.sharding import Mesh
from jax.sharding import PartitionSpec as P


ALL = ("z", "y", "x", "c")
PLANE = ("y", "x", "c")
NZ, NY, NX, NC = 4, 4, 4, 2
NK = NX * NC
PEERS = NY * NK
OWN = 128
ROWS = 64
EMBED = 256
RANK = 512
COLS = 1024
SAMPLES = NZ * OWN
EXT = 16
PACK = 400
HALF = EMBED // 2
FAR = SAMPLES - OWN
ORDER = (0, 2, 1, 3)
F32 = jnp.float32
BF16 = jnp.bfloat16


def dot(a, b, da, db):
    return lax.dot_general(a, b, (((da,), (db,)), ((), ())), preferred_element_type=F32)


def flat(z, y, x, c):
    return (((z % NZ) * NY + y % NY) * NX + x % NX) * NC + c % NC


def shift(value, dz=0, dy=0, dx=0, dc=0):
    pairs = [
        (flat(z, y, x, c), flat(z + dz, y + dy, x + dx, c + dc))
        for z in range(NZ)
        for y in range(NY)
        for x in range(NX)
        for c in range(NC)
    ]
    return lax.ppermute(value, ALL, pairs)


def near(value):
    return pltpu.with_memory_space_constraint(value, pltpu.VMEM)


def far(value):
    return pltpu.with_memory_space_constraint(value, pltpu.HBM)


def call(body, outs, args, specs=None, scratch=(), mib=24, cost=None):
    return pl.pallas_call(
        body,
        in_specs=specs or [pl.BlockSpec(memory_space=pltpu.VMEM)] * len(args),
        out_specs=[pl.BlockSpec(memory_space=pltpu.VMEM)] * len(outs),
        out_shape=outs,
        scratch_shapes=list(scratch),
        compiler_params=pltpu.CompilerParams(vmem_limit_bytes=mib << 20),
        cost_estimate=cost,
    )(*args)


IN_SMEM = pl.BlockSpec(memory_space=pltpu.SMEM)
IN_VMEM = pl.BlockSpec(memory_space=pltpu.VMEM)
IN_HBM = pl.BlockSpec(memory_space=pltpu.HBM)


def pack_counts(place, counts_t, slab):
    strip = NK * OWN

    def body(place_ref, counts_ref, slab_ref, out, held, slab_s, sems, slab_sem):
        def copy(y, n):
            z = lax.rem(place_ref[0] + ORDER[n], NZ)
            start = pl.multiple_of(z * (NY * strip) + y * strip, strip)
            return pltpu.make_async_copy(counts_ref.at[:, pl.ds(start, strip)], held.at[y, n], sems.at[y, n])

        slab_copy = pltpu.make_async_copy(slab_ref, slab_s, slab_sem)
        slab_copy.start()
        for y in range(NY):
            for n in range(NZ):
                copy(y, n).start()
        slab_copy.wait()
        for k in range(PEERS):
            half = k % NC
            out[k, :, SAMPLES:] = slab_s[:, half * HALF : (half + 1) * HALF]
        for y in range(NY):
            for n in range(NZ):
                copy(y, n).wait()
                for k in range(NK):
                    out[y * NK + k, :, n * OWN : (n + 1) * OWN] = (
                        held[y, n, :, k * OWN : (k + 1) * OWN].astype(F32).astype(BF16)
                    )

    return call(
        body,
        [pltpu.VMEM((PEERS, ROWS, SAMPLES + HALF), BF16)],
        (place, far(counts_t), far(slab)),
        [IN_SMEM, IN_HBM, IN_HBM],
        [
            pltpu.VMEM((NY, NZ, ROWS, strip), jnp.int32),
            pltpu.VMEM((ROWS, EMBED), BF16),
            pltpu.SemaphoreType.DMA((NY, NZ)),
            pltpu.SemaphoreType.DMA,
        ],
    )[0]


def prepare(place, down, up, w, bias):
    def body(place_ref, down_ref, up_ref, w_ref, bias_ref, rows_out, own_out, up_out, down_s, up_s, w_s, bias_s, sems):
        start = pl.multiple_of(place_ref[0] * COLS, COLS)
        copies = [
            pltpu.make_async_copy(down_ref.at[pl.ds(start, COLS), :], down_s, sems.at[0]),
            pltpu.make_async_copy(up_ref.at[:, pl.ds(start, COLS)], up_s, sems.at[1]),
            pltpu.make_async_copy(w_ref.at[:, pl.ds(start, COLS)], w_s, sems.at[2]),
            pltpu.make_async_copy(bias_ref.at[:, pl.ds(start, COLS)], bias_s, sems.at[3]),
        ]
        for copy in copies:
            copy.start()
        for copy in copies:
            copy.wait()
        w = w_s[...]
        scaled_up = (up_s[...].astype(F32) * w).astype(BF16)
        rows_out[0:RANK, :] = down_s[...].T
        rows_out[RANK : 2 * RANK, :] = scaled_up
        v = w * (1.0 + bias_s[...])
        high = v.astype(BF16).astype(F32)
        at = lax.broadcasted_iota(jnp.int32, (EXT, COLS), 0)
        rows_out[2 * RANK :, :] = jnp.where(at < 2, high, jnp.where(at == 2, v - high, 0.0)).astype(BF16)
        k = place_ref[2] * NC + place_ref[3]
        strip = pl.multiple_of((place_ref[1] * 2 + lax.div(k, 4)) * 128, 128)
        offset = lax.rem(k, 4) * 32
        lane = lax.broadcasted_iota(jnp.int32, (32, 128), 1)
        row = lax.broadcasted_iota(jnp.int32, (32, 128), 0)
        own = lane == row + offset
        w_own = jnp.sum(jnp.where(own, w_s[:, pl.ds(strip, 128)], 0.0), axis=1, keepdims=True)
        bias_own = jnp.sum(jnp.where(own, bias_s[:, pl.ds(strip, 128)], 0.0), axis=1, keepdims=True)
        place_own = (row + offset).astype(F32)
        own_out[...] = jnp.where(lane == 0, w_own, jnp.where(lane == 1, bias_own, place_own))
        up_out[...] = dot(jnp.where(own, 1.0, 0.0).astype(BF16), up_s[:, pl.ds(strip, 128)], 1, 1)

    return call(
        body,
        [
            pltpu.VMEM((2 * RANK + EXT, COLS), BF16),
            pltpu.VMEM((32, 128), F32),
            pltpu.VMEM((32, RANK), F32),
        ],
        (place, *(far(v) for v in (down, up, w, bias))),
        [IN_SMEM] + [IN_HBM] * 4,
        [
            pltpu.VMEM((COLS, RANK), BF16),
            pltpu.VMEM((RANK, COLS), BF16),
            pltpu.VMEM((1, COLS), F32),
            pltpu.VMEM((1, COLS), F32),
            pltpu.SemaphoreType.DMA((4,)),
        ],
        cost=pl.CostEstimate(flops=1 << 30, bytes_accessed=6 << 20, transcendentals=0),
    )


def head_of(rows_ref, pooled):
    head = dot(rows_ref[2 * RANK :, :], pooled, 1, 0)
    sums = head[0:1] + head[2:3]
    high = sums.astype(BF16).astype(F32)
    at = lax.broadcasted_iota(jnp.int32, (EXT, pooled.shape[1]), 0)
    return jnp.where(at == 0, high, jnp.where(at == 1, sums - high, 0.0)).astype(BF16)


def forward_far(place, arrived, other, rows):
    def body(place_ref, in_ref, other_ref, rows_ref, pooled_ref, slab_out, *outs):
        low_core = place_ref[3] == 0
        for y in range(NY):
            at = slice(y * 512, (y + 1) * 512)
            own, partner = in_ref[at, SAMPLES:].T, other_ref[at, :].T
            slab = jnp.concatenate(
                [jnp.where(low_core, own, partner), jnp.where(low_core, partner, own)], axis=0
            )
            table = slice(y * EMBED, (y + 1) * EMBED)
            slab_out[table, :] = slab
            pooled_ref[table, :] = dot(slab, in_ref[at, OWN:SAMPLES], 1, 0).astype(BF16)
        pooled = pooled_ref[...]
        for part in range(4):
            at = slice(part * 256, (part + 1) * 256)
            product = dot(rows_ref[at, :], pooled, 1, 0).astype(BF16)
            for i, out in enumerate(outs):
                out[at, :] = product[:, i * OWN : (i + 1) * OWN]
        ext = head_of(rows_ref, pooled)
        for i, out in enumerate(outs):
            out[2 * RANK :, :] = ext[:, i * OWN : (i + 1) * OWN]

    return call(
        body,
        [pltpu.VMEM((COLS, FAR), BF16), pltpu.VMEM((COLS, 512), BF16)]
        + [pltpu.VMEM((2 * RANK + EXT, OWN), BF16)] * (NZ - 1),
        (place, near(arrived), near(other), near(rows)),
        [IN_SMEM] + [IN_VMEM] * 3,
        cost=pl.CostEstimate(flops=3 << 30, bytes_accessed=4 << 20, transcendentals=0),
    )


def forward_own(arrived, slab, rows):
    def body(in_ref, slab_ref, rows_ref, pooled_ref, out):
        for y in range(NY):
            table = slice(y * EMBED, (y + 1) * EMBED)
            at = slice(y * 512, (y + 1) * 512)
            pooled_ref[table, :] = dot(slab_ref[table, :], in_ref[at, :OWN], 1, 0).astype(BF16)
        pooled = pooled_ref[...]
        out[0 : 2 * RANK, :] = dot(rows_ref[0 : 2 * RANK, :], pooled, 1, 0).astype(BF16)
        out[2 * RANK :, :] = head_of(rows_ref, pooled)

    return call(
        body,
        [pltpu.VMEM((COLS, OWN), BF16), pltpu.VMEM((2 * RANK + EXT, OWN), BF16)],
        (near(arrived), near(slab), near(rows)),
        cost=pl.CostEstimate(flops=1 << 30, bytes_accessed=1 << 20, transcendentals=0),
    )


def own_samples(parts, labels):
    def body(p0, p1, p2, p3, labels_ref, out):
        def total(rows):
            a, b, c, d = (p[rows, :].astype(F32) for p in (p0, p1, p2, p3))
            return (a + b) + (c + d)

        squeezed = total(slice(0, RANK)).astype(BF16).astype(F32)
        other = total(slice(RANK, 2 * RANK))
        ext = total(slice(2 * RANK, 2 * RANK + EXT))
        logits = ext[0:1] + ext[1:2] + jnp.sum(squeezed * other, axis=0, keepdims=True)
        g = jax.nn.sigmoid(logits) - labels_ref[...].astype(F32)
        out[0:RANK, :] = (g * other).astype(BF16)
        out[RANK : 2 * RANK, :] = (g * squeezed).astype(BF16)
        high = g.astype(BF16).astype(F32)
        at = lax.broadcasted_iota(jnp.int32, (EXT, OWN), 0)
        rows = jnp.where((at == 0) | (at == 2), high, jnp.where(at == 1, g - high, 0.0))
        out[2 * RANK :, :] = rows.astype(BF16)

    return call(body, [pltpu.VMEM((2 * RANK + EXT, OWN), BF16)], (*(near(p) for p in parts), labels))[0]


def by_sample(*blocks):
    return jnp.concatenate([b[...].T for b in blocks], axis=0)


def slab_sums(y, counts, g, rows_ref):
    table = slice(y * EMBED, (y + 1) * EMBED)
    return dot(counts, dot(g, rows_ref[:, table], 1, 0).astype(BF16), 1, 0)


def backward_first(block0, block2, pooled_own, pooled_far, arrived, rows):
    def body(b0, b2, own_ref, far_ref, in_ref, rows_ref, both_out, sums_out, slab_out):
        g = by_sample(b0, b2)
        pooled = jnp.concatenate([own_ref[...], far_ref[:, :OWN]], axis=1)
        for j in range(4):
            at = slice(j * 256, (j + 1) * 256)
            both_out[:, at] = dot(pooled, g[:, at], 1, 0)
        ext = jnp.concatenate([b0[2 * RANK :, :], b2[2 * RANK :, :]], axis=1)
        sums_out[...] = dot(ext, pooled, 1, 1)
        for y in range(NY):
            at = slice(y * 512, (y + 1) * 512)
            slab_out[at, :] = slab_sums(y, in_ref[at, : 2 * OWN], g, rows_ref)

    return call(
        body,
        [
            pltpu.VMEM((COLS, 2 * RANK), F32),
            pltpu.VMEM((EXT, COLS), F32),
            pltpu.VMEM((PEERS * ROWS, EMBED), F32),
        ],
        tuple(near(v) for v in (block0, block2, pooled_own, pooled_far, arrived, rows)),
        cost=pl.CostEstimate(flops=2 << 30, bytes_accessed=6 << 20, transcendentals=0),
    )


def put(low_core, mine, other, targets, at, value):
    pair = value.astype(BF16).reshape(-1, NC, *value.shape[1:])
    even, odd = pair[:, 0], pair[:, 1]
    mine[targets, at, :] = jnp.where(low_core, even, odd)
    other[targets, at, :] = jnp.where(low_core, odd, even)


EVERYONE = slice(0, NY * NX)


def backward_weights(place, block1, block3, pooled_far, both, sums):
    def body(place_ref, b1, b3, pooled_ref, both_ref, sums_ref, mine, other, g_out):
        low_core = place_ref[3] == 0
        g = by_sample(b1, b3)
        g_out[...] = g
        pooled = pooled_ref[:, OWN:]
        for j in range(4):
            value = dot(pooled, g[:, j * 256 : (j + 1) * 256], 1, 0)
            for h in range(2):
                at = (2 * j + h) * 128
                held = both_ref[:, at : at + 128] + value[:, h * 128 : (h + 1) * 128]
                to = slice((2 * j + h) * 32, (2 * j + h + 1) * 32)
                put(low_core, mine, other, EVERYONE, to, held.reshape(PEERS, 32, 128))
        ext = jnp.concatenate([b1[2 * RANK :, :], b3[2 * RANK :, :]], axis=1)
        held = (dot(ext, pooled, 1, 1) + sums_ref[...]).astype(BF16)
        for strip in range(8):
            row = held[:, strip * 128 : (strip + 1) * 128]
            for i in range(2):
                mine[strip * 2 + i, 256:, :] = row
                other[strip * 2 + i, 256:, :] = row

    return call(
        body,
        [pltpu.VMEM((NY * NX, 272, 128), BF16)] * 2 + [pltpu.VMEM((2 * OWN, 2 * RANK + EXT), BF16)],
        (place, *(near(v) for v in (block1, block3, pooled_far, both, sums))),
        [IN_SMEM] + [IN_VMEM] * 5,
        cost=pl.CostEstimate(flops=1 << 30, bytes_accessed=4 << 20, transcendentals=0),
    )


def backward_slab(place, g, arrived, rows, slab_first):
    def body(place_ref, g_ref, in_ref, rows_ref, first_ref, mine, other):
        low_core = place_ref[3] == 0
        g = g_ref[...]
        for y in range(NY):
            at = slice(y * 512, (y + 1) * 512)
            slab = first_ref[at, :] + slab_sums(y, in_ref[at, 2 * OWN : SAMPLES], g, rows_ref)
            for j in range(2):
                put(
                    low_core,
                    mine,
                    other,
                    slice(y * NX, (y + 1) * NX),
                    slice(j * ROWS, (j + 1) * ROWS),
                    slab[:, j * 128 : (j + 1) * 128].reshape(NK, ROWS, 128),
                )

    return call(
        body,
        [pltpu.VMEM((NY * NX, 2 * ROWS, 128), BF16)] * 2,
        (place, *(near(v) for v in (g, arrived, rows, slab_first))),
        [IN_SMEM] + [IN_VMEM] * 4,
        cost=pl.CostEstimate(flops=1 << 30, bytes_accessed=4 << 20, transcendentals=0),
    )


def pair_sums(slab, slab_partner, weights, weights_partner):
    def body(a, b, c, d, out):
        out[:, : 2 * ROWS, :] = (a[...].astype(F32) + b[...].astype(F32)).astype(BF16)
        out[:, 2 * ROWS :, :] = (c[...].astype(F32) + d[...].astype(F32)).astype(BF16)

    return call(
        body,
        [pltpu.VMEM((NY * NX, PACK, 128), BF16)],
        tuple(near(v) for v in (slab, slab_partner, weights, weights_partner)),
    )[0]


def finish(shares, own, up_own):
    def body(in_ref, own_ref, up_ref, slab_out, down_out, up_out, bias_out, out_out):
        def total(at):
            held = in_ref[0, at, :].astype(F32)
            for i in range(1, NY * NX):
                held = held + in_ref[i, at, :].astype(F32)
            return held

        slab_out[:, :128] = total(slice(0, ROWS))
        slab_out[:, 128:] = total(slice(ROWS, 2 * ROWS))
        both = [total(slice(128 + j * 32, 160 + j * 32)) for j in range(8)]
        for j in range(4):
            down_out[:, j * 128 : (j + 1) * 128] = both[j].astype(BF16)
        product = jnp.concatenate(both[4:], axis=1)
        w_own, bias_own = own_ref[:, 0:1], own_ref[:, 1:2]
        up_out[...] = (product * w_own).astype(BF16)
        lane = lax.broadcasted_iota(jnp.int32, (32, 128), 1)
        row = lax.broadcasted_iota(jnp.int32, (32, 128), 0)
        last = total(slice(384, 400))
        own = lane.astype(F32) == own_ref[:, 2:3]
        sums = jnp.sum(jnp.where(own, last[0:1] + last[1:2], 0.0), axis=1, keepdims=True)
        out = (1.0 + bias_own) * sums + jnp.sum(product * up_ref[...], axis=1, keepdims=True)
        bias_out[...] = jnp.sum(jnp.where(lane == row, w_own * sums, 0.0), axis=0, keepdims=True)[:, :32]
        out_out[...] = jnp.sum(jnp.where(lane == row, out, 0.0), axis=0, keepdims=True)[:, :32]

    return call(
        body,
        [
            jax.ShapeDtypeStruct((ROWS, EMBED), F32),
            jax.ShapeDtypeStruct((32, RANK), BF16),
            jax.ShapeDtypeStruct((32, RANK), BF16),
            jax.ShapeDtypeStruct((1, 32), F32),
            jax.ShapeDtypeStruct((1, 32), F32),
        ],
        (near(shares), near(own), near(up_own)),
    )


def local(slab, counts, cross_down, cross_up, cross_bias, out_weight, labels):
    place = jnp.stack([lax.axis_index(a) for a in ALL]).astype(jnp.int32)
    rows, own, up_own = prepare(
        place, cross_down, cross_up, out_weight.reshape(1, -1), cross_bias.reshape(1, -1)
    )
    sent = pack_counts(place, counts.T, slab)
    arrived = lax.all_to_all(sent, PLANE, 0, 0, tiled=True).reshape(PEERS * ROWS, SAMPLES + HALF)
    other = shift(arrived[:, SAMPLES:], dc=1)
    pooled, slab_t, *chunks = forward_far(place, arrived, other, rows)
    parts = []
    for i, chunk in zip(ORDER[1:], chunks):
        parts.append(shift(chunk, dz=i))
    pooled_own, chunk = forward_own(arrived, slab_t, rows)
    block0 = own_samples([chunk] + parts, labels.reshape(1, OWN))
    blocks = []
    for i in ORDER[1:]:
        blocks.append(shift(block0, dz=-i))
    block2, block1, block3 = blocks
    both, sums, slab_first = backward_first(block0, block2, pooled_own, pooled, arrived, rows)
    weights, given, g = backward_weights(place, block1, block3, pooled, both, sums)
    weights_partner = shift(given, dc=1)
    slabs, given = backward_slab(place, g, arrived, rows, slab_first)
    paired = pair_sums(slabs, shift(given, dc=1), weights, weights_partner)
    shares = lax.all_to_all(paired, ("y", "x"), 0, 0, tiled=True)
    grad_slab, grad_down, grad_up, grad_bias, grad_out = finish(shares, own, up_own)
    return grad_slab, grad_down, grad_up.T, grad_bias.reshape(32), grad_out.reshape(32)


def solution(mesh):
    torus = Mesh(mesh.devices.reshape(NZ, NY, NX, NC), ALL)
    return jax.shard_map(
        local,
        mesh=torus,
        in_specs=(P(ALL, None), P(None, ALL), P(), P(), P(), P(), P(ALL)),
        out_specs=(P(ALL, None), P(ALL, None), P(None, ALL), P(ALL), P(ALL)),
        check_vma=False,
    )
```

```python
import jax
import jax.numpy as jnp
from jax import lax
from jax.experimental import pallas as pl
from jax.experimental.pallas import tpu as pltpu
from jax.sharding import Mesh
from jax.sharding import PartitionSpec as P


ALL = ("z", "y", "x", "c")
PLANE = ("y", "x", "c")
NZ, NY, NX, NC = 4, 4, 4, 2
NK = NX * NC
PEERS = NY * NK
OWN = 128
ROWS = 64
EMBED = 256
RANK = 512
COLS = 1024
SAMPLES = NZ * OWN
EXT = 16
PACK = 400
HALF = EMBED // 2
ORDER = (0, 2, 1, 3)
F32 = jnp.float32
BF16 = jnp.bfloat16


def dot(a, b, da, db):
    return lax.dot_general(a, b, (((da,), (db,)), ((), ())), preferred_element_type=F32)


def flat(z, y, x, c):
    return (((z % NZ) * NY + y % NY) * NX + x % NX) * NC + c % NC


def shift(value, dz=0, dy=0, dx=0, dc=0):
    pairs = [
        (flat(z, y, x, c), flat(z + dz, y + dy, x + dx, c + dc))
        for z in range(NZ)
        for y in range(NY)
        for x in range(NX)
        for c in range(NC)
    ]
    return lax.ppermute(value, ALL, pairs)


def near(value):
    return pltpu.with_memory_space_constraint(value, pltpu.VMEM)


def far(value):
    return pltpu.with_memory_space_constraint(value, pltpu.HBM)


def call(body, outs, args, specs=None, scratch=(), mib=24, cost=None):
    return pl.pallas_call(
        body,
        in_specs=specs or [pl.BlockSpec(memory_space=pltpu.VMEM)] * len(args),
        out_specs=[pl.BlockSpec(memory_space=pltpu.VMEM)] * len(outs),
        out_shape=outs,
        scratch_shapes=list(scratch),
        compiler_params=pltpu.CompilerParams(vmem_limit_bytes=mib << 20),
        cost_estimate=cost,
    )(*args)


IN_SMEM = pl.BlockSpec(memory_space=pltpu.SMEM)
IN_VMEM = pl.BlockSpec(memory_space=pltpu.VMEM)
IN_HBM = pl.BlockSpec(memory_space=pltpu.HBM)


def pack_counts(place, counts_t, slab):
    strip = NK * OWN

    def body(place_ref, counts_ref, slab_ref, out, held, slab_s, sems, slab_sem):
        def copy(y, n):
            z = lax.rem(place_ref[0] + ORDER[n], NZ)
            start = pl.multiple_of(z * (NY * strip) + y * strip, strip)
            return pltpu.make_async_copy(counts_ref.at[:, pl.ds(start, strip)], held.at[y, n], sems.at[y, n])

        slab_copy = pltpu.make_async_copy(slab_ref, slab_s, slab_sem)
        slab_copy.start()
        for y in range(NY):
            for n in range(NZ):
                copy(y, n).start()
        slab_copy.wait()
        for k in range(PEERS):
            half = k % NC
            out[k, :, SAMPLES:] = slab_s[:, half * HALF : (half + 1) * HALF]
        for y in range(NY):
            for n in range(NZ):
                copy(y, n).wait()
                for k in range(NK):
                    out[y * NK + k, :, n * OWN : (n + 1) * OWN] = (
                        held[y, n, :, k * OWN : (k + 1) * OWN].astype(F32).astype(BF16)
                    )

    return call(
        body,
        [pltpu.VMEM((PEERS, ROWS, SAMPLES + HALF), BF16)],
        (place, far(counts_t), far(slab)),
        [IN_SMEM, IN_HBM, IN_HBM],
        [
            pltpu.VMEM((NY, NZ, ROWS, strip), jnp.int32),
            pltpu.VMEM((ROWS, EMBED), BF16),
            pltpu.SemaphoreType.DMA((NY, NZ)),
            pltpu.SemaphoreType.DMA,
        ],
    )[0]


def prepare(place, down, up, w, bias):
    def body(place_ref, down_ref, up_ref, w_ref, bias_ref, rows_out, own_out, up_out):
        start = pl.multiple_of(place_ref[0] * COLS, COLS)
        here = pl.ds(start, COLS)
        w = w_ref[:, here]
        for part in range(4):
            at = slice(part * 128, (part + 1) * 128)
            rows_out[at, :] = down_ref[here, at].T
        rows_out[RANK : 2 * RANK, :] = (up_ref[:, here].astype(F32) * w).astype(BF16)
        v = w * (1.0 + bias_ref[:, here])
        high = v.astype(BF16).astype(F32)
        at = lax.broadcasted_iota(jnp.int32, (EXT, COLS), 0)
        rows_out[2 * RANK :, :] = jnp.where(at < 2, high, jnp.where(at == 2, v - high, 0.0)).astype(BF16)
        k = place_ref[2] * NC + place_ref[3]
        strip = pl.ds(pl.multiple_of(start + (place_ref[1] * 2 + lax.div(k, 4)) * 128, 128), 128)
        offset = lax.rem(k, 4) * 32
        lane = lax.broadcasted_iota(jnp.int32, (32, 128), 1)
        row = lax.broadcasted_iota(jnp.int32, (32, 128), 0)
        own = lane == row + offset
        w_own = jnp.sum(jnp.where(own, w_ref[:, strip], 0.0), axis=1, keepdims=True)
        bias_own = jnp.sum(jnp.where(own, bias_ref[:, strip], 0.0), axis=1, keepdims=True)
        place_own = (row + offset).astype(F32)
        own_out[...] = jnp.where(lane == 0, w_own, jnp.where(lane == 1, bias_own, place_own))
        up_out[...] = dot(jnp.where(own, 1.0, 0.0).astype(BF16), up_ref[:, strip], 1, 1)

    return call(
        body,
        [
            pltpu.VMEM((2 * RANK + EXT, COLS), BF16),
            pltpu.VMEM((32, 128), F32),
            pltpu.VMEM((32, RANK), F32),
        ],
        (place, *(near(v) for v in (down, up, w, bias))),
        [IN_SMEM] + [IN_VMEM] * 4,
        cost=pl.CostEstimate(flops=1 << 29, bytes_accessed=6 << 20, transcendentals=0),
    )


def pool_half(arrived):
    def body(in_ref, pooled_ref):
        for y in range(NY):
            at = slice(y * 512, (y + 1) * 512)
            half = slice(y * HALF, (y + 1) * HALF)
            pooled_ref[half, :] = dot(in_ref[at, SAMPLES:].T, in_ref[at, :SAMPLES], 1, 0).astype(BF16)

    return call(
        body,
        [pltpu.VMEM((NY * HALF, SAMPLES), BF16)],
        (near(arrived),),
        cost=pl.CostEstimate(flops=1 << 29, bytes_accessed=2 << 20, transcendentals=0),
    )[0]


def head_of(rows_ref, pooled):
    head = dot(rows_ref[2 * RANK :, :], pooled, 1, 0)
    sums = head[0:1] + head[2:3]
    high = sums.astype(BF16).astype(F32)
    at = lax.broadcasted_iota(jnp.int32, (EXT, pooled.shape[1]), 0)
    return jnp.where(at == 0, high, jnp.where(at == 1, sums - high, 0.0)).astype(BF16)


def forward_far(place, arrived, other, half, rows):
    def body(place_ref, in_ref, other_ref, half_ref, rows_ref, pooled_ref, *outs):
        core = place_ref[3]
        for y in range(NY):
            at = slice(y * 512, (y + 1) * 512)
            mine = pl.multiple_of(y * EMBED + core * HALF, HALF)
            partners = pl.multiple_of(y * EMBED + (1 - core) * HALF, HALF)
            pooled_ref[pl.ds(mine, HALF), :] = half_ref[y * HALF : (y + 1) * HALF, :]
            pooled_ref[pl.ds(partners, HALF), :] = dot(
                other_ref[at, :].T, in_ref[at, :SAMPLES], 1, 0
            ).astype(BF16)
        pooled = pooled_ref[:, OWN:]
        for part in range(4):
            at = slice(part * 256, (part + 1) * 256)
            product = dot(rows_ref[at, :], pooled, 1, 0).astype(BF16)
            for i, out in enumerate(outs):
                out[at, :] = product[:, i * OWN : (i + 1) * OWN]
        ext = head_of(rows_ref, pooled)
        for i, out in enumerate(outs):
            out[2 * RANK :, :] = ext[:, i * OWN : (i + 1) * OWN]

    return call(
        body,
        [pltpu.VMEM((COLS, SAMPLES), BF16)] + [pltpu.VMEM((2 * RANK + EXT, OWN), BF16)] * (NZ - 1),
        (place, near(arrived), near(other), near(half), near(rows)),
        [IN_SMEM] + [IN_VMEM] * 4,
        cost=pl.CostEstimate(flops=3 << 30, bytes_accessed=4 << 20, transcendentals=0),
    )


def forward_own(pooled, rows):
    def body(pooled_ref, rows_ref, out):
        pooled = pooled_ref[:, :OWN]
        out[0 : 2 * RANK, :] = dot(rows_ref[0 : 2 * RANK, :], pooled, 1, 0).astype(BF16)
        out[2 * RANK :, :] = head_of(rows_ref, pooled)

    return call(
        body,
        [pltpu.VMEM((2 * RANK + EXT, OWN), BF16)],
        (near(pooled), near(rows)),
        cost=pl.CostEstimate(flops=1 << 30, bytes_accessed=1 << 20, transcendentals=0),
    )[0]


def own_samples(parts, labels):
    def body(p0, p1, p2, p3, labels_ref, out):
        def total(rows):
            a, b, c, d = (p[rows, :].astype(F32) for p in (p0, p1, p2, p3))
            return (a + b) + (c + d)

        squeezed = total(slice(0, RANK)).astype(BF16).astype(F32)
        other = total(slice(RANK, 2 * RANK))
        ext = total(slice(2 * RANK, 2 * RANK + EXT))
        logits = ext[0:1] + ext[1:2] + jnp.sum(squeezed * other, axis=0, keepdims=True)
        g = jax.nn.sigmoid(logits) - labels_ref[...].astype(F32)
        out[0:RANK, :] = (g * other).astype(BF16)
        out[RANK : 2 * RANK, :] = (g * squeezed).astype(BF16)
        high = g.astype(BF16).astype(F32)
        at = lax.broadcasted_iota(jnp.int32, (EXT, OWN), 0)
        rows = jnp.where((at == 0) | (at == 2), high, jnp.where(at == 1, g - high, 0.0))
        out[2 * RANK :, :] = rows.astype(BF16)

    return call(body, [pltpu.VMEM((2 * RANK + EXT, OWN), BF16)], (*(near(p) for p in parts), labels))[0]


def by_sample(*blocks):
    return jnp.concatenate([b[...].T for b in blocks], axis=0)


def grad_pooled_of(g, rows_ref):
    tables = [slice(y * EMBED, (y + 1) * EMBED) for y in range(NY)]
    return [dot(g, rows_ref[:, table], 1, 0).astype(BF16) for table in tables]


def backward_first(block0, block2, pooled, arrived, rows):
    def body(b0, b2, pooled_ref, in_ref, rows_ref, both_out, sums_out, slab_out):
        g = by_sample(b0, b2)
        products = grad_pooled_of(g, rows_ref)
        pooled = pooled_ref[:, : 2 * OWN]
        for j in range(4):
            at = slice(j * 256, (j + 1) * 256)
            both_out[:, at] = dot(pooled, g[:, at], 1, 0)
        ext = jnp.concatenate([b0[2 * RANK :, :], b2[2 * RANK :, :]], axis=1)
        sums_out[...] = dot(ext, pooled, 1, 1)
        for y, grad_pooled in enumerate(products):
            at = slice(y * 512, (y + 1) * 512)
            slab_out[at, :] = dot(in_ref[at, : 2 * OWN], grad_pooled, 1, 0)

    return call(
        body,
        [
            pltpu.VMEM((COLS, 2 * RANK), F32),
            pltpu.VMEM((EXT, COLS), F32),
            pltpu.VMEM((PEERS * ROWS, EMBED), F32),
        ],
        tuple(near(v) for v in (block0, block2, pooled, arrived, rows)),
        cost=pl.CostEstimate(flops=2 << 30, bytes_accessed=6 << 20, transcendentals=0),
    )


def put(low_core, mine, other, targets, at, value):
    pair = value.astype(BF16).reshape(-1, NC, *value.shape[1:])
    even, odd = pair[:, 0], pair[:, 1]
    mine[targets, at, :] = jnp.where(low_core, even, odd)
    other[targets, at, :] = jnp.where(low_core, odd, even)


EVERYONE = slice(0, NY * NX)


def backward_weights(place, block1, block3, pooled, both, sums):
    def body(place_ref, b1, b3, pooled_ref, both_ref, sums_ref, mine, other, g_out):
        low_core = place_ref[3] == 0
        g = by_sample(b1, b3)
        g_out[...] = g
        pooled = pooled_ref[:, 2 * OWN :]
        for j in range(4):
            value = dot(pooled, g[:, j * 256 : (j + 1) * 256], 1, 0)
            for h in range(2):
                at = (2 * j + h) * 128
                held = both_ref[:, at : at + 128] + value[:, h * 128 : (h + 1) * 128]
                to = slice((2 * j + h) * 32, (2 * j + h + 1) * 32)
                put(low_core, mine, other, EVERYONE, to, held.reshape(PEERS, 32, 128))
        ext = jnp.concatenate([b1[2 * RANK :, :], b3[2 * RANK :, :]], axis=1)
        held = (dot(ext, pooled, 1, 1) + sums_ref[...]).astype(BF16)
        for strip in range(8):
            row = held[:, strip * 128 : (strip + 1) * 128]
            for i in range(2):
                mine[strip * 2 + i, 256:, :] = row
                other[strip * 2 + i, 256:, :] = row

    return call(
        body,
        [pltpu.VMEM((NY * NX, 272, 128), BF16)] * 2 + [pltpu.VMEM((2 * OWN, 2 * RANK + EXT), BF16)],
        (place, *(near(v) for v in (block1, block3, pooled, both, sums))),
        [IN_SMEM] + [IN_VMEM] * 5,
        cost=pl.CostEstimate(flops=1 << 30, bytes_accessed=4 << 20, transcendentals=0),
    )


def backward_slab(place, g, arrived, rows, slab_first):
    def body(place_ref, g_ref, in_ref, rows_ref, first_ref, mine, other):
        low_core = place_ref[3] == 0
        for y, grad_pooled in enumerate(grad_pooled_of(g_ref[...], rows_ref)):
            at = slice(y * 512, (y + 1) * 512)
            slab = first_ref[at, :] + dot(in_ref[at, 2 * OWN : SAMPLES], grad_pooled, 1, 0)
            for j in range(2):
                put(
                    low_core,
                    mine,
                    other,
                    slice(y * NX, (y + 1) * NX),
                    slice(j * ROWS, (j + 1) * ROWS),
                    slab[:, j * 128 : (j + 1) * 128].reshape(NK, ROWS, 128),
                )

    return call(
        body,
        [pltpu.VMEM((NY * NX, 2 * ROWS, 128), BF16)] * 2,
        (place, *(near(v) for v in (g, arrived, rows, slab_first))),
        [IN_SMEM] + [IN_VMEM] * 4,
        cost=pl.CostEstimate(flops=1 << 30, bytes_accessed=4 << 20, transcendentals=0),
    )


def pair_sums(slab, slab_partner, weights, weights_partner):
    def body(a, b, c, d, out):
        out[:, : 2 * ROWS, :] = (a[...].astype(F32) + b[...].astype(F32)).astype(BF16)
        out[:, 2 * ROWS :, :] = (c[...].astype(F32) + d[...].astype(F32)).astype(BF16)

    return call(
        body,
        [pltpu.VMEM((NY * NX, PACK, 128), BF16)],
        tuple(near(v) for v in (slab, slab_partner, weights, weights_partner)),
    )[0]


def finish(shares, own, up_own):
    def body(in_ref, own_ref, up_ref, slab_out, down_out, up_out, bias_out, out_out):
        def total(at):
            held = in_ref[0, at, :].astype(F32)
            for i in range(1, NY * NX):
                held = held + in_ref[i, at, :].astype(F32)
            return held

        slab_out[:, :128] = total(slice(0, ROWS))
        slab_out[:, 128:] = total(slice(ROWS, 2 * ROWS))
        both = [total(slice(128 + j * 32, 160 + j * 32)) for j in range(8)]
        for j in range(4):
            down_out[:, j * 128 : (j + 1) * 128] = both[j].astype(BF16)
        product = jnp.concatenate(both[4:], axis=1)
        w_own, bias_own = own_ref[:, 0:1], own_ref[:, 1:2]
        up_out[...] = (product * w_own).astype(BF16)
        lane = lax.broadcasted_iota(jnp.int32, (32, 128), 1)
        row = lax.broadcasted_iota(jnp.int32, (32, 128), 0)
        last = total(slice(384, 400))
        own = lane.astype(F32) == own_ref[:, 2:3]
        sums = jnp.sum(jnp.where(own, last[0:1] + last[1:2], 0.0), axis=1, keepdims=True)
        out = (1.0 + bias_own) * sums + jnp.sum(product * up_ref[...], axis=1, keepdims=True)
        bias_out[...] = jnp.sum(jnp.where(lane == row, w_own * sums, 0.0), axis=0, keepdims=True)[:, :32]
        out_out[...] = jnp.sum(jnp.where(lane == row, out, 0.0), axis=0, keepdims=True)[:, :32]

    return call(
        body,
        [
            jax.ShapeDtypeStruct((ROWS, EMBED), F32),
            jax.ShapeDtypeStruct((32, RANK), BF16),
            jax.ShapeDtypeStruct((32, RANK), BF16),
            jax.ShapeDtypeStruct((1, 32), F32),
            jax.ShapeDtypeStruct((1, 32), F32),
        ],
        (near(shares), near(own), near(up_own)),
    )


def local(slab, counts, cross_down, cross_up, cross_bias, out_weight, labels):
    place = jnp.stack([lax.axis_index(a) for a in ALL]).astype(jnp.int32)
    rows, own, up_own = prepare(
        place, cross_down, cross_up, out_weight.reshape(1, -1), cross_bias.reshape(1, -1)
    )
    sent = pack_counts(place, counts.T, slab)
    arrived = lax.all_to_all(sent, PLANE, 0, 0, tiled=True).reshape(PEERS * ROWS, SAMPLES + HALF)
    other = shift(arrived[:, SAMPLES:], dc=1)
    half = pool_half(arrived)
    pooled, *chunks = forward_far(place, arrived, other, half, rows)
    parts = []
    for i, chunk in zip(ORDER[1:], chunks):
        parts.append(shift(chunk, dz=i))
    chunk = forward_own(pooled, rows)
    block0 = own_samples([chunk] + parts, labels.reshape(1, OWN))
    blocks = []
    for i in ORDER[1:]:
        blocks.append(shift(block0, dz=-i))
    block2, block1, block3 = blocks
    both, sums, slab_first = backward_first(block0, block2, pooled, arrived, rows)
    weights, given, g = backward_weights(place, block1, block3, pooled, both, sums)
    weights_partner = shift(given, dc=1)
    slabs, given = backward_slab(place, g, arrived, rows, slab_first)
    paired = pair_sums(slabs, shift(given, dc=1), weights, weights_partner)
    shares = lax.all_to_all(paired, ("y", "x"), 0, 0, tiled=True)
    grad_slab, grad_down, grad_up, grad_bias, grad_out = finish(shares, own, up_own)
    return grad_slab, grad_down, grad_up.T, grad_bias.reshape(32), grad_out.reshape(32)


def solution(mesh):
    torus = Mesh(mesh.devices.reshape(NZ, NY, NX, NC), ALL)
    return jax.shard_map(
        local,
        mesh=torus,
        in_specs=(P(ALL, None), P(None, ALL), P(), P(), P(), P(), P(ALL)),
        out_specs=(P(ALL, None), P(ALL, None), P(None, ALL), P(ALL), P(ALL)),
        check_vma=False,
    )
```

```python
import jax
import jax.numpy as jnp
from jax import lax
from jax.experimental import pallas as pl
from jax.experimental.pallas import tpu as pltpu
from jax.sharding import Mesh
from jax.sharding import PartitionSpec as P


ALL = ("z", "y", "x", "c")
PLANE = ("y", "x", "c")
NZ, NY, NX, NC = 4, 4, 4, 2
NK = NX * NC
PEERS = NY * NK
OWN = 128
ROWS = 64
EMBED = 256
RANK = 512
COLS = 1024
SAMPLES = NZ * OWN
EXT = 16
PACK = 400
HALF = EMBED // 2
ORDER = (0, 2, 1, 3)
F32 = jnp.float32
BF16 = jnp.bfloat16


def dot(a, b, da, db):
    return lax.dot_general(a, b, (((da,), (db,)), ((), ())), preferred_element_type=F32)


def flat(z, y, x, c):
    return (((z % NZ) * NY + y % NY) * NX + x % NX) * NC + c % NC


def shift(value, dz=0, dy=0, dx=0, dc=0):
    pairs = [
        (flat(z, y, x, c), flat(z + dz, y + dy, x + dx, c + dc))
        for z in range(NZ)
        for y in range(NY)
        for x in range(NX)
        for c in range(NC)
    ]
    return lax.ppermute(value, ALL, pairs)


def near(value):
    return pltpu.with_memory_space_constraint(value, pltpu.VMEM)


def far(value):
    return pltpu.with_memory_space_constraint(value, pltpu.HBM)


def call(body, outs, args, specs=None, scratch=(), mib=24, cost=None):
    return pl.pallas_call(
        body,
        in_specs=specs or [pl.BlockSpec(memory_space=pltpu.VMEM)] * len(args),
        out_specs=[pl.BlockSpec(memory_space=pltpu.VMEM)] * len(outs),
        out_shape=outs,
        scratch_shapes=list(scratch),
        compiler_params=pltpu.CompilerParams(vmem_limit_bytes=mib << 20),
        cost_estimate=cost,
    )(*args)


IN_SMEM = pl.BlockSpec(memory_space=pltpu.SMEM)
IN_VMEM = pl.BlockSpec(memory_space=pltpu.VMEM)
IN_HBM = pl.BlockSpec(memory_space=pltpu.HBM)


def pack_counts(place, counts_t, slab):
    group = 16

    def body(place_ref, counts_ref, slab_ref, out, held, slab_s, sems, slab_sem):
        def copy(n):
            rows = pl.ds(n * group, group)
            return pltpu.make_async_copy(counts_ref.at[rows, :], held.at[rows, :], sems.at[n])

        for n in range(ROWS // group):
            copy(n).start()
        slab_copy = pltpu.make_async_copy(slab_ref, slab_s, slab_sem)
        slab_copy.start()
        slab_copy.wait()
        for k in range(PEERS):
            half = k % NC
            out[k, :, SAMPLES:] = slab_s[:, half * HALF : (half + 1) * HALF]
        starts = [lax.rem(place_ref[0] + z, NZ) * (PEERS * OWN) for z in ORDER]
        for n in range(ROWS // group):
            copy(n).wait()
            rows = slice(n * group, (n + 1) * group)
            for i, start in enumerate(starts):
                for k in range(PEERS):
                    at = pl.ds(pl.multiple_of(start + k * OWN, OWN), OWN)
                    out[k, rows, i * OWN : (i + 1) * OWN] = held[rows, at].astype(F32).astype(BF16)

    return call(
        body,
        [pltpu.VMEM((PEERS, ROWS, SAMPLES + HALF), BF16)],
        (place, far(counts_t), far(slab)),
        [IN_SMEM, IN_HBM, IN_HBM],
        [
            pltpu.VMEM((ROWS, NZ * PEERS * OWN), jnp.int32),
            pltpu.VMEM((ROWS, EMBED), BF16),
            pltpu.SemaphoreType.DMA((ROWS // group,)),
            pltpu.SemaphoreType.DMA,
        ],
    )[0]


def prepare(place, down, up, w, bias):
    def body(place_ref, down_ref, up_ref, w_ref, bias_ref, rows_out):
        here = pl.ds(pl.multiple_of(place_ref[0] * COLS, COLS), COLS)
        w = w_ref[:, here]
        for part in range(4):
            at = slice(part * 128, (part + 1) * 128)
            rows_out[at, :] = down_ref[here, at].T
        rows_out[RANK : 2 * RANK, :] = (up_ref[:, here].astype(F32) * w).astype(BF16)
        v = w * (1.0 + bias_ref[:, here])
        high = v.astype(BF16).astype(F32)
        at = lax.broadcasted_iota(jnp.int32, (EXT, COLS), 0)
        rows_out[2 * RANK :, :] = jnp.where(at < 2, high, jnp.where(at == 2, v - high, 0.0)).astype(BF16)

    return call(
        body,
        [pltpu.VMEM((2 * RANK + EXT, COLS), BF16)],
        (place, *(near(v) for v in (down, up, w, bias))),
        [IN_SMEM] + [IN_VMEM] * 4,
        cost=pl.CostEstimate(flops=1 << 29, bytes_accessed=6 << 20, transcendentals=0),
    )[0]


def prepare_own(place, up, w, bias):
    def body(place_ref, up_ref, w_ref, bias_ref, own_out, up_out):
        k = place_ref[2] * NC + place_ref[3]
        start = place_ref[0] * COLS + (place_ref[1] * 2 + lax.div(k, 4)) * 128
        strip = pl.ds(pl.multiple_of(start, 128), 128)
        offset = lax.rem(k, 4) * 32
        lane = lax.broadcasted_iota(jnp.int32, (32, 128), 1)
        row = lax.broadcasted_iota(jnp.int32, (32, 128), 0)
        own = lane == row + offset
        w_own = jnp.sum(jnp.where(own, w_ref[:, strip], 0.0), axis=1, keepdims=True)
        bias_own = jnp.sum(jnp.where(own, bias_ref[:, strip], 0.0), axis=1, keepdims=True)
        place_own = (row + offset).astype(F32)
        own_out[...] = jnp.where(lane == 0, w_own, jnp.where(lane == 1, bias_own, place_own))
        up_out[...] = dot(jnp.where(own, 1.0, 0.0).astype(BF16), up_ref[:, strip], 1, 1)

    return call(
        body,
        [pltpu.VMEM((32, 128), F32), pltpu.VMEM((32, RANK), F32)],
        (place, *(near(v) for v in (up, w, bias))),
        [IN_SMEM] + [IN_VMEM] * 3,
        cost=pl.CostEstimate(flops=1 << 27, bytes_accessed=1 << 20, transcendentals=0),
    )


def pool_half(arrived):
    def body(in_ref, pooled_ref):
        for y in range(NY):
            at = slice(y * 512, (y + 1) * 512)
            half = slice(y * HALF, (y + 1) * HALF)
            pooled_ref[half, :] = dot(in_ref[at, SAMPLES:].T, in_ref[at, :SAMPLES], 1, 0).astype(BF16)

    return call(
        body,
        [pltpu.VMEM((NY * HALF, SAMPLES), BF16)],
        (near(arrived),),
        cost=pl.CostEstimate(flops=1 << 29, bytes_accessed=2 << 20, transcendentals=0),
    )[0]


def head_of(rows_ref, pooled):
    head = dot(rows_ref[2 * RANK :, :], pooled, 1, 0)
    sums = head[0:1] + head[2:3]
    high = sums.astype(BF16).astype(F32)
    at = lax.broadcasted_iota(jnp.int32, (EXT, pooled.shape[1]), 0)
    return jnp.where(at == 0, high, jnp.where(at == 1, sums - high, 0.0)).astype(BF16)


def products(rows_ref, pooled, outs):
    for part in range(4):
        at = slice(part * 256, (part + 1) * 256)
        product = dot(rows_ref[at, :], pooled, 1, 0).astype(BF16)
        for i, out in enumerate(outs):
            out[at, :] = product[:, i * OWN : (i + 1) * OWN]
    ext = head_of(rows_ref, pooled)
    for i, out in enumerate(outs):
        out[2 * RANK :, :] = ext[:, i * OWN : (i + 1) * OWN]


def forward_far(place, arrived, other, half, rows):
    def body(place_ref, in_ref, other_ref, half_ref, rows_ref, pooled_ref, out):
        core = place_ref[3]
        for y in range(NY):
            at = slice(y * 512, (y + 1) * 512)
            mine = pl.multiple_of(y * EMBED + core * HALF, HALF)
            partners = pl.multiple_of(y * EMBED + (1 - core) * HALF, HALF)
            pooled_ref[pl.ds(mine, HALF), :] = half_ref[y * HALF : (y + 1) * HALF, :]
            pooled_ref[pl.ds(partners, HALF), :] = dot(
                other_ref[at, :].T, in_ref[at, :SAMPLES], 1, 0
            ).astype(BF16)
        products(rows_ref, pooled_ref[:, OWN : 2 * OWN], (out,))

    return call(
        body,
        [pltpu.VMEM((COLS, SAMPLES), BF16), pltpu.VMEM((2 * RANK + EXT, OWN), BF16)],
        (place, near(arrived), near(other), near(half), near(rows)),
        [IN_SMEM] + [IN_VMEM] * 4,
        cost=pl.CostEstimate(flops=3 << 30, bytes_accessed=4 << 20, transcendentals=0),
    )


def forward_near(pooled, rows):
    def body(pooled_ref, rows_ref, *outs):
        products(rows_ref, pooled_ref[:, 2 * OWN :], outs)

    return call(
        body,
        [pltpu.VMEM((2 * RANK + EXT, OWN), BF16)] * 2,
        (near(pooled), near(rows)),
        cost=pl.CostEstimate(flops=1 << 30, bytes_accessed=2 << 20, transcendentals=0),
    )


def forward_own(pooled, rows):
    def body(pooled_ref, rows_ref, out):
        products(rows_ref, pooled_ref[:, :OWN], (out,))

    return call(
        body,
        [pltpu.VMEM((2 * RANK + EXT, OWN), BF16)],
        (near(pooled), near(rows)),
        cost=pl.CostEstimate(flops=1 << 30, bytes_accessed=1 << 20, transcendentals=0),
    )[0]


def own_samples(parts, labels):
    def body(p0, p1, p2, p3, labels_ref, out):
        def total(rows):
            a, b, c, d = (p[rows, :].astype(F32) for p in (p0, p1, p2, p3))
            return (a + b) + (c + d)

        squeezed = total(slice(0, RANK)).astype(BF16).astype(F32)
        other = total(slice(RANK, 2 * RANK))
        ext = total(slice(2 * RANK, 2 * RANK + EXT))
        logits = ext[0:1] + ext[1:2] + jnp.sum(squeezed * other, axis=0, keepdims=True)
        g = jax.nn.sigmoid(logits) - labels_ref[...].astype(F32)
        out[0:RANK, :] = (g * other).astype(BF16)
        out[RANK : 2 * RANK, :] = (g * squeezed).astype(BF16)
        high = g.astype(BF16).astype(F32)
        at = lax.broadcasted_iota(jnp.int32, (EXT, OWN), 0)
        rows = jnp.where((at == 0) | (at == 2), high, jnp.where(at == 1, g - high, 0.0))
        out[2 * RANK :, :] = rows.astype(BF16)

    return call(
        body, [pltpu.VMEM((2 * RANK + EXT, OWN), BF16)], (*(near(p) for p in parts), labels)
    )[0]


def by_sample(*blocks):
    return jnp.concatenate([b[...].T for b in blocks], axis=0)


def grad_pooled_of(g, rows_ref):
    tables = [slice(y * EMBED, (y + 1) * EMBED) for y in range(NY)]
    return [dot(g, rows_ref[:, table], 1, 0).astype(BF16) for table in tables]


def backward_first(block0, block2, pooled, arrived, rows):
    def body(b0, b2, pooled_ref, in_ref, rows_ref, both_out, sums_out, slab_out):
        g = by_sample(b0, b2)
        products = grad_pooled_of(g, rows_ref)
        pooled = pooled_ref[:, : 2 * OWN]
        for j in range(4):
            at = slice(j * 256, (j + 1) * 256)
            both_out[:, at] = dot(pooled, g[:, at], 1, 0)
        ext = jnp.concatenate([b0[2 * RANK :, :], b2[2 * RANK :, :]], axis=1)
        sums_out[...] = dot(ext, pooled, 1, 1)
        for y, grad_pooled in enumerate(products):
            at = slice(y * 512, (y + 1) * 512)
            slab_out[at, :] = dot(in_ref[at, : 2 * OWN], grad_pooled, 1, 0)

    return call(
        body,
        [
            pltpu.VMEM((COLS, 2 * RANK), F32),
            pltpu.VMEM((EXT, COLS), F32),
            pltpu.VMEM((PEERS * ROWS, EMBED), F32),
        ],
        tuple(near(v) for v in (block0, block2, pooled, arrived, rows)),
        cost=pl.CostEstimate(flops=2 << 30, bytes_accessed=6 << 20, transcendentals=0),
    )


def put(low_core, mine, other, targets, at, value):
    pair = value.astype(BF16).reshape(-1, NC, *value.shape[1:])
    even, odd = pair[:, 0], pair[:, 1]
    mine[targets, at, :] = jnp.where(low_core, even, odd)
    other[targets, at, :] = jnp.where(low_core, odd, even)


EVERYONE = slice(0, NY * NX)


def backward_weights(place, block1, block3, pooled, both, sums):
    def body(place_ref, b1, b3, pooled_ref, both_ref, sums_ref, mine, other, g_out):
        low_core = place_ref[3] == 0
        g = by_sample(b1, b3)
        g_out[...] = g
        pooled = pooled_ref[:, 2 * OWN :]
        for j in range(4):
            value = dot(pooled, g[:, j * 256 : (j + 1) * 256], 1, 0)
            for h in range(2):
                at = (2 * j + h) * 128
                held = both_ref[:, at : at + 128] + value[:, h * 128 : (h + 1) * 128]
                to = slice((2 * j + h) * 32, (2 * j + h + 1) * 32)
                put(low_core, mine, other, EVERYONE, to, held.reshape(PEERS, 32, 128))
        ext = jnp.concatenate([b1[2 * RANK :, :], b3[2 * RANK :, :]], axis=1)
        held = (dot(ext, pooled, 1, 1) + sums_ref[...]).astype(BF16)
        for strip in range(8):
            row = held[:, strip * 128 : (strip + 1) * 128]
            for i in range(2):
                mine[strip * 2 + i, 256:, :] = row
                other[strip * 2 + i, 256:, :] = row

    return call(
        body,
        [pltpu.VMEM((NY * NX, 272, 128), BF16)] * 2 + [pltpu.VMEM((2 * OWN, 2 * RANK + EXT), BF16)],
        (place, *(near(v) for v in (block1, block3, pooled, both, sums))),
        [IN_SMEM] + [IN_VMEM] * 5,
        cost=pl.CostEstimate(flops=1 << 30, bytes_accessed=4 << 20, transcendentals=0),
    )


def backward_slab(place, g, arrived, rows, slab_first):
    def body(place_ref, g_ref, in_ref, rows_ref, first_ref, mine, other):
        low_core = place_ref[3] == 0
        for y, grad_pooled in enumerate(grad_pooled_of(g_ref[...], rows_ref)):
            at = slice(y * 512, (y + 1) * 512)
            slab = first_ref[at, :] + dot(in_ref[at, 2 * OWN : SAMPLES], grad_pooled, 1, 0)
            for j in range(2):
                put(
                    low_core,
                    mine,
                    other,
                    slice(y * NX, (y + 1) * NX),
                    slice(j * ROWS, (j + 1) * ROWS),
                    slab[:, j * 128 : (j + 1) * 128].reshape(NK, ROWS, 128),
                )

    return call(
        body,
        [pltpu.VMEM((NY * NX, 2 * ROWS, 128), BF16)] * 2,
        (place, *(near(v) for v in (g, arrived, rows, slab_first))),
        [IN_SMEM] + [IN_VMEM] * 4,
        cost=pl.CostEstimate(flops=1 << 30, bytes_accessed=4 << 20, transcendentals=0),
    )


def pair_sums(slab, slab_partner, weights, weights_partner):
    def body(a, b, c, d, out):
        out[:, : 2 * ROWS, :] = (a[...].astype(F32) + b[...].astype(F32)).astype(BF16)
        out[:, 2 * ROWS :, :] = (c[...].astype(F32) + d[...].astype(F32)).astype(BF16)

    return call(
        body,
        [pltpu.VMEM((NY * NX, PACK, 128), BF16)],
        tuple(near(v) for v in (slab, slab_partner, weights, weights_partner)),
    )[0]


def finish(shares, own, up_own):
    def body(in_ref, own_ref, up_ref, slab_out, down_out, up_out, bias_out, out_out):
        def total(at):
            held = in_ref[0, at, :].astype(F32)
            for i in range(1, NY * NX):
                held = held + in_ref[i, at, :].astype(F32)
            return held

        slab_out[:, :128] = total(slice(0, ROWS))
        slab_out[:, 128:] = total(slice(ROWS, 2 * ROWS))
        both = [total(slice(128 + j * 32, 160 + j * 32)) for j in range(8)]
        for j in range(4):
            down_out[:, j * 128 : (j + 1) * 128] = both[j].astype(BF16)
        product = jnp.concatenate(both[4:], axis=1)
        w_own, bias_own = own_ref[:, 0:1], own_ref[:, 1:2]
        up_out[...] = (product * w_own).astype(BF16)
        lane = lax.broadcasted_iota(jnp.int32, (32, 128), 1)
        row = lax.broadcasted_iota(jnp.int32, (32, 128), 0)
        last = total(slice(384, 400))
        own = lane.astype(F32) == own_ref[:, 2:3]
        sums = jnp.sum(jnp.where(own, last[0:1] + last[1:2], 0.0), axis=1, keepdims=True)
        out = (1.0 + bias_own) * sums + jnp.sum(product * up_ref[...], axis=1, keepdims=True)
        bias_out[...] = jnp.sum(jnp.where(lane == row, w_own * sums, 0.0), axis=0, keepdims=True)[:, :32]
        out_out[...] = jnp.sum(jnp.where(lane == row, out, 0.0), axis=0, keepdims=True)[:, :32]

    return call(
        body,
        [
            jax.ShapeDtypeStruct((ROWS, EMBED), F32),
            jax.ShapeDtypeStruct((32, RANK), BF16),
            jax.ShapeDtypeStruct((32, RANK), BF16),
            jax.ShapeDtypeStruct((1, 32), F32),
            jax.ShapeDtypeStruct((1, 32), F32),
        ],
        (near(shares), near(own), near(up_own)),
    )


def local(slab, counts, cross_down, cross_up, cross_bias, out_weight, labels):
    place = jnp.stack([lax.axis_index(a) for a in ALL]).astype(jnp.int32)
    w_row, bias_row = out_weight.reshape(1, -1), cross_bias.reshape(1, -1)
    rows = prepare(place, cross_down, cross_up, w_row, bias_row)
    own, up_own = prepare_own(place, cross_up, w_row, bias_row)
    sent = pack_counts(place, counts.T, slab)
    arrived = lax.all_to_all(sent, PLANE, 0, 0, tiled=True).reshape(PEERS * ROWS, SAMPLES + HALF)
    other = shift(arrived[:, SAMPLES:], dc=1)
    half = pool_half(arrived)
    pooled, chunk2 = forward_far(place, arrived, other, half, rows)
    part2 = shift(chunk2, dz=2)
    chunk1, chunk3 = forward_near(pooled, rows)
    part1 = shift(chunk1, dz=1)
    part3 = shift(chunk3, dz=3)
    parts = [part2, part1, part3]
    chunk = forward_own(pooled, rows)
    block0 = own_samples([chunk] + parts, labels.reshape(1, OWN))
    blocks = []
    for i in ORDER[1:]:
        blocks.append(shift(block0, dz=-i))
    block2, block1, block3 = blocks
    both, sums, slab_first = backward_first(block0, block2, pooled, arrived, rows)
    weights, given, g = backward_weights(place, block1, block3, pooled, both, sums)
    weights_partner = shift(given, dc=1)
    slabs, given = backward_slab(place, g, arrived, rows, slab_first)
    paired = pair_sums(slabs, shift(given, dc=1), weights, weights_partner)
    shares = lax.all_to_all(paired, ("y", "x"), 0, 0, tiled=True)
    grad_slab, grad_down, grad_up, grad_bias, grad_out = finish(shares, own, up_own)
    return grad_slab, grad_down, grad_up.T, grad_bias.reshape(32), grad_out.reshape(32)


def solution(mesh):
    torus = Mesh(mesh.devices.reshape(NZ, NY, NX, NC), ALL)
    return jax.shard_map(
        local,
        mesh=torus,
        in_specs=(P(ALL, None), P(None, ALL), P(), P(), P(), P(), P(ALL)),
        out_specs=(P(ALL, None), P(ALL, None), P(None, ALL), P(ALL), P(ALL)),
        check_vma=False,
    )
```

```python
import jax
import jax.numpy as jnp
from jax import lax
from jax.experimental import pallas as pl
from jax.experimental.pallas import tpu as pltpu
from jax.sharding import Mesh
from jax.sharding import PartitionSpec as P


ALL = ("z", "y", "x", "c")
PLANE = ("y", "x", "c")
NZ, NY, NX, NC = 4, 4, 4, 2
NK = NX * NC
PEERS = NY * NK
OWN = 128
ROWS = 64
EMBED = 256
RANK = 512
COLS = 1024
SAMPLES = NZ * OWN
EXT = 16
PACK = 400
HALF = EMBED // 2
ORDER = (0, 2, 1, 3)
F32 = jnp.float32
BF16 = jnp.bfloat16


def dot(a, b, da, db):
    return lax.dot_general(a, b, (((da,), (db,)), ((), ())), preferred_element_type=F32)


def flat(z, y, x, c):
    return (((z % NZ) * NY + y % NY) * NX + x % NX) * NC + c % NC


def shift(value, dz=0, dy=0, dx=0, dc=0):
    pairs = [
        (flat(z, y, x, c), flat(z + dz, y + dy, x + dx, c + dc))
        for z in range(NZ)
        for y in range(NY)
        for x in range(NX)
        for c in range(NC)
    ]
    return lax.ppermute(value, ALL, pairs)


def near(value):
    return pltpu.with_memory_space_constraint(value, pltpu.VMEM)


def far(value):
    return pltpu.with_memory_space_constraint(value, pltpu.HBM)


def call(body, outs, args, specs=None, scratch=(), mib=24, cost=None):
    return pl.pallas_call(
        body,
        in_specs=specs or [pl.BlockSpec(memory_space=pltpu.VMEM)] * len(args),
        out_specs=[pl.BlockSpec(memory_space=pltpu.VMEM)] * len(outs),
        out_shape=outs,
        scratch_shapes=list(scratch),
        compiler_params=pltpu.CompilerParams(vmem_limit_bytes=mib << 20),
        cost_estimate=cost,
    )(*args)


IN_SMEM = pl.BlockSpec(memory_space=pltpu.SMEM)
IN_VMEM = pl.BlockSpec(memory_space=pltpu.VMEM)
IN_HBM = pl.BlockSpec(memory_space=pltpu.HBM)


def pack_counts(place, counts_t, slab):
    group = 16

    def body(place_ref, counts_ref, slab_ref, out, held, slab_s, sems, slab_sem):
        def copy(n):
            rows = pl.ds(n * group, group)
            return pltpu.make_async_copy(counts_ref.at[rows, :], held.at[rows, :], sems.at[n])

        for n in range(ROWS // group):
            copy(n).start()
        slab_copy = pltpu.make_async_copy(slab_ref, slab_s, slab_sem)
        slab_copy.start()
        slab_copy.wait()
        for k in range(PEERS):
            half = k % NC
            out[k, :, SAMPLES:] = slab_s[:, half * HALF : (half + 1) * HALF]
        starts = [lax.rem(place_ref[0] + z, NZ) * (PEERS * OWN) for z in ORDER]
        for n in range(ROWS // group):
            copy(n).wait()
            rows = slice(n * group, (n + 1) * group)
            for i, start in enumerate(starts):
                for k in range(PEERS):
                    at = pl.ds(pl.multiple_of(start + k * OWN, OWN), OWN)
                    out[k, rows, i * OWN : (i + 1) * OWN] = held[rows, at].astype(F32).astype(BF16)

    return call(
        body,
        [pltpu.VMEM((PEERS, ROWS, SAMPLES + HALF), BF16)],
        (place, far(counts_t), far(slab)),
        [IN_SMEM, IN_HBM, IN_HBM],
        [
            pltpu.VMEM((ROWS, NZ * PEERS * OWN), jnp.int32),
            pltpu.VMEM((ROWS, EMBED), BF16),
            pltpu.SemaphoreType.DMA((ROWS // group,)),
            pltpu.SemaphoreType.DMA,
        ],
    )[0]


def prepare(place, down, up, w, bias):
    def body(place_ref, down_ref, up_ref, w_ref, bias_ref, rows_out):
        here = pl.ds(pl.multiple_of(place_ref[0] * COLS, COLS), COLS)
        w = w_ref[:, here]
        for part in range(4):
            at = slice(part * 128, (part + 1) * 128)
            rows_out[at, :] = down_ref[here, at].T
        rows_out[RANK : 2 * RANK, :] = (up_ref[:, here].astype(F32) * w).astype(BF16)
        v = w * (1.0 + bias_ref[:, here])
        high = v.astype(BF16).astype(F32)
        at = lax.broadcasted_iota(jnp.int32, (EXT, COLS), 0)
        rows_out[2 * RANK :, :] = jnp.where(at < 2, high, jnp.where(at == 2, v - high, 0.0)).astype(BF16)

    return call(
        body,
        [pltpu.VMEM((2 * RANK + EXT, COLS), BF16)],
        (place, *(near(v) for v in (down, up, w, bias))),
        [IN_SMEM] + [IN_VMEM] * 4,
        cost=pl.CostEstimate(flops=1 << 29, bytes_accessed=6 << 20, transcendentals=0),
    )[0]


def prepare_own(place, up, w, bias):
    def body(place_ref, up_ref, w_ref, bias_ref, own_out, up_out):
        k = place_ref[2] * NC + place_ref[3]
        start = place_ref[0] * COLS + (place_ref[1] * 2 + lax.div(k, 4)) * 128
        strip = pl.ds(pl.multiple_of(start, 128), 128)
        offset = lax.rem(k, 4) * 32
        lane = lax.broadcasted_iota(jnp.int32, (32, 128), 1)
        row = lax.broadcasted_iota(jnp.int32, (32, 128), 0)
        own = lane == row + offset
        w_own = jnp.sum(jnp.where(own, w_ref[:, strip], 0.0), axis=1, keepdims=True)
        bias_own = jnp.sum(jnp.where(own, bias_ref[:, strip], 0.0), axis=1, keepdims=True)
        place_own = (row + offset).astype(F32)
        own_out[...] = jnp.where(lane == 0, w_own, jnp.where(lane == 1, bias_own, place_own))
        up_out[...] = dot(jnp.where(own, 1.0, 0.0).astype(BF16), up_ref[:, strip], 1, 1)

    return call(
        body,
        [pltpu.VMEM((32, 128), F32), pltpu.VMEM((32, RANK), F32)],
        (place, *(near(v) for v in (up, w, bias))),
        [IN_SMEM] + [IN_VMEM] * 3,
        cost=pl.CostEstimate(flops=1 << 27, bytes_accessed=1 << 20, transcendentals=0),
    )


def pool_half(arrived):
    def body(in_ref, pooled_ref):
        for y in range(NY):
            at = slice(y * 512, (y + 1) * 512)
            half = slice(y * HALF, (y + 1) * HALF)
            pooled_ref[half, :] = dot(in_ref[at, SAMPLES:].T, in_ref[at, :SAMPLES], 1, 0).astype(BF16)

    return call(
        body,
        [pltpu.VMEM((NY * HALF, SAMPLES), BF16)],
        (near(arrived),),
        cost=pl.CostEstimate(flops=1 << 29, bytes_accessed=2 << 20, transcendentals=0),
    )[0]


def head_of(rows_ref, pooled):
    head = dot(rows_ref[2 * RANK :, :], pooled, 1, 0)
    sums = head[0:1] + head[2:3]
    high = sums.astype(BF16).astype(F32)
    at = lax.broadcasted_iota(jnp.int32, (EXT, pooled.shape[1]), 0)
    return jnp.where(at == 0, high, jnp.where(at == 1, sums - high, 0.0)).astype(BF16)


def products(rows_ref, pooled, outs):
    for part in range(4):
        at = slice(part * 256, (part + 1) * 256)
        product = dot(rows_ref[at, :], pooled, 1, 0).astype(BF16)
        for i, out in enumerate(outs):
            out[at, :] = product[:, i * OWN : (i + 1) * OWN]
    ext = head_of(rows_ref, pooled)
    for i, out in enumerate(outs):
        out[2 * RANK :, :] = ext[:, i * OWN : (i + 1) * OWN]


def forward_far(place, arrived, other, half, rows):
    def body(place_ref, in_ref, other_ref, half_ref, rows_ref, pooled_ref, out):
        core = place_ref[3]
        for y in range(NY):
            at = slice(y * 512, (y + 1) * 512)
            mine = pl.multiple_of(y * EMBED + core * HALF, HALF)
            partners = pl.multiple_of(y * EMBED + (1 - core) * HALF, HALF)
            pooled_ref[pl.ds(mine, HALF), :] = half_ref[y * HALF : (y + 1) * HALF, :]
            pooled_ref[pl.ds(partners, HALF), :] = dot(
                other_ref[at, :].T, in_ref[at, :SAMPLES], 1, 0
            ).astype(BF16)
        products(rows_ref, pooled_ref[:, OWN : 2 * OWN], (out,))

    return call(
        body,
        [pltpu.VMEM((COLS, SAMPLES), BF16), pltpu.VMEM((2 * RANK + EXT, OWN), BF16)],
        (place, near(arrived), near(other), near(half), near(rows)),
        [IN_SMEM] + [IN_VMEM] * 4,
        cost=pl.CostEstimate(flops=3 << 30, bytes_accessed=4 << 20, transcendentals=0),
    )


def forward_near(pooled, rows):
    def body(pooled_ref, rows_ref, *outs):
        products(rows_ref, pooled_ref[:, 2 * OWN :], outs)

    return call(
        body,
        [pltpu.VMEM((2 * RANK + EXT, OWN), BF16)] * 2,
        (near(pooled), near(rows)),
        cost=pl.CostEstimate(flops=1 << 30, bytes_accessed=2 << 20, transcendentals=0),
    )


def forward_own(pooled, rows):
    def body(pooled_ref, rows_ref, out):
        products(rows_ref, pooled_ref[:, :OWN], (out,))

    return call(
        body,
        [pltpu.VMEM((2 * RANK + EXT, OWN), BF16)],
        (near(pooled), near(rows)),
        cost=pl.CostEstimate(flops=1 << 30, bytes_accessed=1 << 20, transcendentals=0),
    )[0]


def own_samples(parts, labels):
    def body(p0, p1, p2, p3, labels_ref, out):
        def total(rows):
            a, b, c, d = (p[rows, :].astype(F32) for p in (p0, p1, p2, p3))
            return (a + b) + (c + d)

        squeezed = total(slice(0, RANK)).astype(BF16).astype(F32)
        other = total(slice(RANK, 2 * RANK))
        ext = total(slice(2 * RANK, 2 * RANK + EXT))
        logits = ext[0:1] + ext[1:2] + jnp.sum(squeezed * other, axis=0, keepdims=True)
        g = jax.nn.sigmoid(logits) - labels_ref[...].astype(F32)
        out[0:RANK, :] = (g * other).astype(BF16)
        out[RANK : 2 * RANK, :] = (g * squeezed).astype(BF16)
        high = g.astype(BF16).astype(F32)
        at = lax.broadcasted_iota(jnp.int32, (EXT, OWN), 0)
        rows = jnp.where((at == 0) | (at == 2), high, jnp.where(at == 1, g - high, 0.0))
        out[2 * RANK :, :] = rows.astype(BF16)

    return call(body, [pltpu.VMEM((2 * RANK + EXT, OWN), BF16)], (*(near(p) for p in parts), labels))[0]


def by_sample(*blocks):
    return jnp.concatenate([b[...].T for b in blocks], axis=0)


def grad_pooled_of(g, rows_ref):
    tables = [slice(y * EMBED, (y + 1) * EMBED) for y in range(NY)]
    return [dot(g, rows_ref[:, table], 1, 0).astype(BF16) for table in tables]


def backward_first(block0, block2, pooled, arrived, rows):
    def body(b0, b2, pooled_ref, in_ref, rows_ref, both_out, sums_out, slab_out):
        g = by_sample(b0, b2)
        products = grad_pooled_of(g, rows_ref)
        pooled = pooled_ref[:, : 2 * OWN]
        for j in range(4):
            at = slice(j * 256, (j + 1) * 256)
            both_out[:, at] = dot(pooled, g[:, at], 1, 0)
        ext = jnp.concatenate([b0[2 * RANK :, :], b2[2 * RANK :, :]], axis=1)
        sums_out[...] = dot(ext, pooled, 1, 1)
        for y, grad_pooled in enumerate(products):
            at = slice(y * 512, (y + 1) * 512)
            slab_out[at, :] = dot(in_ref[at, : 2 * OWN], grad_pooled, 1, 0)

    return call(
        body,
        [
            pltpu.VMEM((COLS, 2 * RANK), F32),
            pltpu.VMEM((EXT, COLS), F32),
            pltpu.VMEM((PEERS * ROWS, EMBED), F32),
        ],
        tuple(near(v) for v in (block0, block2, pooled, arrived, rows)),
        cost=pl.CostEstimate(flops=2 << 30, bytes_accessed=6 << 20, transcendentals=0),
    )


def put(low_core, mine, other, targets, at, value):
    pair = value.astype(BF16).reshape(-1, NC, *value.shape[1:])
    even, odd = pair[:, 0], pair[:, 1]
    mine[targets, at, :] = jnp.where(low_core, even, odd)
    other[targets, at, :] = jnp.where(low_core, odd, even)


EVERYONE = slice(0, NY * NX)


def backward_weights(place, block1, block3, pooled, both, sums):
    def body(place_ref, b1, b3, pooled_ref, both_ref, sums_ref, mine, other, g_out):
        low_core = place_ref[3] == 0
        g = by_sample(b1, b3)
        g_out[...] = g
        pooled = pooled_ref[:, 2 * OWN :]
        for j in range(4):
            value = dot(pooled, g[:, j * 256 : (j + 1) * 256], 1, 0)
            for h in range(2):
                at = (2 * j + h) * 128
                held = both_ref[:, at : at + 128] + value[:, h * 128 : (h + 1) * 128]
                to = slice((2 * j + h) * 32, (2 * j + h + 1) * 32)
                put(low_core, mine, other, EVERYONE, to, held.reshape(PEERS, 32, 128))
        ext = jnp.concatenate([b1[2 * RANK :, :], b3[2 * RANK :, :]], axis=1)
        held = (dot(ext, pooled, 1, 1) + sums_ref[...]).astype(BF16)
        for strip in range(8):
            row = held[:, strip * 128 : (strip + 1) * 128]
            for i in range(2):
                mine[strip * 2 + i, 256:, :] = row
                other[strip * 2 + i, 256:, :] = row

    return call(
        body,
        [pltpu.VMEM((NY * NX, 272, 128), BF16)] * 2 + [pltpu.VMEM((2 * OWN, 2 * RANK + EXT), BF16)],
        (place, *(near(v) for v in (block1, block3, pooled, both, sums))),
        [IN_SMEM] + [IN_VMEM] * 5,
        cost=pl.CostEstimate(flops=1 << 30, bytes_accessed=4 << 20, transcendentals=0),
    )


def backward_slab(place, g, arrived, rows, slab_first):
    def body(place_ref, g_ref, in_ref, rows_ref, first_ref, mine, other):
        low_core = place_ref[3] == 0
        for y, grad_pooled in enumerate(grad_pooled_of(g_ref[...], rows_ref)):
            at = slice(y * 512, (y + 1) * 512)
            slab = first_ref[at, :] + dot(in_ref[at, 2 * OWN : SAMPLES], grad_pooled, 1, 0)
            for j in range(2):
                put(
                    low_core,
                    mine,
                    other,
                    slice(y * NX, (y + 1) * NX),
                    slice(j * ROWS, (j + 1) * ROWS),
                    slab[:, j * 128 : (j + 1) * 128].reshape(NK, ROWS, 128),
                )

    return call(
        body,
        [pltpu.VMEM((NY * NX, 2 * ROWS, 128), BF16)] * 2,
        (place, *(near(v) for v in (g, arrived, rows, slab_first))),
        [IN_SMEM] + [IN_VMEM] * 4,
        cost=pl.CostEstimate(flops=1 << 30, bytes_accessed=4 << 20, transcendentals=0),
    )


AWAY = (
    (2, 2), (2, 1), (1, 2), (2, 3), (3, 2), (1, 1), (3, 3), (1, 3), (3, 1), (2, 0), (0, 2), (1, 0), (0, 1), (3, 0), (0, 3)
)


def pair_sums(place, slab, slab_partner, weights, weights_partner):
    def body(place_ref, a, b, c, d, *outs):
        for (dy, dx), out in zip(AWAY + ((0, 0),), outs):
            at = lax.rem(place_ref[1] + dy, NY) * NX + lax.rem(place_ref[2] + dx, NX)
            out[: 2 * ROWS, :] = (a[at].astype(F32) + b[at].astype(F32)).astype(BF16)
            out[2 * ROWS :, :] = (c[at].astype(F32) + d[at].astype(F32)).astype(BF16)

    return call(
        body,
        [pltpu.VMEM((PACK, 128), BF16)] * (NY * NX),
        (place, *(near(v) for v in (slab, slab_partner, weights, weights_partner))),
        [IN_SMEM] + [IN_VMEM] * 4,
    )


def finish(shares, own, up_own):
    def body(*refs):
        ins = refs[: NY * NX]
        own_ref, up_ref, slab_out, down_out, up_out, bias_out, out_out = refs[NY * NX :]

        def total(at):
            held = [ref[at, :].astype(F32) for ref in ins]
            while len(held) > 1:
                held = [a + b for a, b in zip(held[::2], held[1::2])]
            return held[0]

        slab_out[:, :128] = total(slice(0, ROWS))
        slab_out[:, 128:] = total(slice(ROWS, 2 * ROWS))
        both = [total(slice(128 + j * 32, 160 + j * 32)) for j in range(8)]
        for j in range(4):
            down_out[:, j * 128 : (j + 1) * 128] = both[j].astype(BF16)
        product = jnp.concatenate(both[4:], axis=1)
        w_own, bias_own = own_ref[:, 0:1], own_ref[:, 1:2]
        up_out[...] = (product * w_own).astype(BF16)
        lane = lax.broadcasted_iota(jnp.int32, (32, 128), 1)
        row = lax.broadcasted_iota(jnp.int32, (32, 128), 0)
        last = total(slice(384, 400))
        own = lane.astype(F32) == own_ref[:, 2:3]
        sums = jnp.sum(jnp.where(own, last[0:1] + last[1:2], 0.0), axis=1, keepdims=True)
        out = (1.0 + bias_own) * sums + jnp.sum(product * up_ref[...], axis=1, keepdims=True)
        bias_out[...] = jnp.sum(jnp.where(lane == row, w_own * sums, 0.0), axis=0, keepdims=True)[:, :32]
        out_out[...] = jnp.sum(jnp.where(lane == row, out, 0.0), axis=0, keepdims=True)[:, :32]

    return call(
        body,
        [
            jax.ShapeDtypeStruct((ROWS, EMBED), F32),
            jax.ShapeDtypeStruct((32, RANK), BF16),
            jax.ShapeDtypeStruct((32, RANK), BF16),
            jax.ShapeDtypeStruct((1, 32), F32),
            jax.ShapeDtypeStruct((1, 32), F32),
        ],
        (*(near(v) for v in shares), near(own), near(up_own)),
    )


def local(slab, counts, cross_down, cross_up, cross_bias, out_weight, labels):
    place = jnp.stack([lax.axis_index(a) for a in ALL]).astype(jnp.int32)
    w_row, bias_row = out_weight.reshape(1, -1), cross_bias.reshape(1, -1)
    rows = prepare(place, cross_down, cross_up, w_row, bias_row)
    own, up_own = prepare_own(place, cross_up, w_row, bias_row)
    sent = pack_counts(place, counts.T, slab)
    arrived = lax.all_to_all(sent, PLANE, 0, 0, tiled=True).reshape(PEERS * ROWS, SAMPLES + HALF)
    other = shift(arrived[:, SAMPLES:], dc=1)
    half = pool_half(arrived)
    pooled, chunk2 = forward_far(place, arrived, other, half, rows)
    part2 = shift(chunk2, dz=2)
    chunk1, chunk3 = forward_near(pooled, rows)
    part1 = shift(chunk1, dz=1)
    part3 = shift(chunk3, dz=3)
    parts = [part2, part1, part3]
    chunk = forward_own(pooled, rows)
    block0 = own_samples([chunk] + parts, labels.reshape(1, OWN))
    blocks = []
    for i in ORDER[1:]:
        blocks.append(shift(block0, dz=-i))
    block2, block1, block3 = blocks
    both, sums, slab_first = backward_first(block0, block2, pooled, arrived, rows)
    weights, given, g = backward_weights(place, block1, block3, pooled, both, sums)
    weights_partner = shift(given, dc=1)
    slabs, given = backward_slab(place, g, arrived, rows, slab_first)
    *leaving, kept = pair_sums(place, slabs, shift(given, dc=1), weights, weights_partner)
    shares = [kept]
    for (dy, dx), value in zip(AWAY, leaving):
        shares.append(shift(value, dy=dy, dx=dx))
    grad_slab, grad_down, grad_up, grad_bias, grad_out = finish(shares, own, up_own)
    return grad_slab, grad_down, grad_up.T, grad_bias.reshape(32), grad_out.reshape(32)


def solution(mesh):
    torus = Mesh(mesh.devices.reshape(NZ, NY, NX, NC), ALL)
    return jax.shard_map(
        local,
        mesh=torus,
        in_specs=(P(ALL, None), P(None, ALL), P(), P(), P(), P(), P(ALL)),
        out_specs=(P(ALL, None), P(ALL, None), P(None, ALL), P(ALL), P(ALL)),
        check_vma=False,
    )
```

```python
import jax
import jax.numpy as jnp
from jax import lax
from jax.experimental import pallas as pl
from jax.experimental.pallas import tpu as pltpu
from jax.sharding import Mesh
from jax.sharding import PartitionSpec as P


ALL = ("z", "y", "x", "c")
PLANE = ("y", "x", "c")
NZ, NY, NX, NC = 4, 4, 4, 2
NK = NX * NC
PEERS = NY * NK
OWN = 128
ROWS = 64
EMBED = 256
RANK = 512
COLS = 1024
SAMPLES = NZ * OWN
EXT = 16
PACK = 400
HALF = EMBED // 2
EARLY = SAMPLES - OWN
ORDER = (0, 1, 3, 2)
F32 = jnp.float32
BF16 = jnp.bfloat16


def dot(a, b, da, db):
    return lax.dot_general(a, b, (((da,), (db,)), ((), ())), preferred_element_type=F32)


def flat(z, y, x, c):
    return (((z % NZ) * NY + y % NY) * NX + x % NX) * NC + c % NC


def shift(value, dz=0, dy=0, dx=0, dc=0):
    pairs = [
        (flat(z, y, x, c), flat(z + dz, y + dy, x + dx, c + dc))
        for z in range(NZ)
        for y in range(NY)
        for x in range(NX)
        for c in range(NC)
    ]
    return lax.ppermute(value, ALL, pairs)


def near(value):
    return pltpu.with_memory_space_constraint(value, pltpu.VMEM)


def far(value):
    return pltpu.with_memory_space_constraint(value, pltpu.HBM)


def call(body, outs, args, specs=None, scratch=(), mib=24, cost=None):
    return pl.pallas_call(
        body,
        in_specs=specs or [pl.BlockSpec(memory_space=pltpu.VMEM)] * len(args),
        out_specs=[pl.BlockSpec(memory_space=pltpu.VMEM)] * len(outs),
        out_shape=outs,
        scratch_shapes=list(scratch),
        compiler_params=pltpu.CompilerParams(vmem_limit_bytes=mib << 20),
        cost_estimate=cost,
    )(*args)


IN_SMEM = pl.BlockSpec(memory_space=pltpu.SMEM)
IN_VMEM = pl.BlockSpec(memory_space=pltpu.VMEM)
IN_HBM = pl.BlockSpec(memory_space=pltpu.HBM)


def pack_counts(place, counts_t, slab):
    strip = NK * OWN

    def body(place_ref, counts_ref, slab_ref, out, held, slab_s, sems, slab_sem):
        def copy(y, n):
            z = lax.rem(place_ref[0] + ORDER[n], NZ)
            start = pl.multiple_of(z * (NY * strip) + y * strip, strip)
            return pltpu.make_async_copy(counts_ref.at[:, pl.ds(start, strip)], held.at[y, n], sems.at[y, n])

        slab_copy = pltpu.make_async_copy(slab_ref, slab_s, slab_sem)
        slab_copy.start()
        for y in range(NY):
            for n in range(NZ):
                copy(y, n).start()
        slab_copy.wait()
        for k in range(PEERS):
            half = k % NC
            out[k, :, SAMPLES:] = slab_s[:, half * HALF : (half + 1) * HALF]
        for y in range(NY):
            for n in range(NZ):
                copy(y, n).wait()
                for k in range(NK):
                    out[y * NK + k, :, n * OWN : (n + 1) * OWN] = (
                        held[y, n, :, k * OWN : (k + 1) * OWN].astype(F32).astype(BF16)
                    )

    return call(
        body,
        [pltpu.VMEM((PEERS, ROWS, SAMPLES + HALF), BF16)],
        (place, far(counts_t), far(slab)),
        [IN_SMEM, IN_HBM, IN_HBM],
        [
            pltpu.VMEM((NY, NZ, ROWS, strip), jnp.int32),
            pltpu.VMEM((ROWS, EMBED), BF16),
            pltpu.SemaphoreType.DMA((NY, NZ)),
            pltpu.SemaphoreType.DMA,
        ],
    )[0]


def prepare(place, down, up, w, bias):
    def body(place_ref, down_ref, up_ref, w_ref, bias_ref, rows_out):
        here = pl.ds(pl.multiple_of(place_ref[0] * COLS, COLS), COLS)
        w = w_ref[:, here]
        for part in range(4):
            at = slice(part * 128, (part + 1) * 128)
            rows_out[at, :] = down_ref[here, at].T
        rows_out[RANK : 2 * RANK, :] = (up_ref[:, here].astype(F32) * w).astype(BF16)
        v = w * (1.0 + bias_ref[:, here])
        high = v.astype(BF16).astype(F32)
        at = lax.broadcasted_iota(jnp.int32, (EXT, COLS), 0)
        rows_out[2 * RANK :, :] = jnp.where(at < 2, high, jnp.where(at == 2, v - high, 0.0)).astype(BF16)

    return call(
        body,
        [pltpu.VMEM((2 * RANK + EXT, COLS), BF16)],
        (place, *(near(v) for v in (down, up, w, bias))),
        [IN_SMEM] + [IN_VMEM] * 4,
        cost=pl.CostEstimate(flops=1 << 29, bytes_accessed=6 << 20, transcendentals=0),
    )[0]


def prepare_own(place, up, w, bias):
    def body(place_ref, up_ref, w_ref, bias_ref, own_out, up_out):
        k = place_ref[2] * NC + place_ref[3]
        start = place_ref[0] * COLS + (place_ref[1] * 2 + lax.div(k, 4)) * 128
        strip = pl.ds(pl.multiple_of(start, 128), 128)
        offset = lax.rem(k, 4) * 32
        lane = lax.broadcasted_iota(jnp.int32, (32, 128), 1)
        row = lax.broadcasted_iota(jnp.int32, (32, 128), 0)
        own = lane == row + offset
        w_own = jnp.sum(jnp.where(own, w_ref[:, strip], 0.0), axis=1, keepdims=True)
        bias_own = jnp.sum(jnp.where(own, bias_ref[:, strip], 0.0), axis=1, keepdims=True)
        place_own = (row + offset).astype(F32)
        own_out[...] = jnp.where(lane == 0, w_own, jnp.where(lane == 1, bias_own, place_own))
        up_out[...] = dot(jnp.where(own, 1.0, 0.0).astype(BF16), up_ref[:, strip], 1, 1)

    return call(
        body,
        [pltpu.VMEM((32, 128), F32), pltpu.VMEM((32, RANK), F32)],
        (place, *(near(v) for v in (up, w, bias))),
        [IN_SMEM] + [IN_VMEM] * 3,
        cost=pl.CostEstimate(flops=1 << 27, bytes_accessed=1 << 20, transcendentals=0),
    )


def pool_half(arrived):
    def body(in_ref, pooled_ref):
        for y in range(NY):
            at = slice(y * 512, (y + 1) * 512)
            half = slice(y * HALF, (y + 1) * HALF)
            pooled_ref[half, :] = dot(in_ref[at, SAMPLES:].T, in_ref[at, :SAMPLES], 1, 0).astype(BF16)

    return call(
        body,
        [pltpu.VMEM((NY * HALF, SAMPLES), BF16)],
        (near(arrived),),
        cost=pl.CostEstimate(flops=1 << 29, bytes_accessed=2 << 20, transcendentals=0),
    )[0]


def head_of(rows_ref, pooled):
    head = dot(rows_ref[2 * RANK :, :], pooled, 1, 0)
    sums = head[0:1] + head[2:3]
    high = sums.astype(BF16).astype(F32)
    at = lax.broadcasted_iota(jnp.int32, (EXT, pooled.shape[1]), 0)
    return jnp.where(at == 0, high, jnp.where(at == 1, sums - high, 0.0)).astype(BF16)


def products(rows_ref, pooled, outs):
    for part in range(4):
        at = slice(part * 256, (part + 1) * 256)
        product = dot(rows_ref[at, :], pooled, 1, 0).astype(BF16)
        for i, out in enumerate(outs):
            out[at, :] = product[:, i * OWN : (i + 1) * OWN]
    ext = head_of(rows_ref, pooled)
    for i, out in enumerate(outs):
        out[2 * RANK :, :] = ext[:, i * OWN : (i + 1) * OWN]


def forward_near(place, arrived, other, half, rows):
    def body(place_ref, in_ref, other_ref, half_ref, rows_ref, pooled_ref, *outs):
        core = place_ref[3]
        for y in range(NY):
            at = slice(y * 512, (y + 1) * 512)
            mine = pl.multiple_of(y * EMBED + core * HALF, HALF)
            partners = pl.multiple_of(y * EMBED + (1 - core) * HALF, HALF)
            pooled_ref[pl.ds(mine, HALF), :] = half_ref[y * HALF : (y + 1) * HALF, :]
            pooled_ref[pl.ds(partners, HALF), :] = dot(
                other_ref[at, :].T, in_ref[at, :SAMPLES], 1, 0
            ).astype(BF16)
        products(rows_ref, pooled_ref[:, OWN:EARLY], outs)

    return call(
        body,
        [pltpu.VMEM((COLS, SAMPLES), BF16)] + [pltpu.VMEM((2 * RANK + EXT, OWN), BF16)] * 2,
        (place, near(arrived), near(other), near(half), near(rows)),
        [IN_SMEM] + [IN_VMEM] * 4,
        cost=pl.CostEstimate(flops=3 << 30, bytes_accessed=4 << 20, transcendentals=0),
    )


def forward_far(pooled, rows):
    def body(pooled_ref, rows_ref, *outs):
        products(rows_ref, pooled_ref[:, EARLY:], outs)

    return call(
        body,
        [pltpu.VMEM((2 * RANK + EXT, OWN), BF16)],
        (near(pooled), near(rows)),
        cost=pl.CostEstimate(flops=1 << 30, bytes_accessed=2 << 20, transcendentals=0),
    )[0]


def forward_own(pooled, rows):
    def body(pooled_ref, rows_ref, out):
        products(rows_ref, pooled_ref[:, :OWN], (out,))

    return call(
        body,
        [pltpu.VMEM((2 * RANK + EXT, OWN), BF16)],
        (near(pooled), near(rows)),
        cost=pl.CostEstimate(flops=1 << 30, bytes_accessed=1 << 20, transcendentals=0),
    )[0]


def own_samples(parts, labels):
    def body(p0, p1, p2, p3, labels_ref, out):
        def total(rows):
            a, b, c, d = (p[rows, :].astype(F32) for p in (p0, p1, p2, p3))
            return (a + b) + (c + d)

        squeezed = total(slice(0, RANK)).astype(BF16).astype(F32)
        other = total(slice(RANK, 2 * RANK))
        ext = total(slice(2 * RANK, 2 * RANK + EXT))
        logits = ext[0:1] + ext[1:2] + jnp.sum(squeezed * other, axis=0, keepdims=True)
        g = jax.nn.sigmoid(logits) - labels_ref[...].astype(F32)
        out[0:RANK, :] = (g * other).astype(BF16)
        out[RANK : 2 * RANK, :] = (g * squeezed).astype(BF16)
        high = g.astype(BF16).astype(F32)
        at = lax.broadcasted_iota(jnp.int32, (EXT, OWN), 0)
        rows = jnp.where((at == 0) | (at == 2), high, jnp.where(at == 1, g - high, 0.0))
        out[2 * RANK :, :] = rows.astype(BF16)

    return call(body, [pltpu.VMEM((2 * RANK + EXT, OWN), BF16)], (*(near(p) for p in parts), labels))[0]


def by_sample(*blocks):
    return jnp.concatenate([b[...].T for b in blocks], axis=0)


def grad_pooled_of(g, rows_ref):
    tables = [slice(y * EMBED, (y + 1) * EMBED) for y in range(NY)]
    return [dot(g, rows_ref[:, table], 1, 0).astype(BF16) for table in tables]


def backward_first(block0, block1, block3, pooled, arrived, rows):
    def body(b0, b1, b3, pooled_ref, in_ref, rows_ref, both_out, sums_out, slab_out):
        g = by_sample(b0, b1, b3)
        products = grad_pooled_of(g, rows_ref)
        pooled = pooled_ref[:, :EARLY]
        for j in range(4):
            at = slice(j * 256, (j + 1) * 256)
            both_out[:, at] = dot(pooled, g[:, at], 1, 0)
        ext = jnp.concatenate([b[2 * RANK :, :] for b in (b0, b1, b3)], axis=1)
        sums_out[...] = dot(ext, pooled, 1, 1)
        for y, grad_pooled in enumerate(products):
            at = slice(y * 512, (y + 1) * 512)
            slab_out[at, :] = dot(in_ref[at, :EARLY], grad_pooled, 1, 0)

    return call(
        body,
        [
            pltpu.VMEM((COLS, 2 * RANK), F32),
            pltpu.VMEM((EXT, COLS), F32),
            pltpu.VMEM((PEERS * ROWS, EMBED), F32),
        ],
        tuple(near(v) for v in (block0, block1, block3, pooled, arrived, rows)),
        cost=pl.CostEstimate(flops=2 << 30, bytes_accessed=6 << 20, transcendentals=0),
    )


def put(low_core, mine, other, targets, at, value):
    pair = value.astype(BF16).reshape(-1, NC, *value.shape[1:])
    even, odd = pair[:, 0], pair[:, 1]
    mine[targets, at, :] = jnp.where(low_core, even, odd)
    other[targets, at, :] = jnp.where(low_core, odd, even)


EVERYONE = slice(0, NY * NX)


def backward_weights(place, block2, pooled, both, sums):
    def body(place_ref, b2, pooled_ref, both_ref, sums_ref, mine, other, g_out):
        low_core = place_ref[3] == 0
        g = by_sample(b2)
        g_out[...] = g
        pooled = pooled_ref[:, EARLY:]
        for j in range(4):
            value = dot(pooled, g[:, j * 256 : (j + 1) * 256], 1, 0)
            for h in range(2):
                at = (2 * j + h) * 128
                held = both_ref[:, at : at + 128] + value[:, h * 128 : (h + 1) * 128]
                to = slice((2 * j + h) * 32, (2 * j + h + 1) * 32)
                put(low_core, mine, other, EVERYONE, to, held.reshape(PEERS, 32, 128))
        held = (dot(b2[2 * RANK :, :], pooled, 1, 1) + sums_ref[...]).astype(BF16)
        for strip in range(8):
            row = held[:, strip * 128 : (strip + 1) * 128]
            for i in range(2):
                mine[strip * 2 + i, 256:, :] = row
                other[strip * 2 + i, 256:, :] = row

    return call(
        body,
        [pltpu.VMEM((NY * NX, 272, 128), BF16)] * 2 + [pltpu.VMEM((OWN, 2 * RANK + EXT), BF16)],
        (place, *(near(v) for v in (block2, pooled, both, sums))),
        [IN_SMEM] + [IN_VMEM] * 4,
        cost=pl.CostEstimate(flops=1 << 30, bytes_accessed=4 << 20, transcendentals=0),
    )


def backward_slab(place, g, arrived, rows, slab_first):
    def body(place_ref, g_ref, in_ref, rows_ref, first_ref, mine, other):
        low_core = place_ref[3] == 0
        for y, grad_pooled in enumerate(grad_pooled_of(g_ref[...], rows_ref)):
            at = slice(y * 512, (y + 1) * 512)
            slab = first_ref[at, :] + dot(in_ref[at, EARLY:SAMPLES], grad_pooled, 1, 0)
            for j in range(2):
                put(
                    low_core,
                    mine,
                    other,
                    slice(y * NX, (y + 1) * NX),
                    slice(j * ROWS, (j + 1) * ROWS),
                    slab[:, j * 128 : (j + 1) * 128].reshape(NK, ROWS, 128),
                )

    return call(
        body,
        [pltpu.VMEM((NY * NX, 2 * ROWS, 128), BF16)] * 2,
        (place, *(near(v) for v in (g, arrived, rows, slab_first))),
        [IN_SMEM] + [IN_VMEM] * 4,
        cost=pl.CostEstimate(flops=1 << 30, bytes_accessed=4 << 20, transcendentals=0),
    )


def pair_sums(slab, slab_partner, weights, weights_partner):
    def body(a, b, c, d, out):
        out[:, : 2 * ROWS, :] = (a[...].astype(F32) + b[...].astype(F32)).astype(BF16)
        out[:, 2 * ROWS :, :] = (c[...].astype(F32) + d[...].astype(F32)).astype(BF16)

    return call(
        body,
        [pltpu.VMEM((NY * NX, PACK, 128), BF16)],
        tuple(near(v) for v in (slab, slab_partner, weights, weights_partner)),
    )[0]


def finish(shares, own, up_own):
    def body(in_ref, own_ref, up_ref, slab_out, down_out, up_out, bias_out, out_out):
        def total(at):
            held = in_ref[0, at, :].astype(F32)
            for i in range(1, NY * NX):
                held = held + in_ref[i, at, :].astype(F32)
            return held

        slab_out[:, :128] = total(slice(0, ROWS))
        slab_out[:, 128:] = total(slice(ROWS, 2 * ROWS))
        both = [total(slice(128 + j * 32, 160 + j * 32)) for j in range(8)]
        for j in range(4):
            down_out[:, j * 128 : (j + 1) * 128] = both[j].astype(BF16)
        product = jnp.concatenate(both[4:], axis=1)
        w_own, bias_own = own_ref[:, 0:1], own_ref[:, 1:2]
        up_out[...] = (product * w_own).astype(BF16)
        lane = lax.broadcasted_iota(jnp.int32, (32, 128), 1)
        row = lax.broadcasted_iota(jnp.int32, (32, 128), 0)
        last = total(slice(384, 400))
        own = lane.astype(F32) == own_ref[:, 2:3]
        sums = jnp.sum(jnp.where(own, last[0:1] + last[1:2], 0.0), axis=1, keepdims=True)
        out = (1.0 + bias_own) * sums + jnp.sum(product * up_ref[...], axis=1, keepdims=True)
        bias_out[...] = jnp.sum(jnp.where(lane == row, w_own * sums, 0.0), axis=0, keepdims=True)[:, :32]
        out_out[...] = jnp.sum(jnp.where(lane == row, out, 0.0), axis=0, keepdims=True)[:, :32]

    return call(
        body,
        [
            jax.ShapeDtypeStruct((ROWS, EMBED), F32),
            jax.ShapeDtypeStruct((32, RANK), BF16),
            jax.ShapeDtypeStruct((32, RANK), BF16),
            jax.ShapeDtypeStruct((1, 32), F32),
            jax.ShapeDtypeStruct((1, 32), F32),
        ],
        (near(shares), near(own), near(up_own)),
    )


def local(slab, counts, cross_down, cross_up, cross_bias, out_weight, labels):
    place = jnp.stack([lax.axis_index(a) for a in ALL]).astype(jnp.int32)
    w_row, bias_row = out_weight.reshape(1, -1), cross_bias.reshape(1, -1)
    rows = prepare(place, cross_down, cross_up, w_row, bias_row)
    own, up_own = prepare_own(place, cross_up, w_row, bias_row)
    sent = pack_counts(place, counts.T, slab)
    arrived = lax.all_to_all(sent, PLANE, 0, 0, tiled=True).reshape(PEERS * ROWS, SAMPLES + HALF)
    other = shift(arrived[:, SAMPLES:], dc=1)
    half = pool_half(arrived)
    pooled, chunk1, chunk3 = forward_near(place, arrived, other, half, rows)
    part1 = shift(chunk1, dz=1)
    part3 = shift(chunk3, dz=3)
    chunk2 = forward_far(pooled, rows)
    part2 = shift(chunk2, dz=2)
    parts = [part1, part3, part2]
    chunk = forward_own(pooled, rows)
    block0 = own_samples([chunk] + parts, labels.reshape(1, OWN))
    blocks = []
    for i in ORDER[1:]:
        blocks.append(shift(block0, dz=-i))
    block1, block3, block2 = blocks
    both, sums, slab_first = backward_first(block0, block1, block3, pooled, arrived, rows)
    weights, given, g = backward_weights(place, block2, pooled, both, sums)
    weights_partner = shift(given, dc=1)
    slabs, given = backward_slab(place, g, arrived, rows, slab_first)
    paired = pair_sums(slabs, shift(given, dc=1), weights, weights_partner)
    shares = lax.all_to_all(paired, ("y", "x"), 0, 0, tiled=True)
    grad_slab, grad_down, grad_up, grad_bias, grad_out = finish(shares, own, up_own)
    return grad_slab, grad_down, grad_up.T, grad_bias.reshape(32), grad_out.reshape(32)


def solution(mesh):
    torus = Mesh(mesh.devices.reshape(NZ, NY, NX, NC), ALL)
    return jax.shard_map(
        local,
        mesh=torus,
        in_specs=(P(ALL, None), P(None, ALL), P(), P(), P(), P(), P(ALL)),
        out_specs=(P(ALL, None), P(ALL, None), P(None, ALL), P(ALL), P(ALL)),
        check_vma=False,
    )
```

```python
import jax
import jax.numpy as jnp
from jax import lax
from jax.experimental import pallas as pl
from jax.experimental.pallas import tpu as pltpu
from jax.sharding import Mesh
from jax.sharding import PartitionSpec as P


ALL = ("z", "y", "x", "c")
PLANE = ("y", "x", "c")
NZ, NY, NX, NC = 4, 4, 4, 2
NK = NX * NC
PEERS = NY * NK
OWN = 128
ROWS = 64
EMBED = 256
RANK = 512
COLS = 1024
SAMPLES = NZ * OWN
EXT = 16
PACK = 400
HALF = EMBED // 2
ORDER = ((0, 1, 2, 3), (0, 3, 2, 1))
PLACES = ((0, 1, 2, 3), (0, 3, 2, 1))
F32 = jnp.float32
BF16 = jnp.bfloat16


def dot(a, b, da, db):
    return lax.dot_general(a, b, (((da,), (db,)), ((), ())), preferred_element_type=F32)


def flat(z, y, x, c):
    return (((z % NZ) * NY + y % NY) * NX + x % NX) * NC + c % NC


def shift(value, dz=(0, 0), dc=0):
    pairs = [
        (flat(z, y, x, c), flat(z + dz[c], y, x, c + dc))
        for z in range(NZ)
        for y in range(NY)
        for x in range(NX)
        for c in range(NC)
    ]
    return lax.ppermute(value, ALL, pairs)


def near(value):
    return pltpu.with_memory_space_constraint(value, pltpu.VMEM)


def far(value):
    return pltpu.with_memory_space_constraint(value, pltpu.HBM)


def call(body, outs, args, specs=None, scratch=(), mib=24, cost=None):
    return pl.pallas_call(
        body,
        in_specs=specs or [pl.BlockSpec(memory_space=pltpu.VMEM)] * len(args),
        out_specs=[pl.BlockSpec(memory_space=pltpu.VMEM)] * len(outs),
        out_shape=outs,
        scratch_shapes=list(scratch),
        compiler_params=pltpu.CompilerParams(vmem_limit_bytes=mib << 20),
        cost_estimate=cost,
    )(*args)


IN_SMEM = pl.BlockSpec(memory_space=pltpu.SMEM)
IN_VMEM = pl.BlockSpec(memory_space=pltpu.VMEM)
IN_HBM = pl.BlockSpec(memory_space=pltpu.HBM)


def pack_counts(place, counts_t, slab):
    strip = NK * OWN

    def body(place_ref, counts_ref, slab_ref, out, held, slab_s, sems, slab_sem):
        def copy(y, n):
            z = lax.rem(place_ref[0] + n, NZ)
            start = pl.multiple_of(z * (NY * strip) + y * strip, strip)
            return pltpu.make_async_copy(counts_ref.at[:, pl.ds(start, strip)], held.at[y, n], sems.at[y, n])

        slab_copy = pltpu.make_async_copy(slab_ref, slab_s, slab_sem)
        slab_copy.start()
        for y in range(NY):
            for n in range(NZ):
                copy(y, n).start()
        slab_copy.wait()
        for k in range(PEERS):
            half = k % NC
            out[k, :, SAMPLES:] = slab_s[:, half * HALF : (half + 1) * HALF]
        for y in range(NY):
            for n in range(NZ):
                copy(y, n).wait()
                for k in range(NK):
                    to = PLACES[k % NC][n] * OWN
                    out[y * NK + k, :, to : to + OWN] = (
                        held[y, n, :, k * OWN : (k + 1) * OWN].astype(F32).astype(BF16)
                    )

    return call(
        body,
        [pltpu.VMEM((PEERS, ROWS, SAMPLES + HALF), BF16)],
        (place, far(counts_t), far(slab)),
        [IN_SMEM, IN_HBM, IN_HBM],
        [
            pltpu.VMEM((NY, NZ, ROWS, strip), jnp.int32),
            pltpu.VMEM((ROWS, EMBED), BF16),
            pltpu.SemaphoreType.DMA((NY, NZ)),
            pltpu.SemaphoreType.DMA,
        ],
    )[0]


def prepare(place, down, up, w, bias):
    def body(place_ref, down_ref, up_ref, w_ref, bias_ref, rows_out):
        here = pl.ds(pl.multiple_of(place_ref[0] * COLS, COLS), COLS)
        w = w_ref[:, here]
        for part in range(4):
            at = slice(part * 128, (part + 1) * 128)
            rows_out[at, :] = down_ref[here, at].T
        rows_out[RANK : 2 * RANK, :] = (up_ref[:, here].astype(F32) * w).astype(BF16)
        v = w * (1.0 + bias_ref[:, here])
        high = v.astype(BF16).astype(F32)
        at = lax.broadcasted_iota(jnp.int32, (EXT, COLS), 0)
        rows_out[2 * RANK :, :] = jnp.where(at < 2, high, jnp.where(at == 2, v - high, 0.0)).astype(BF16)

    return call(
        body,
        [pltpu.VMEM((2 * RANK + EXT, COLS), BF16)],
        (place, *(near(v) for v in (down, up, w, bias))),
        [IN_SMEM] + [IN_VMEM] * 4,
        cost=pl.CostEstimate(flops=1 << 29, bytes_accessed=6 << 20, transcendentals=0),
    )[0]


def prepare_own(place, up, w, bias):
    def body(place_ref, up_ref, w_ref, bias_ref, own_out, up_out):
        k = place_ref[2] * NC + place_ref[3]
        start = place_ref[0] * COLS + (place_ref[1] * 2 + lax.div(k, 4)) * 128
        strip = pl.ds(pl.multiple_of(start, 128), 128)
        offset = lax.rem(k, 4) * 32
        lane = lax.broadcasted_iota(jnp.int32, (32, 128), 1)
        row = lax.broadcasted_iota(jnp.int32, (32, 128), 0)
        own = lane == row + offset
        w_own = jnp.sum(jnp.where(own, w_ref[:, strip], 0.0), axis=1, keepdims=True)
        bias_own = jnp.sum(jnp.where(own, bias_ref[:, strip], 0.0), axis=1, keepdims=True)
        place_own = (row + offset).astype(F32)
        own_out[...] = jnp.where(lane == 0, w_own, jnp.where(lane == 1, bias_own, place_own))
        up_out[...] = dot(jnp.where(own, 1.0, 0.0).astype(BF16), up_ref[:, strip], 1, 1)

    return call(
        body,
        [pltpu.VMEM((32, 128), F32), pltpu.VMEM((32, RANK), F32)],
        (place, *(near(v) for v in (up, w, bias))),
        [IN_SMEM] + [IN_VMEM] * 3,
        cost=pl.CostEstimate(flops=1 << 27, bytes_accessed=1 << 20, transcendentals=0),
    )


def pool_half(arrived):
    def body(in_ref, pooled_ref):
        for y in range(NY):
            at = slice(y * 512, (y + 1) * 512)
            half = slice(y * HALF, (y + 1) * HALF)
            pooled_ref[half, :] = dot(in_ref[at, SAMPLES:].T, in_ref[at, :SAMPLES], 1, 0).astype(BF16)

    return call(
        body,
        [pltpu.VMEM((NY * HALF, SAMPLES), BF16)],
        (near(arrived),),
        cost=pl.CostEstimate(flops=1 << 29, bytes_accessed=2 << 20, transcendentals=0),
    )[0]


def head_of(rows_ref, pooled):
    head = dot(rows_ref[2 * RANK :, :], pooled, 1, 0)
    sums = head[0:1] + head[2:3]
    high = sums.astype(BF16).astype(F32)
    at = lax.broadcasted_iota(jnp.int32, (EXT, pooled.shape[1]), 0)
    return jnp.where(at == 0, high, jnp.where(at == 1, sums - high, 0.0)).astype(BF16)


def products(rows_ref, pooled, outs):
    for part in range(4):
        at = slice(part * 256, (part + 1) * 256)
        product = dot(rows_ref[at, :], pooled, 1, 0).astype(BF16)
        for i, out in enumerate(outs):
            out[at, :] = product[:, i * OWN : (i + 1) * OWN]
    ext = head_of(rows_ref, pooled)
    for i, out in enumerate(outs):
        out[2 * RANK :, :] = ext[:, i * OWN : (i + 1) * OWN]


def forward_far(place, arrived, other, half, rows):
    def body(place_ref, in_ref, other_ref, half_ref, rows_ref, pooled_ref, out):
        core = place_ref[3]
        for y in range(NY):
            at = slice(y * 512, (y + 1) * 512)
            mine = pl.multiple_of(y * EMBED + core * HALF, HALF)
            partners = pl.multiple_of(y * EMBED + (1 - core) * HALF, HALF)
            pooled_ref[pl.ds(mine, HALF), :] = half_ref[y * HALF : (y + 1) * HALF, :]
            pooled_ref[pl.ds(partners, HALF), :] = dot(
                other_ref[at, :].T, in_ref[at, :SAMPLES], 1, 0
            ).astype(BF16)
        products(rows_ref, pooled_ref[:, OWN : 2 * OWN], (out,))

    return call(
        body,
        [pltpu.VMEM((COLS, SAMPLES), BF16), pltpu.VMEM((2 * RANK + EXT, OWN), BF16)],
        (place, near(arrived), near(other), near(half), near(rows)),
        [IN_SMEM] + [IN_VMEM] * 4,
        cost=pl.CostEstimate(flops=3 << 30, bytes_accessed=4 << 20, transcendentals=0),
    )


def forward_near(pooled, rows):
    def body(pooled_ref, rows_ref, *outs):
        products(rows_ref, pooled_ref[:, 2 * OWN :], outs)

    return call(
        body,
        [pltpu.VMEM((2 * RANK + EXT, OWN), BF16)] * 2,
        (near(pooled), near(rows)),
        cost=pl.CostEstimate(flops=1 << 30, bytes_accessed=2 << 20, transcendentals=0),
    )


def forward_own(pooled, rows):
    def body(pooled_ref, rows_ref, out):
        products(rows_ref, pooled_ref[:, :OWN], (out,))

    return call(
        body,
        [pltpu.VMEM((2 * RANK + EXT, OWN), BF16)],
        (near(pooled), near(rows)),
        cost=pl.CostEstimate(flops=1 << 30, bytes_accessed=1 << 20, transcendentals=0),
    )[0]


def own_samples(parts, labels):
    def body(p0, p1, p2, p3, labels_ref, out):
        def total(rows):
            a, b, c, d = (p[rows, :].astype(F32) for p in (p0, p1, p2, p3))
            return (a + b) + (c + d)

        squeezed = total(slice(0, RANK)).astype(BF16).astype(F32)
        other = total(slice(RANK, 2 * RANK))
        ext = total(slice(2 * RANK, 2 * RANK + EXT))
        logits = ext[0:1] + ext[1:2] + jnp.sum(squeezed * other, axis=0, keepdims=True)
        g = jax.nn.sigmoid(logits) - labels_ref[...].astype(F32)
        out[0:RANK, :] = (g * other).astype(BF16)
        out[RANK : 2 * RANK, :] = (g * squeezed).astype(BF16)
        high = g.astype(BF16).astype(F32)
        at = lax.broadcasted_iota(jnp.int32, (EXT, OWN), 0)
        rows = jnp.where((at == 0) | (at == 2), high, jnp.where(at == 1, g - high, 0.0))
        out[2 * RANK :, :] = rows.astype(BF16)

    return call(body, [pltpu.VMEM((2 * RANK + EXT, OWN), BF16)], (*(near(p) for p in parts), labels))[0]


def by_sample(*blocks):
    return jnp.concatenate([b[...].T for b in blocks], axis=0)


def grad_pooled_of(g, rows_ref):
    tables = [slice(y * EMBED, (y + 1) * EMBED) for y in range(NY)]
    return [dot(g, rows_ref[:, table], 1, 0).astype(BF16) for table in tables]


def backward_first(block0, block1, pooled, arrived, rows):
    def body(b0, b1, pooled_ref, in_ref, rows_ref, both_out, sums_out, slab_out):
        g = by_sample(b0, b1)
        products = grad_pooled_of(g, rows_ref)
        pooled = pooled_ref[:, : 2 * OWN]
        for j in range(4):
            at = slice(j * 256, (j + 1) * 256)
            both_out[:, at] = dot(pooled, g[:, at], 1, 0)
        ext = jnp.concatenate([b0[2 * RANK :, :], b1[2 * RANK :, :]], axis=1)
        sums_out[...] = dot(ext, pooled, 1, 1)
        for y, grad_pooled in enumerate(products):
            at = slice(y * 512, (y + 1) * 512)
            slab_out[at, :] = dot(in_ref[at, : 2 * OWN], grad_pooled, 1, 0)

    return call(
        body,
        [
            pltpu.VMEM((COLS, 2 * RANK), F32),
            pltpu.VMEM((EXT, COLS), F32),
            pltpu.VMEM((PEERS * ROWS, EMBED), F32),
        ],
        tuple(near(v) for v in (block0, block1, pooled, arrived, rows)),
        cost=pl.CostEstimate(flops=2 << 30, bytes_accessed=6 << 20, transcendentals=0),
    )


def put(low_core, mine, other, targets, at, value):
    pair = value.astype(BF16).reshape(-1, NC, *value.shape[1:])
    even, odd = pair[:, 0], pair[:, 1]
    mine[targets, at, :] = jnp.where(low_core, even, odd)
    other[targets, at, :] = jnp.where(low_core, odd, even)


EVERYONE = slice(0, NY * NX)


def backward_weights(place, block2, block3, pooled, both, sums):
    def body(place_ref, b2, b3, pooled_ref, both_ref, sums_ref, mine, other, g_out):
        low_core = place_ref[3] == 0
        g = by_sample(b2, b3)
        g_out[...] = g
        pooled = pooled_ref[:, 2 * OWN :]
        for j in range(4):
            value = dot(pooled, g[:, j * 256 : (j + 1) * 256], 1, 0)
            for h in range(2):
                at = (2 * j + h) * 128
                held = both_ref[:, at : at + 128] + value[:, h * 128 : (h + 1) * 128]
                to = slice((2 * j + h) * 32, (2 * j + h + 1) * 32)
                put(low_core, mine, other, EVERYONE, to, held.reshape(PEERS, 32, 128))
        ext = jnp.concatenate([b2[2 * RANK :, :], b3[2 * RANK :, :]], axis=1)
        held = (dot(ext, pooled, 1, 1) + sums_ref[...]).astype(BF16)
        for strip in range(8):
            row = held[:, strip * 128 : (strip + 1) * 128]
            for i in range(2):
                mine[strip * 2 + i, 256:, :] = row
                other[strip * 2 + i, 256:, :] = row

    return call(
        body,
        [pltpu.VMEM((NY * NX, 272, 128), BF16)] * 2 + [pltpu.VMEM((2 * OWN, 2 * RANK + EXT), BF16)],
        (place, *(near(v) for v in (block2, block3, pooled, both, sums))),
        [IN_SMEM] + [IN_VMEM] * 5,
        cost=pl.CostEstimate(flops=1 << 30, bytes_accessed=4 << 20, transcendentals=0),
    )


def backward_slab(place, g, arrived, rows, slab_first):
    def body(place_ref, g_ref, in_ref, rows_ref, first_ref, mine, other):
        low_core = place_ref[3] == 0
        for y, grad_pooled in enumerate(grad_pooled_of(g_ref[...], rows_ref)):
            at = slice(y * 512, (y + 1) * 512)
            slab = first_ref[at, :] + dot(in_ref[at, 2 * OWN : SAMPLES], grad_pooled, 1, 0)
            for j in range(2):
                put(
                    low_core,
                    mine,
                    other,
                    slice(y * NX, (y + 1) * NX),
                    slice(j * ROWS, (j + 1) * ROWS),
                    slab[:, j * 128 : (j + 1) * 128].reshape(NK, ROWS, 128),
                )

    return call(
        body,
        [pltpu.VMEM((NY * NX, 2 * ROWS, 128), BF16)] * 2,
        (place, *(near(v) for v in (g, arrived, rows, slab_first))),
        [IN_SMEM] + [IN_VMEM] * 4,
        cost=pl.CostEstimate(flops=1 << 30, bytes_accessed=4 << 20, transcendentals=0),
    )


def pair_sums(slab, slab_partner, weights, weights_partner):
    def body(a, b, c, d, out):
        out[:, : 2 * ROWS, :] = (a[...].astype(F32) + b[...].astype(F32)).astype(BF16)
        out[:, 2 * ROWS :, :] = (c[...].astype(F32) + d[...].astype(F32)).astype(BF16)

    return call(
        body,
        [pltpu.VMEM((NY * NX, PACK, 128), BF16)],
        tuple(near(v) for v in (slab, slab_partner, weights, weights_partner)),
    )[0]


def finish(shares, own, up_own):
    def body(in_ref, own_ref, up_ref, slab_out, down_out, up_out, bias_out, out_out):
        def total(at):
            held = in_ref[0, at, :].astype(F32)
            for i in range(1, NY * NX):
                held = held + in_ref[i, at, :].astype(F32)
            return held

        slab_out[:, :128] = total(slice(0, ROWS))
        slab_out[:, 128:] = total(slice(ROWS, 2 * ROWS))
        both = [total(slice(128 + j * 32, 160 + j * 32)) for j in range(8)]
        for j in range(4):
            down_out[:, j * 128 : (j + 1) * 128] = both[j].astype(BF16)
        product = jnp.concatenate(both[4:], axis=1)
        w_own, bias_own = own_ref[:, 0:1], own_ref[:, 1:2]
        up_out[...] = (product * w_own).astype(BF16)
        lane = lax.broadcasted_iota(jnp.int32, (32, 128), 1)
        row = lax.broadcasted_iota(jnp.int32, (32, 128), 0)
        last = total(slice(384, 400))
        own = lane.astype(F32) == own_ref[:, 2:3]
        sums = jnp.sum(jnp.where(own, last[0:1] + last[1:2], 0.0), axis=1, keepdims=True)
        out = (1.0 + bias_own) * sums + jnp.sum(product * up_ref[...], axis=1, keepdims=True)
        bias_out[...] = jnp.sum(jnp.where(lane == row, w_own * sums, 0.0), axis=0, keepdims=True)[:, :32]
        out_out[...] = jnp.sum(jnp.where(lane == row, out, 0.0), axis=0, keepdims=True)[:, :32]

    return call(
        body,
        [
            jax.ShapeDtypeStruct((ROWS, EMBED), F32),
            jax.ShapeDtypeStruct((32, RANK), BF16),
            jax.ShapeDtypeStruct((32, RANK), BF16),
            jax.ShapeDtypeStruct((1, 32), F32),
            jax.ShapeDtypeStruct((1, 32), F32),
        ],
        (near(shares), near(own), near(up_own)),
    )


def local(slab, counts, cross_down, cross_up, cross_bias, out_weight, labels):
    place = jnp.stack([lax.axis_index(a) for a in ALL]).astype(jnp.int32)
    w_row, bias_row = out_weight.reshape(1, -1), cross_bias.reshape(1, -1)
    rows = prepare(place, cross_down, cross_up, w_row, bias_row)
    own, up_own = prepare_own(place, cross_up, w_row, bias_row)
    sent = pack_counts(place, counts.T, slab)
    arrived = lax.all_to_all(sent, PLANE, 0, 0, tiled=True).reshape(PEERS * ROWS, SAMPLES + HALF)
    other = shift(arrived[:, SAMPLES:], dc=1)
    half = pool_half(arrived)
    pooled, chunk1 = forward_far(place, arrived, other, half, rows)
    part1 = shift(chunk1, dz=(ORDER[0][1], ORDER[1][1]))
    chunk2, chunk3 = forward_near(pooled, rows)
    part2 = shift(chunk2, dz=(ORDER[0][2], ORDER[1][2]))
    part3 = shift(chunk3, dz=(ORDER[0][3], ORDER[1][3]))
    parts = [part1, part2, part3]
    chunk = forward_own(pooled, rows)
    block0 = own_samples([chunk] + parts, labels.reshape(1, OWN))
    blocks = []
    for i in range(1, NZ):
        blocks.append(shift(block0, dz=(-ORDER[0][i], -ORDER[1][i])))
    block1, block2, block3 = blocks
    both, sums, slab_first = backward_first(block0, block1, pooled, arrived, rows)
    weights, given, g = backward_weights(place, block2, block3, pooled, both, sums)
    weights_partner = shift(given, dc=1)
    slabs, given = backward_slab(place, g, arrived, rows, slab_first)
    paired = pair_sums(slabs, shift(given, dc=1), weights, weights_partner)
    shares = lax.all_to_all(paired, ("y", "x"), 0, 0, tiled=True)
    grad_slab, grad_down, grad_up, grad_bias, grad_out = finish(shares, own, up_own)
    return grad_slab, grad_down, grad_up.T, grad_bias.reshape(32), grad_out.reshape(32)


def solution(mesh):
    torus = Mesh(mesh.devices.reshape(NZ, NY, NX, NC), ALL)
    return jax.shard_map(
        local,
        mesh=torus,
        in_specs=(P(ALL, None), P(None, ALL), P(), P(), P(), P(), P(ALL)),
        out_specs=(P(ALL, None), P(ALL, None), P(None, ALL), P(ALL), P(ALL)),
        check_vma=False,
    )
```

```python
import jax
import jax.numpy as jnp
from jax import lax
from jax.experimental import pallas as pl
from jax.experimental.pallas import tpu as pltpu
from jax.sharding import Mesh
from jax.sharding import PartitionSpec as P


ALL = ("z", "y", "x", "c")
PLANE = ("y", "x", "c")
NZ, NY, NX, NC = 4, 4, 4, 2
NK = NX * NC
PEERS = NY * NK
OWN = 128
ROWS = 64
EMBED = 256
RANK = 512
COLS = 1024
SAMPLES = NZ * OWN
EXT = 16
PACK = 400
HALF = EMBED // 2
LATE = SAMPLES // 2
ORDER = ((0, 2, 1, 3), (0, 2, 3, 1))
PLACES = ((0, 2, 1, 3), (0, 3, 1, 2))
F32 = jnp.float32
BF16 = jnp.bfloat16


def dot(a, b, da, db):
    return lax.dot_general(a, b, (((da,), (db,)), ((), ())), preferred_element_type=F32)


def flat(z, y, x, c):
    return (((z % NZ) * NY + y % NY) * NX + x % NX) * NC + c % NC


def shift(value, dz=(0, 0), dc=0):
    pairs = [
        (flat(z, y, x, c), flat(z + dz[c], y, x, c + dc))
        for z in range(NZ)
        for y in range(NY)
        for x in range(NX)
        for c in range(NC)
    ]
    return lax.ppermute(value, ALL, pairs)


def near(value):
    return pltpu.with_memory_space_constraint(value, pltpu.VMEM)


def far(value):
    return pltpu.with_memory_space_constraint(value, pltpu.HBM)


def call(body, outs, args, specs=None, scratch=(), mib=24, cost=None):
    return pl.pallas_call(
        body,
        in_specs=specs or [pl.BlockSpec(memory_space=pltpu.VMEM)] * len(args),
        out_specs=[pl.BlockSpec(memory_space=pltpu.VMEM)] * len(outs),
        out_shape=outs,
        scratch_shapes=list(scratch),
        compiler_params=pltpu.CompilerParams(vmem_limit_bytes=mib << 20),
        cost_estimate=cost,
    )(*args)


IN_SMEM = pl.BlockSpec(memory_space=pltpu.SMEM)
IN_VMEM = pl.BlockSpec(memory_space=pltpu.VMEM)
IN_HBM = pl.BlockSpec(memory_space=pltpu.HBM)


def pack_counts(place, counts_t, slab):
    strip = NK * OWN

    def body(place_ref, counts_ref, slab_ref, out, held, slab_s, sems, slab_sem):
        def copy(y, n):
            z = lax.rem(place_ref[0] + n, NZ)
            start = pl.multiple_of(z * (NY * strip) + y * strip, strip)
            return pltpu.make_async_copy(counts_ref.at[:, pl.ds(start, strip)], held.at[y, n], sems.at[y, n])

        slab_copy = pltpu.make_async_copy(slab_ref, slab_s, slab_sem)
        slab_copy.start()
        for y in range(NY):
            for n in range(NZ):
                copy(y, n).start()
        slab_copy.wait()
        for k in range(PEERS):
            half = k % NC
            out[k, :, SAMPLES:] = slab_s[:, half * HALF : (half + 1) * HALF]
        for y in range(NY):
            for n in range(NZ):
                copy(y, n).wait()
                for k in range(NK):
                    to = PLACES[k % NC][n] * OWN
                    out[y * NK + k, :, to : to + OWN] = (
                        held[y, n, :, k * OWN : (k + 1) * OWN].astype(F32).astype(BF16)
                    )

    return call(
        body,
        [pltpu.VMEM((PEERS, ROWS, SAMPLES + HALF), BF16)],
        (place, far(counts_t), far(slab)),
        [IN_SMEM, IN_HBM, IN_HBM],
        [
            pltpu.VMEM((NY, NZ, ROWS, strip), jnp.int32),
            pltpu.VMEM((ROWS, EMBED), BF16),
            pltpu.SemaphoreType.DMA((NY, NZ)),
            pltpu.SemaphoreType.DMA,
        ],
    )[0]


def prepare(place, down, up, w, bias):
    def body(place_ref, down_ref, up_ref, w_ref, bias_ref, rows_out):
        here = pl.ds(pl.multiple_of(place_ref[0] * COLS, COLS), COLS)
        w = w_ref[:, here]
        for part in range(4):
            at = slice(part * 128, (part + 1) * 128)
            rows_out[at, :] = down_ref[here, at].T
        rows_out[RANK : 2 * RANK, :] = (up_ref[:, here].astype(F32) * w).astype(BF16)
        v = w * (1.0 + bias_ref[:, here])
        high = v.astype(BF16).astype(F32)
        at = lax.broadcasted_iota(jnp.int32, (EXT, COLS), 0)
        rows_out[2 * RANK :, :] = jnp.where(at < 2, high, jnp.where(at == 2, v - high, 0.0)).astype(BF16)

    return call(
        body,
        [pltpu.VMEM((2 * RANK + EXT, COLS), BF16)],
        (place, *(near(v) for v in (down, up, w, bias))),
        [IN_SMEM] + [IN_VMEM] * 4,
        cost=pl.CostEstimate(flops=1 << 29, bytes_accessed=6 << 20, transcendentals=0),
    )[0]


def prepare_own(place, up, w, bias):
    def body(place_ref, up_ref, w_ref, bias_ref, own_out, up_out):
        k = place_ref[2] * NC + place_ref[3]
        start = place_ref[0] * COLS + (place_ref[1] * 2 + lax.div(k, 4)) * 128
        strip = pl.ds(pl.multiple_of(start, 128), 128)
        offset = lax.rem(k, 4) * 32
        lane = lax.broadcasted_iota(jnp.int32, (32, 128), 1)
        row = lax.broadcasted_iota(jnp.int32, (32, 128), 0)
        own = lane == row + offset
        w_own = jnp.sum(jnp.where(own, w_ref[:, strip], 0.0), axis=1, keepdims=True)
        bias_own = jnp.sum(jnp.where(own, bias_ref[:, strip], 0.0), axis=1, keepdims=True)
        place_own = (row + place_ref[2] * 32).astype(F32)
        own_out[...] = jnp.where(lane == 0, w_own, jnp.where(lane == 1, bias_own, place_own))
        up_out[...] = dot(jnp.where(own, 1.0, 0.0).astype(BF16), up_ref[:, strip], 1, 1)

    return call(
        body,
        [pltpu.VMEM((32, 128), F32), pltpu.VMEM((32, RANK), F32)],
        (place, *(near(v) for v in (up, w, bias))),
        [IN_SMEM] + [IN_VMEM] * 3,
        cost=pl.CostEstimate(flops=1 << 27, bytes_accessed=1 << 20, transcendentals=0),
    )


def pool_half(arrived):
    def body(in_ref, pooled_ref):
        for y in range(NY):
            at = slice(y * 512, (y + 1) * 512)
            half = slice(y * HALF, (y + 1) * HALF)
            pooled_ref[half, :] = dot(in_ref[at, SAMPLES:].T, in_ref[at, :SAMPLES], 1, 0).astype(BF16)

    return call(
        body,
        [pltpu.VMEM((NY * HALF, SAMPLES), BF16)],
        (near(arrived),),
        cost=pl.CostEstimate(flops=1 << 29, bytes_accessed=2 << 20, transcendentals=0),
    )[0]


def head_of(rows_ref, pooled):
    head = dot(rows_ref[2 * RANK :, :], pooled, 1, 0)
    sums = head[0:1] + head[2:3]
    high = sums.astype(BF16).astype(F32)
    at = lax.broadcasted_iota(jnp.int32, (EXT, pooled.shape[1]), 0)
    return jnp.where(at == 0, high, jnp.where(at == 1, sums - high, 0.0)).astype(BF16)


def products(rows_ref, pooled, outs):
    for part in range(4):
        at = slice(part * 256, (part + 1) * 256)
        product = dot(rows_ref[at, :], pooled, 1, 0).astype(BF16)
        for i, out in enumerate(outs):
            out[at, :] = product[:, i * OWN : (i + 1) * OWN]
    ext = head_of(rows_ref, pooled)
    for i, out in enumerate(outs):
        out[2 * RANK :, :] = ext[:, i * OWN : (i + 1) * OWN]


def forward_far(place, arrived, other, half, rows):
    def body(place_ref, in_ref, other_ref, half_ref, rows_ref, pooled_ref, out):
        core = place_ref[3]
        for y in range(NY):
            at = slice(y * 512, (y + 1) * 512)
            mine = pl.multiple_of(y * EMBED + core * HALF, HALF)
            partners = pl.multiple_of(y * EMBED + (1 - core) * HALF, HALF)
            pooled_ref[pl.ds(mine, HALF), :] = half_ref[y * HALF : (y + 1) * HALF, :]
            pooled_ref[pl.ds(partners, HALF), :] = dot(
                other_ref[at, :].T, in_ref[at, :SAMPLES], 1, 0
            ).astype(BF16)
        products(rows_ref, pooled_ref[:, OWN : 2 * OWN], (out,))

    return call(
        body,
        [pltpu.VMEM((COLS, SAMPLES), BF16), pltpu.VMEM((2 * RANK + EXT, OWN), BF16)],
        (place, near(arrived), near(other), near(half), near(rows)),
        [IN_SMEM] + [IN_VMEM] * 4,
        cost=pl.CostEstimate(flops=3 << 30, bytes_accessed=4 << 20, transcendentals=0),
    )


def forward_near(pooled, rows):
    def body(pooled_ref, rows_ref, *outs):
        products(rows_ref, pooled_ref[:, 2 * OWN :], outs)

    return call(
        body,
        [pltpu.VMEM((2 * RANK + EXT, OWN), BF16)] * 2,
        (near(pooled), near(rows)),
        cost=pl.CostEstimate(flops=1 << 30, bytes_accessed=2 << 20, transcendentals=0),
    )


def forward_own(pooled, rows):
    def body(pooled_ref, rows_ref, out):
        products(rows_ref, pooled_ref[:, :OWN], (out,))

    return call(
        body,
        [pltpu.VMEM((2 * RANK + EXT, OWN), BF16)],
        (near(pooled), near(rows)),
        cost=pl.CostEstimate(flops=1 << 30, bytes_accessed=1 << 20, transcendentals=0),
    )[0]


def own_samples(parts, labels):
    def body(p0, p1, p2, p3, labels_ref, out):
        def total(rows):
            a, b, c, d = (p[rows, :].astype(F32) for p in (p0, p1, p2, p3))
            return (a + b) + (c + d)

        squeezed = total(slice(0, RANK)).astype(BF16).astype(F32)
        other = total(slice(RANK, 2 * RANK))
        ext = total(slice(2 * RANK, 2 * RANK + EXT))
        logits = ext[0:1] + ext[1:2] + jnp.sum(squeezed * other, axis=0, keepdims=True)
        g = jax.nn.sigmoid(logits) - labels_ref[...].astype(F32)
        out[0:RANK, :] = (g * other).astype(BF16)
        out[RANK : 2 * RANK, :] = (g * squeezed).astype(BF16)
        high = g.astype(BF16).astype(F32)
        at = lax.broadcasted_iota(jnp.int32, (EXT, OWN), 0)
        rows = jnp.where((at == 0) | (at == 2), high, jnp.where(at == 1, g - high, 0.0))
        out[2 * RANK :, :] = rows.astype(BF16)

    return call(body, [pltpu.VMEM((2 * RANK + EXT, OWN), BF16)], (*(near(p) for p in parts), labels))[0]


def by_sample(*blocks):
    return jnp.concatenate([b[...].T for b in blocks], axis=0)


def grad_pooled_of(g, rows_ref):
    tables = [slice(y * EMBED, (y + 1) * EMBED) for y in range(NY)]
    return [dot(g, rows_ref[:, table], 1, 0).astype(BF16) for table in tables]


def by_core(low_core, value, width):
    pairs = value.reshape(-1, NC, width, value.shape[1])
    even, odd = (pairs[:, c].reshape(-1, value.shape[1]) for c in range(NC))
    return jnp.where(low_core, even, odd), jnp.where(low_core, odd, even)


def late_values(place, pooled, arrived):
    def body(place_ref, pooled_ref, in_ref, mine, theirs):
        low_core = place_ref[3] == 0
        half = COLS // NC
        mine[:half, :], theirs[:half, :] = by_core(low_core, pooled_ref[:, LATE:], 32)
        for y in range(NY):
            rows = slice(half + y * 256, half + (y + 1) * 256)
            counts = in_ref[y * 512 : (y + 1) * 512, LATE:SAMPLES]
            mine[rows, :], theirs[rows, :] = by_core(low_core, counts, ROWS)

    return call(
        body,
        [pltpu.VMEM((COLS // NC + NY * 256, SAMPLES - LATE), BF16)] * 2,
        (place, near(pooled), near(arrived)),
        [IN_SMEM] + [IN_VMEM] * 2,
        cost=pl.CostEstimate(flops=1 << 27, bytes_accessed=2 << 20, transcendentals=0),
    )


def put_weights(out, first, j, value):
    for h in range(2):
        at = first + (2 * j + h) * 32
        held = value[:, h * 128 : (h + 1) * 128].reshape(NY * NX, 32, 128)
        out(slice(0, NY * NX), slice(at, at + 32), held)


def put_sums(out, first, value):
    for y in range(NY):
        row = value[:, y * 128 : (y + 1) * 128]
        for x in range(NX):
            out(y * NX + x, slice(first, first + EXT), row)


def put_slab(out, y, value):
    for h in range(2):
        held = value[:, h * 128 : (h + 1) * 128].reshape(NX, ROWS, 128)
        out(slice(y * NX, (y + 1) * NX), slice(h * ROWS, (h + 1) * ROWS), held)


def backward_first(place, block0, block1, pooled, arrived, rows):
    def body(place_ref, b0, b1, pooled_ref, in_ref, rows_ref, mine, theirs):
        low_core = place_ref[3] == 0
        g = by_sample(b0, b1)
        products = grad_pooled_of(g, rows_ref)
        ext = jnp.concatenate([b0[2 * RANK :, :], b1[2 * RANK :, :]], axis=1)

        def writer(ref):
            def write(targets, at, value):
                ref[targets, at, :] = value.astype(ref.dtype)

            return write

        outs = [writer(mine), writer(theirs)]
        for out, part in zip(outs, by_core(low_core, pooled_ref[:, :LATE], 32)):
            for j in range(4):
                put_weights(out, 2 * ROWS, j, dot(part, g[:, j * 256 : (j + 1) * 256], 1, 0))
            put_sums(out, 384, dot(ext, part, 1, 1))
        for y, grad_pooled in enumerate(products):
            counts = in_ref[y * 512 : (y + 1) * 512, :LATE]
            for out, part in zip(outs, by_core(low_core, counts, ROWS)):
                put_slab(out, y, dot(part, grad_pooled, 1, 0))

    return call(
        body,
        [pltpu.VMEM((NY * NX, PACK, 128), F32), pltpu.VMEM((NY * NX, PACK, 128), BF16)],
        (place, *(near(v) for v in (block0, block1, pooled, arrived, rows))),
        [IN_SMEM] + [IN_VMEM] * 5,
        cost=pl.CostEstimate(flops=2 << 30, bytes_accessed=6 << 20, transcendentals=0),
    )


def late_products(block2, block3, rows):
    def body(b2, b3, rows_ref, g_out, out):
        g = by_sample(b2, b3)
        g_out[...] = g
        for y, grad_pooled in enumerate(grad_pooled_of(g, rows_ref)):
            out[:, y * EMBED : (y + 1) * EMBED] = grad_pooled

    return call(
        body,
        [pltpu.VMEM((SAMPLES - LATE, 2 * RANK + EXT), BF16), pltpu.VMEM((SAMPLES - LATE, COLS), BF16)],
        tuple(near(v) for v in (block2, block3, rows)),
        cost=pl.CostEstimate(flops=1 << 30, bytes_accessed=4 << 20, transcendentals=0),
    )


def late_own(g, blocks, values, first):
    def body(g_ref, b2, b3, own_ref, first_ref, out):
        pooled = own_ref[: COLS // NC, :]

        def write(targets, at, value):
            shifted = slice(at.start + 2 * ROWS, at.stop + 2 * ROWS)
            out[targets, at, :] = first_ref[targets, shifted, :] + value

        for j in range(4):
            put_weights(write, 0, j, dot(pooled, g_ref[:, j * 256 : (j + 1) * 256], 1, 0))
        ext = jnp.concatenate([b2[2 * RANK :, :], b3[2 * RANK :, :]], axis=1)
        put_sums(write, 256, dot(ext, pooled, 1, 1))

    return call(
        body,
        [pltpu.VMEM((NY * NX, PACK - 2 * ROWS, 128), F32)],
        tuple(near(v) for v in (g, *blocks, values, first)),
        cost=pl.CostEstimate(flops=1 << 30, bytes_accessed=4 << 20, transcendentals=0),
    )[0]


def late_weights(blocks, values, so_far, first):
    def body(b2, b3, values_ref, so_far_ref, first_ref, out):
        pooled = values_ref[: COLS // NC, :]
        g = by_sample(b2, b3)

        def write(targets, at, value):
            shifted = slice(at.start + 2 * ROWS, at.stop + 2 * ROWS)
            held = so_far_ref[targets, at, :] + first_ref[targets, shifted, :].astype(F32)
            out[targets, at, :] = (held + value).astype(BF16)

        for j in range(4):
            put_weights(write, 0, j, dot(pooled, g[:, j * 256 : (j + 1) * 256], 1, 0))
        ext = jnp.concatenate([b2[2 * RANK :, :], b3[2 * RANK :, :]], axis=1)
        put_sums(write, 256, dot(ext, pooled, 1, 1))

    return call(
        body,
        [pltpu.VMEM((NY * NX, PACK - 2 * ROWS, 128), BF16)],
        tuple(near(v) for v in (*blocks, values, so_far, first)),
        cost=pl.CostEstimate(flops=1 << 30, bytes_accessed=4 << 20, transcendentals=0),
    )[0]


def late_slab(products, partner_products, values, partner_values, first, partner_first, weights):
    def body(own_products, their_products, own_ref, partner_ref, first_ref, other_ref, weights_ref, out):
        half = COLS // NC
        out[:, 2 * ROWS :, :] = weights_ref[...]

        def write(targets, at, value):
            held = first_ref[targets, at, :] + other_ref[targets, at, :].astype(F32)
            out[targets, at, :] = (held + value).astype(BF16)

        for y in range(NY):
            rows = slice(half + y * 256, half + (y + 1) * 256)
            table = slice(y * EMBED, (y + 1) * EMBED)
            counts = jnp.concatenate([own_ref[rows, :], partner_ref[rows, :]], axis=1)
            both = jnp.concatenate([own_products[:, table], their_products[:, table]], axis=0)
            put_slab(write, y, dot(counts, both, 1, 0))

    return call(
        body,
        [pltpu.VMEM((NY * NX, PACK, 128), BF16)],
        tuple(
            near(v)
            for v in (products, partner_products, values, partner_values, first, partner_first, weights)
        ),
        cost=pl.CostEstimate(flops=1 << 29, bytes_accessed=4 << 20, transcendentals=0),
    )[0]


def finish(shares, own, up_own):
    def body(in_ref, own_ref, up_ref, slab_out, down_out, up_out, bias_out, out_out):
        def total(at):
            held = [(in_ref[i, at, :] + in_ref[i + 1, at, :]).astype(F32) for i in range(0, NY * NX, 2)]
            while len(held) > 1:
                held = [a + b for a, b in zip(held[::2], held[1::2])]
            return held[0]

        slab_out[:, :128] = total(slice(0, ROWS))
        slab_out[:, 128:] = total(slice(ROWS, 2 * ROWS))
        both = [total(slice(128 + j * 32, 160 + j * 32)) for j in range(8)]
        for j in range(4):
            down_out[:, j * 128 : (j + 1) * 128] = both[j].astype(BF16)
        product = jnp.concatenate(both[4:], axis=1)
        w_own, bias_own = own_ref[:, 0:1], own_ref[:, 1:2]
        up_out[...] = (product * w_own).astype(BF16)
        lane = lax.broadcasted_iota(jnp.int32, (32, 128), 1)
        row = lax.broadcasted_iota(jnp.int32, (32, 128), 0)
        last = total(slice(384, 400))
        own = lane.astype(F32) == own_ref[:, 2:3]
        sums = jnp.sum(jnp.where(own, last[0:1] + last[1:2], 0.0), axis=1, keepdims=True)
        out = (1.0 + bias_own) * sums + jnp.sum(product * up_ref[...], axis=1, keepdims=True)
        bias_out[...] = jnp.sum(jnp.where(lane == row, w_own * sums, 0.0), axis=0, keepdims=True)[:, :32]
        out_out[...] = jnp.sum(jnp.where(lane == row, out, 0.0), axis=0, keepdims=True)[:, :32]

    return call(
        body,
        [
            jax.ShapeDtypeStruct((ROWS, EMBED), F32),
            jax.ShapeDtypeStruct((32, RANK), BF16),
            jax.ShapeDtypeStruct((32, RANK), BF16),
            jax.ShapeDtypeStruct((1, 32), F32),
            jax.ShapeDtypeStruct((1, 32), F32),
        ],
        (near(shares), near(own), near(up_own)),
    )


def local(slab, counts, cross_down, cross_up, cross_bias, out_weight, labels):
    place = jnp.stack([lax.axis_index(a) for a in ALL]).astype(jnp.int32)
    w_row, bias_row = out_weight.reshape(1, -1), cross_bias.reshape(1, -1)
    rows = prepare(place, cross_down, cross_up, w_row, bias_row)
    own, up_own = prepare_own(place, cross_up, w_row, bias_row)
    sent = pack_counts(place, counts.T, slab)
    arrived = lax.all_to_all(sent, PLANE, 0, 0, tiled=True).reshape(PEERS * ROWS, SAMPLES + HALF)
    other = shift(arrived[:, SAMPLES:], dc=1)
    half = pool_half(arrived)
    pooled, chunk1 = forward_far(place, arrived, other, half, rows)
    part1 = shift(chunk1, dz=(ORDER[0][1], ORDER[1][1]))
    chunk2, chunk3 = forward_near(pooled, rows)
    part2 = shift(chunk2, dz=(ORDER[0][2], ORDER[1][2]))
    part3 = shift(chunk3, dz=(ORDER[0][3], ORDER[1][3]))
    parts = [part1, part2, part3]
    chunk = forward_own(pooled, rows)
    values, theirs = late_values(place, pooled, arrived)
    partner_values = shift(theirs, dc=1)
    block0 = own_samples([chunk] + parts, labels.reshape(1, OWN))
    blocks = []
    for i in range(1, NZ):
        blocks.append(shift(block0, dz=(-ORDER[0][i], -ORDER[1][i])))
    block1, *late = blocks
    first, theirs = backward_first(place, block0, block1, pooled, arrived, rows)
    partner_first = shift(theirs, dc=1)
    partner_late = []
    for block in late:
        partner_late.append(shift(block, dc=1))
    g, products = late_products(*late, rows)
    partner_products = shift(products, dc=1)
    so_far = late_own(g, late, values, first)
    weights = late_weights(partner_late, partner_values, so_far, partner_first)
    summed = late_slab(products, partner_products, values, partner_values, first, partner_first, weights)
    shares = lax.all_to_all(summed, ("y", "x"), 0, 0, tiled=True)
    grad_slab, grad_down, grad_up, grad_bias, grad_out = finish(shares, own, up_own)
    return grad_slab, grad_down, grad_up.T, grad_bias.reshape(32), grad_out.reshape(32)


def solution(mesh):
    torus = Mesh(mesh.devices.reshape(NZ, NY, NX, NC), ALL)
    return jax.shard_map(
        local,
        mesh=torus,
        in_specs=(P(ALL, None), P(None, ALL), P(), P(), P(), P(), P(ALL)),
        out_specs=(P(ALL, None), P(ALL, None), P(None, ALL), P(ALL), P(ALL)),
        check_vma=False,
    )
```

```python
import jax
import jax.numpy as jnp
from jax import lax
from jax.experimental import pallas as pl
from jax.experimental.pallas import tpu as pltpu
from jax.sharding import Mesh
from jax.sharding import PartitionSpec as P


ALL = ("z", "y", "x", "c")
PLANE = ("y", "x", "c")
NZ, NY, NX, NC = 4, 4, 4, 2
NK = NX * NC
PEERS = NY * NK
OWN = 128
ROWS = 64
EMBED = 256
RANK = 512
COLS = 1024
SAMPLES = NZ * OWN
EXT = 16
PACK = 400
HALF = EMBED // 2
LATE = SAMPLES // 2
ORDER = ((0, 2, 1, 3), (0, 2, 3, 1))
PLACES = ((0, 2, 1, 3), (0, 3, 1, 2))
F32 = jnp.float32
BF16 = jnp.bfloat16


def dot(a, b, da, db):
    return lax.dot_general(a, b, (((da,), (db,)), ((), ())), preferred_element_type=F32)


def flat(z, y, x, c):
    return (((z % NZ) * NY + y % NY) * NX + x % NX) * NC + c % NC


def shift(value, dz=(0, 0), dc=0):
    pairs = [
        (flat(z, y, x, c), flat(z + dz[c], y, x, c + dc))
        for z in range(NZ)
        for y in range(NY)
        for x in range(NX)
        for c in range(NC)
    ]
    return lax.ppermute(value, ALL, pairs)


def near(value):
    return pltpu.with_memory_space_constraint(value, pltpu.VMEM)


def far(value):
    return pltpu.with_memory_space_constraint(value, pltpu.HBM)


def call(body, outs, args, specs=None, scratch=(), mib=24, cost=None):
    return pl.pallas_call(
        body,
        in_specs=specs or [pl.BlockSpec(memory_space=pltpu.VMEM)] * len(args),
        out_specs=[pl.BlockSpec(memory_space=pltpu.VMEM)] * len(outs),
        out_shape=outs,
        scratch_shapes=list(scratch),
        compiler_params=pltpu.CompilerParams(vmem_limit_bytes=mib << 20),
        cost_estimate=cost,
    )(*args)


IN_SMEM = pl.BlockSpec(memory_space=pltpu.SMEM)
IN_VMEM = pl.BlockSpec(memory_space=pltpu.VMEM)
IN_HBM = pl.BlockSpec(memory_space=pltpu.HBM)


def pack_counts(place, counts_t, slab):
    strip = NK * OWN

    def body(place_ref, counts_ref, slab_ref, out, held, slab_s, sems, slab_sem):
        def copy(y, n):
            z = lax.rem(place_ref[0] + n, NZ)
            start = pl.multiple_of(z * (NY * strip) + y * strip, strip)
            return pltpu.make_async_copy(counts_ref.at[:, pl.ds(start, strip)], held.at[y, n], sems.at[y, n])

        slab_copy = pltpu.make_async_copy(slab_ref, slab_s, slab_sem)
        slab_copy.start()
        for y in range(NY):
            for n in range(NZ):
                copy(y, n).start(priority=n % 2)
        slab_copy.wait()
        for k in range(PEERS):
            half = k % NC
            out[k, :, SAMPLES:] = slab_s[:, half * HALF : (half + 1) * HALF]
        for y in range(NY):
            for n in range(NZ):
                copy(y, n).wait()
                for k in range(NK):
                    to = PLACES[k % NC][n] * OWN
                    out[y * NK + k, :, to : to + OWN] = (
                        held[y, n, :, k * OWN : (k + 1) * OWN].astype(F32).astype(BF16)
                    )

    return call(
        body,
        [pltpu.VMEM((PEERS, ROWS, SAMPLES + HALF), BF16)],
        (place, far(counts_t), far(slab)),
        [IN_SMEM, IN_HBM, IN_HBM],
        [
            pltpu.VMEM((NY, NZ, ROWS, strip), jnp.int32),
            pltpu.VMEM((ROWS, EMBED), BF16),
            pltpu.SemaphoreType.DMA((NY, NZ)),
            pltpu.SemaphoreType.DMA,
        ],
    )[0]


def prepare(place, down, up, w, bias):
    def body(place_ref, down_ref, up_ref, w_ref, bias_ref, rows_out):
        here = pl.ds(pl.multiple_of(place_ref[0] * COLS, COLS), COLS)
        w = w_ref[:, here]
        for part in range(4):
            at = slice(part * 128, (part + 1) * 128)
            rows_out[at, :] = down_ref[here, at].T
        rows_out[RANK : 2 * RANK, :] = (up_ref[:, here].astype(F32) * w).astype(BF16)
        v = w * (1.0 + bias_ref[:, here])
        high = v.astype(BF16).astype(F32)
        at = lax.broadcasted_iota(jnp.int32, (EXT, COLS), 0)
        rows_out[2 * RANK :, :] = jnp.where(at < 2, high, jnp.where(at == 2, v - high, 0.0)).astype(BF16)

    return call(
        body,
        [pltpu.VMEM((2 * RANK + EXT, COLS), BF16)],
        (place, *(near(v) for v in (down, up, w, bias))),
        [IN_SMEM] + [IN_VMEM] * 4,
        cost=pl.CostEstimate(flops=1 << 29, bytes_accessed=6 << 20, transcendentals=0),
    )[0]


def prepare_own(place, up, w, bias):
    def body(place_ref, up_ref, w_ref, bias_ref, own_out, up_out):
        k = place_ref[2] * NC + place_ref[3]
        start = place_ref[0] * COLS + (place_ref[1] * 2 + lax.div(k, 4)) * 128
        strip = pl.ds(pl.multiple_of(start, 128), 128)
        offset = lax.rem(k, 4) * 32
        lane = lax.broadcasted_iota(jnp.int32, (32, 128), 1)
        row = lax.broadcasted_iota(jnp.int32, (32, 128), 0)
        own = lane == row + offset
        w_own = jnp.sum(jnp.where(own, w_ref[:, strip], 0.0), axis=1, keepdims=True)
        bias_own = jnp.sum(jnp.where(own, bias_ref[:, strip], 0.0), axis=1, keepdims=True)
        place_own = (row + place_ref[2] * 32).astype(F32)
        own_out[...] = jnp.where(lane == 0, w_own, jnp.where(lane == 1, bias_own, place_own))
        up_out[...] = dot(jnp.where(own, 1.0, 0.0).astype(BF16), up_ref[:, strip], 1, 1)

    return call(
        body,
        [pltpu.VMEM((32, 128), F32), pltpu.VMEM((32, RANK), F32)],
        (place, *(near(v) for v in (up, w, bias))),
        [IN_SMEM] + [IN_VMEM] * 3,
        cost=pl.CostEstimate(flops=1 << 27, bytes_accessed=1 << 20, transcendentals=0),
    )


def pool_half(arrived):
    def body(in_ref, pooled_ref):
        for y in range(NY):
            at = slice(y * 512, (y + 1) * 512)
            half = slice(y * HALF, (y + 1) * HALF)
            pooled_ref[half, :] = dot(in_ref[at, SAMPLES:].T, in_ref[at, :SAMPLES], 1, 0).astype(BF16)

    return call(
        body,
        [pltpu.VMEM((NY * HALF, SAMPLES), BF16)],
        (near(arrived),),
        cost=pl.CostEstimate(flops=1 << 29, bytes_accessed=2 << 20, transcendentals=0),
    )[0]


def head_of(rows_ref, pooled):
    head = dot(rows_ref[2 * RANK :, :], pooled, 1, 0)
    sums = head[0:1] + head[2:3]
    high = sums.astype(BF16).astype(F32)
    at = lax.broadcasted_iota(jnp.int32, (EXT, pooled.shape[1]), 0)
    return jnp.where(at == 0, high, jnp.where(at == 1, sums - high, 0.0)).astype(BF16)


def products(rows_ref, pooled, outs):
    for part in range(4):
        at = slice(part * 256, (part + 1) * 256)
        product = dot(rows_ref[at, :], pooled, 1, 0).astype(BF16)
        for i, out in enumerate(outs):
            out[at, :] = product[:, i * OWN : (i + 1) * OWN]
    ext = head_of(rows_ref, pooled)
    for i, out in enumerate(outs):
        out[2 * RANK :, :] = ext[:, i * OWN : (i + 1) * OWN]


def forward_far(place, arrived, other, half, rows):
    def body(place_ref, in_ref, other_ref, half_ref, rows_ref, pooled_ref, out):
        core = place_ref[3]
        for y in range(NY):
            at = slice(y * 512, (y + 1) * 512)
            mine = pl.multiple_of(y * EMBED + core * HALF, HALF)
            partners = pl.multiple_of(y * EMBED + (1 - core) * HALF, HALF)
            pooled_ref[pl.ds(mine, HALF), :] = half_ref[y * HALF : (y + 1) * HALF, :]
            pooled_ref[pl.ds(partners, HALF), :] = dot(
                other_ref[at, :].T, in_ref[at, :SAMPLES], 1, 0
            ).astype(BF16)
        products(rows_ref, pooled_ref[:, OWN : 2 * OWN], (out,))

    return call(
        body,
        [pltpu.VMEM((COLS, SAMPLES), BF16), pltpu.VMEM((2 * RANK + EXT, OWN), BF16)],
        (place, near(arrived), near(other), near(half), near(rows)),
        [IN_SMEM] + [IN_VMEM] * 4,
        cost=pl.CostEstimate(flops=3 << 30, bytes_accessed=4 << 20, transcendentals=0),
    )


def forward_near(pooled, rows):
    def body(pooled_ref, rows_ref, *outs):
        products(rows_ref, pooled_ref[:, 2 * OWN :], outs)

    return call(
        body,
        [pltpu.VMEM((2 * RANK + EXT, OWN), BF16)] * 2,
        (near(pooled), near(rows)),
        cost=pl.CostEstimate(flops=1 << 30, bytes_accessed=2 << 20, transcendentals=0),
    )


def forward_own(pooled, rows):
    def body(pooled_ref, rows_ref, out):
        products(rows_ref, pooled_ref[:, :OWN], (out,))

    return call(
        body,
        [pltpu.VMEM((2 * RANK + EXT, OWN), BF16)],
        (near(pooled), near(rows)),
        cost=pl.CostEstimate(flops=1 << 30, bytes_accessed=1 << 20, transcendentals=0),
    )[0]


def own_samples(parts, labels):
    def body(p0, p1, p2, p3, labels_ref, out):
        def total(rows):
            a, b, c, d = (p[rows, :].astype(F32) for p in (p0, p1, p2, p3))
            return (a + b) + (c + d)

        squeezed = total(slice(0, RANK)).astype(BF16).astype(F32)
        other = total(slice(RANK, 2 * RANK))
        ext = total(slice(2 * RANK, 2 * RANK + EXT))
        logits = ext[0:1] + ext[1:2] + jnp.sum(squeezed * other, axis=0, keepdims=True)
        g = jax.nn.sigmoid(logits) - labels_ref[...].astype(F32)
        out[0:RANK, :] = (g * other).astype(BF16)
        out[RANK : 2 * RANK, :] = (g * squeezed).astype(BF16)
        high = g.astype(BF16).astype(F32)
        at = lax.broadcasted_iota(jnp.int32, (EXT, OWN), 0)
        rows = jnp.where((at == 0) | (at == 2), high, jnp.where(at == 1, g - high, 0.0))
        out[2 * RANK :, :] = rows.astype(BF16)

    return call(body, [pltpu.VMEM((2 * RANK + EXT, OWN), BF16)], (*(near(p) for p in parts), labels))[0]


def by_sample(*blocks):
    return jnp.concatenate([b[...].T for b in blocks], axis=0)


def grad_pooled_of(g, rows_ref):
    tables = [slice(y * EMBED, (y + 1) * EMBED) for y in range(NY)]
    return [dot(g, rows_ref[:, table], 1, 0).astype(BF16) for table in tables]


def by_core(low_core, value, width):
    pairs = value.reshape(-1, NC, width, value.shape[1])
    even, odd = (pairs[:, c].reshape(-1, value.shape[1]) for c in range(NC))
    return jnp.where(low_core, even, odd), jnp.where(low_core, odd, even)


def late_values(place, pooled, arrived):
    def body(place_ref, pooled_ref, in_ref, mine, theirs):
        low_core = place_ref[3] == 0
        half = COLS // NC
        mine[:half, :], theirs[:half, :] = by_core(low_core, pooled_ref[:, LATE:], 32)
        for y in range(NY):
            rows = slice(half + y * 256, half + (y + 1) * 256)
            counts = in_ref[y * 512 : (y + 1) * 512, LATE:SAMPLES]
            mine[rows, :], theirs[rows, :] = by_core(low_core, counts, ROWS)

    return call(
        body,
        [pltpu.VMEM((COLS // NC + NY * 256, SAMPLES - LATE), BF16)] * 2,
        (place, near(pooled), near(arrived)),
        [IN_SMEM] + [IN_VMEM] * 2,
        cost=pl.CostEstimate(flops=1 << 27, bytes_accessed=2 << 20, transcendentals=0),
    )


def put_weights(out, first, j, value):
    for h in range(2):
        at = first + (2 * j + h) * 32
        held = value[:, h * 128 : (h + 1) * 128].reshape(NY * NX, 32, 128)
        out(slice(0, NY * NX), slice(at, at + 32), held)


def put_sums(out, first, value):
    for y in range(NY):
        row = value[:, y * 128 : (y + 1) * 128]
        for x in range(NX):
            out(y * NX + x, slice(first, first + EXT), row)


def put_slab(out, y, value):
    for h in range(2):
        held = value[:, h * 128 : (h + 1) * 128].reshape(NX, ROWS, 128)
        out(slice(y * NX, (y + 1) * NX), slice(h * ROWS, (h + 1) * ROWS), held)


def backward_first(place, block0, block1, pooled, arrived, rows):
    def body(place_ref, b0, b1, pooled_ref, in_ref, rows_ref, mine, theirs):
        low_core = place_ref[3] == 0
        g = by_sample(b0, b1)
        products = grad_pooled_of(g, rows_ref)
        ext = jnp.concatenate([b0[2 * RANK :, :], b1[2 * RANK :, :]], axis=1)

        def writer(ref):
            def write(targets, at, value):
                ref[targets, at, :] = value.astype(ref.dtype)

            return write

        outs = [writer(mine), writer(theirs)]
        for out, part in zip(outs, by_core(low_core, pooled_ref[:, :LATE], 32)):
            for j in range(4):
                put_weights(out, 2 * ROWS, j, dot(part, g[:, j * 256 : (j + 1) * 256], 1, 0))
            put_sums(out, 384, dot(ext, part, 1, 1))
        for y, grad_pooled in enumerate(products):
            counts = in_ref[y * 512 : (y + 1) * 512, :LATE]
            for out, part in zip(outs, by_core(low_core, counts, ROWS)):
                put_slab(out, y, dot(part, grad_pooled, 1, 0))

    return call(
        body,
        [pltpu.VMEM((NY * NX, PACK, 128), F32), pltpu.VMEM((NY * NX, PACK, 128), BF16)],
        (place, *(near(v) for v in (block0, block1, pooled, arrived, rows))),
        [IN_SMEM] + [IN_VMEM] * 5,
        cost=pl.CostEstimate(flops=2 << 30, bytes_accessed=6 << 20, transcendentals=0),
    )


def late_products(block2, block3, rows):
    def body(b2, b3, rows_ref, g_out, out):
        g = by_sample(b2, b3)
        g_out[...] = g
        for y, grad_pooled in enumerate(grad_pooled_of(g, rows_ref)):
            out[:, y * EMBED : (y + 1) * EMBED] = grad_pooled

    return call(
        body,
        [pltpu.VMEM((SAMPLES - LATE, 2 * RANK + EXT), BF16), pltpu.VMEM((SAMPLES - LATE, COLS), BF16)],
        tuple(near(v) for v in (block2, block3, rows)),
        cost=pl.CostEstimate(flops=1 << 30, bytes_accessed=4 << 20, transcendentals=0),
    )


def late_weights(g, blocks, partner_blocks, values, partner_values, first, partner_first):
    def body(g_ref, b2, b3, p2, p3, own_ref, partner_ref, first_ref, other_ref, out):
        half = COLS // NC
        pooled = jnp.concatenate([own_ref[:half, :], partner_ref[:half, :]], axis=1)
        both = jnp.concatenate([g_ref[...], by_sample(p2, p3)], axis=0)

        def write(targets, at, value):
            shifted = slice(at.start + 2 * ROWS, at.stop + 2 * ROWS)
            held = first_ref[targets, shifted, :] + other_ref[targets, shifted, :].astype(F32)
            out[targets, at, :] = (held + value).astype(BF16)

        for j in range(4):
            put_weights(write, 0, j, dot(pooled, both[:, j * 256 : (j + 1) * 256], 1, 0))
        ext = jnp.concatenate([b[2 * RANK :, :] for b in (b2, b3, p2, p3)], axis=1)
        put_sums(write, 256, dot(ext, pooled, 1, 1))

    return call(
        body,
        [pltpu.VMEM((NY * NX, PACK - 2 * ROWS, 128), BF16)],
        tuple(near(v) for v in (g, *blocks, *partner_blocks, values, partner_values, first, partner_first)),
        cost=pl.CostEstimate(flops=1 << 30, bytes_accessed=4 << 20, transcendentals=0),
    )[0]


def late_slab(products, partner_products, values, partner_values, first, partner_first, weights):
    def body(own_products, their_products, own_ref, partner_ref, first_ref, other_ref, weights_ref, out):
        half = COLS // NC
        out[:, 2 * ROWS :, :] = weights_ref[...]

        def write(targets, at, value):
            held = first_ref[targets, at, :] + other_ref[targets, at, :].astype(F32)
            out[targets, at, :] = (held + value).astype(BF16)

        for y in range(NY):
            rows = slice(half + y * 256, half + (y + 1) * 256)
            table = slice(y * EMBED, (y + 1) * EMBED)
            counts = jnp.concatenate([own_ref[rows, :], partner_ref[rows, :]], axis=1)
            both = jnp.concatenate([own_products[:, table], their_products[:, table]], axis=0)
            put_slab(write, y, dot(counts, both, 1, 0))

    return call(
        body,
        [pltpu.VMEM((NY * NX, PACK, 128), BF16)],
        tuple(
            near(v)
            for v in (products, partner_products, values, partner_values, first, partner_first, weights)
        ),
        cost=pl.CostEstimate(flops=1 << 29, bytes_accessed=4 << 20, transcendentals=0),
    )[0]


def finish(shares, own, up_own):
    def body(in_ref, own_ref, up_ref, slab_out, down_out, up_out, bias_out, out_out):
        def total(at):
            held = in_ref[0, at, :].astype(F32)
            for i in range(1, NY * NX):
                held = held + in_ref[i, at, :].astype(F32)
            return held

        slab_out[:, :128] = total(slice(0, ROWS))
        slab_out[:, 128:] = total(slice(ROWS, 2 * ROWS))
        both = [total(slice(128 + j * 32, 160 + j * 32)) for j in range(8)]
        for j in range(4):
            down_out[:, j * 128 : (j + 1) * 128] = both[j].astype(BF16)
        product = jnp.concatenate(both[4:], axis=1)
        w_own, bias_own = own_ref[:, 0:1], own_ref[:, 1:2]
        up_out[...] = (product * w_own).astype(BF16)
        lane = lax.broadcasted_iota(jnp.int32, (32, 128), 1)
        row = lax.broadcasted_iota(jnp.int32, (32, 128), 0)
        last = total(slice(384, 400))
        own = lane.astype(F32) == own_ref[:, 2:3]
        sums = jnp.sum(jnp.where(own, last[0:1] + last[1:2], 0.0), axis=1, keepdims=True)
        out = (1.0 + bias_own) * sums + jnp.sum(product * up_ref[...], axis=1, keepdims=True)
        bias_out[...] = jnp.sum(jnp.where(lane == row, w_own * sums, 0.0), axis=0, keepdims=True)[:, :32]
        out_out[...] = jnp.sum(jnp.where(lane == row, out, 0.0), axis=0, keepdims=True)[:, :32]

    return call(
        body,
        [
            jax.ShapeDtypeStruct((ROWS, EMBED), F32),
            jax.ShapeDtypeStruct((32, RANK), BF16),
            jax.ShapeDtypeStruct((32, RANK), BF16),
            jax.ShapeDtypeStruct((1, 32), F32),
            jax.ShapeDtypeStruct((1, 32), F32),
        ],
        (near(shares), near(own), near(up_own)),
    )


def local(slab, counts, cross_down, cross_up, cross_bias, out_weight, labels):
    place = jnp.stack([lax.axis_index(a) for a in ALL]).astype(jnp.int32)
    w_row, bias_row = out_weight.reshape(1, -1), cross_bias.reshape(1, -1)
    rows = prepare(place, cross_down, cross_up, w_row, bias_row)
    own, up_own = prepare_own(place, cross_up, w_row, bias_row)
    sent = pack_counts(place, counts.T, slab)
    arrived = lax.all_to_all(sent, PLANE, 0, 0, tiled=True).reshape(PEERS * ROWS, SAMPLES + HALF)
    other = shift(arrived[:, SAMPLES:], dc=1)
    half = pool_half(arrived)
    pooled, chunk1 = forward_far(place, arrived, other, half, rows)
    part1 = shift(chunk1, dz=(ORDER[0][1], ORDER[1][1]))
    chunk2, chunk3 = forward_near(pooled, rows)
    part2 = shift(chunk2, dz=(ORDER[0][2], ORDER[1][2]))
    part3 = shift(chunk3, dz=(ORDER[0][3], ORDER[1][3]))
    parts = [part1, part2, part3]
    chunk = forward_own(pooled, rows)
    values, theirs = late_values(place, pooled, arrived)
    partner_values = shift(theirs, dc=1)
    block0 = own_samples([chunk] + parts, labels.reshape(1, OWN))
    blocks = []
    for i in range(1, NZ):
        blocks.append(shift(block0, dz=(-ORDER[0][i], -ORDER[1][i])))
    block1, *late = blocks
    first, theirs = backward_first(place, block0, block1, pooled, arrived, rows)
    partner_first = shift(theirs, dc=1)
    partner_late = []
    for block in late:
        partner_late.append(shift(block, dc=1))
    g, products = late_products(*late, rows)
    partner_products = shift(products, dc=1)
    weights = late_weights(g, late, partner_late, values, partner_values, first, partner_first)
    summed = late_slab(products, partner_products, values, partner_values, first, partner_first, weights)
    shares = lax.all_to_all(summed, ("y", "x"), 0, 0, tiled=True)
    grad_slab, grad_down, grad_up, grad_bias, grad_out = finish(shares, own, up_own)
    return grad_slab, grad_down, grad_up.T, grad_bias.reshape(32), grad_out.reshape(32)


def solution(mesh):
    torus = Mesh(mesh.devices.reshape(NZ, NY, NX, NC), ALL)
    return jax.shard_map(
        local,
        mesh=torus,
        in_specs=(P(ALL, None), P(None, ALL), P(), P(), P(), P(), P(ALL)),
        out_specs=(P(ALL, None), P(ALL, None), P(None, ALL), P(ALL), P(ALL)),
        check_vma=False,
    )
```

```python
import jax
import jax.numpy as jnp
from jax import lax
from jax.experimental import pallas as pl
from jax.experimental.pallas import tpu as pltpu
from jax.sharding import Mesh
from jax.sharding import PartitionSpec as P


ALL = ("z", "y", "x", "c")
PLANE = ("y", "x", "c")
NZ, NY, NX, NC = 4, 4, 4, 2
NK = NX * NC
PEERS = NY * NK
OWN = 128
ROWS = 64
EMBED = 256
RANK = 512
COLS = 1024
SAMPLES = NZ * OWN
EXT = 16
PACK = 400
HALF = EMBED // 2
LATE = SAMPLES // 2
ORDER = ((0, 2, 1, 3), (0, 2, 3, 1))
PLACES = ((0, 2, 1, 3), (0, 3, 1, 2))
F32 = jnp.float32
BF16 = jnp.bfloat16


def dot(a, b, da, db):
    return lax.dot_general(a, b, (((da,), (db,)), ((), ())), preferred_element_type=F32)


def flat(z, y, x, c):
    return (((z % NZ) * NY + y % NY) * NX + x % NX) * NC + c % NC


def shift(value, dz=(0, 0), dc=0):
    pairs = [
        (flat(z, y, x, c), flat(z + dz[c], y, x, c + dc))
        for z in range(NZ)
        for y in range(NY)
        for x in range(NX)
        for c in range(NC)
    ]
    return lax.ppermute(value, ALL, pairs)


def near(value):
    return pltpu.with_memory_space_constraint(value, pltpu.VMEM)


def far(value):
    return pltpu.with_memory_space_constraint(value, pltpu.HBM)


def call(body, outs, args, specs=None, scratch=(), mib=24, cost=None):
    return pl.pallas_call(
        body,
        in_specs=specs or [pl.BlockSpec(memory_space=pltpu.VMEM)] * len(args),
        out_specs=[pl.BlockSpec(memory_space=pltpu.VMEM)] * len(outs),
        out_shape=outs,
        scratch_shapes=list(scratch),
        compiler_params=pltpu.CompilerParams(vmem_limit_bytes=mib << 20),
        cost_estimate=cost,
    )(*args)


IN_SMEM = pl.BlockSpec(memory_space=pltpu.SMEM)
IN_VMEM = pl.BlockSpec(memory_space=pltpu.VMEM)
IN_HBM = pl.BlockSpec(memory_space=pltpu.HBM)


def pack_counts(place, counts_t, slab):
    strip = NK * OWN

    def body(place_ref, counts_ref, slab_ref, out, held, slab_s, sems, slab_sem):
        def copy(y, n):
            z = lax.rem(place_ref[0] + n, NZ)
            start = pl.multiple_of(z * (NY * strip) + y * strip, strip)
            return pltpu.make_async_copy(counts_ref.at[:, pl.ds(start, strip)], held.at[y, n], sems.at[y, n])

        slab_copy = pltpu.make_async_copy(slab_ref, slab_s, slab_sem)
        slab_copy.start()
        for y in range(NY):
            for n in range(NZ):
                copy(y, n).start(priority=n % 2)
        slab_copy.wait()
        for k in range(PEERS):
            half = k % NC
            out[k, :, SAMPLES:] = slab_s[:, half * HALF : (half + 1) * HALF]
        for y in range(NY):
            for n in range(NZ):
                copy(y, n).wait()
                for k in range(NK):
                    to = PLACES[k % NC][n] * OWN
                    out[y * NK + k, :, to : to + OWN] = (
                        held[y, n, :, k * OWN : (k + 1) * OWN].astype(F32).astype(BF16)
                    )

    return call(
        body,
        [pltpu.VMEM((PEERS, ROWS, SAMPLES + HALF), BF16)],
        (place, far(counts_t), far(slab)),
        [IN_SMEM, IN_HBM, IN_HBM],
        [
            pltpu.VMEM((NY, NZ, ROWS, strip), jnp.int32),
            pltpu.VMEM((ROWS, EMBED), BF16),
            pltpu.SemaphoreType.DMA((NY, NZ)),
            pltpu.SemaphoreType.DMA,
        ],
    )[0]


def prepare(place, down, up, w, bias):
    def body(place_ref, down_ref, up_ref, w_ref, bias_ref, rows_out):
        here = pl.ds(pl.multiple_of(place_ref[0] * COLS, COLS), COLS)
        w = w_ref[:, here]
        for part in range(4):
            at = slice(part * 128, (part + 1) * 128)
            rows_out[at, :] = down_ref[here, at].T
        rows_out[RANK : 2 * RANK, :] = (up_ref[:, here].astype(F32) * w).astype(BF16)
        v = w * (1.0 + bias_ref[:, here])
        high = v.astype(BF16).astype(F32)
        at = lax.broadcasted_iota(jnp.int32, (EXT, COLS), 0)
        rows_out[2 * RANK :, :] = jnp.where(at < 2, high, jnp.where(at == 2, v - high, 0.0)).astype(BF16)

    return call(
        body,
        [pltpu.VMEM((2 * RANK + EXT, COLS), BF16)],
        (place, *(near(v) for v in (down, up, w, bias))),
        [IN_SMEM] + [IN_VMEM] * 4,
        cost=pl.CostEstimate(flops=1 << 29, bytes_accessed=6 << 20, transcendentals=0),
    )[0]


def prepare_own(place, up, w, bias):
    def body(place_ref, up_ref, w_ref, bias_ref, own_out, up_out):
        k = place_ref[2] * NC + place_ref[3]
        start = place_ref[0] * COLS + (place_ref[1] * 2 + lax.div(k, 4)) * 128
        strip = pl.ds(pl.multiple_of(start, 128), 128)
        offset = lax.rem(k, 4) * 32
        lane = lax.broadcasted_iota(jnp.int32, (32, 128), 1)
        row = lax.broadcasted_iota(jnp.int32, (32, 128), 0)
        own = lane == row + offset
        w_own = jnp.sum(jnp.where(own, w_ref[:, strip], 0.0), axis=1, keepdims=True)
        bias_own = jnp.sum(jnp.where(own, bias_ref[:, strip], 0.0), axis=1, keepdims=True)
        place_own = (row + place_ref[2] * 32).astype(F32)
        own_out[...] = jnp.where(lane == 0, w_own, jnp.where(lane == 1, bias_own, place_own))
        up_out[...] = dot(jnp.where(own, 1.0, 0.0).astype(BF16), up_ref[:, strip], 1, 1)

    return call(
        body,
        [pltpu.VMEM((32, 128), F32), pltpu.VMEM((32, RANK), F32)],
        (place, *(near(v) for v in (up, w, bias))),
        [IN_SMEM] + [IN_VMEM] * 3,
        cost=pl.CostEstimate(flops=1 << 27, bytes_accessed=1 << 20, transcendentals=0),
    )


def pool_half(arrived):
    def body(in_ref, pooled_ref):
        for y in range(NY):
            at = slice(y * 512, (y + 1) * 512)
            half = slice(y * HALF, (y + 1) * HALF)
            pooled_ref[half, :] = dot(in_ref[at, SAMPLES:].T, in_ref[at, :SAMPLES], 1, 0).astype(BF16)

    return call(
        body,
        [pltpu.VMEM((NY * HALF, SAMPLES), BF16)],
        (near(arrived),),
        cost=pl.CostEstimate(flops=1 << 29, bytes_accessed=2 << 20, transcendentals=0),
    )[0]


def head_of(rows_ref, pooled):
    head = dot(rows_ref[2 * RANK :, :], pooled, 1, 0)
    sums = head[0:1] + head[2:3]
    high = sums.astype(BF16).astype(F32)
    at = lax.broadcasted_iota(jnp.int32, (EXT, pooled.shape[1]), 0)
    return jnp.where(at == 0, high, jnp.where(at == 1, sums - high, 0.0)).astype(BF16)


def products(rows_ref, pooled, outs):
    for part in range(4):
        at = slice(part * 256, (part + 1) * 256)
        product = dot(rows_ref[at, :], pooled, 1, 0).astype(BF16)
        for i, out in enumerate(outs):
            out[at, :] = product[:, i * OWN : (i + 1) * OWN]
    ext = head_of(rows_ref, pooled)
    for i, out in enumerate(outs):
        out[2 * RANK :, :] = ext[:, i * OWN : (i + 1) * OWN]


def forward_far(place, arrived, other, half, rows):
    def body(place_ref, in_ref, other_ref, half_ref, rows_ref, pooled_ref, out):
        core = place_ref[3]
        for y in range(NY):
            at = slice(y * 512, (y + 1) * 512)
            mine = pl.multiple_of(y * EMBED + core * HALF, HALF)
            partners = pl.multiple_of(y * EMBED + (1 - core) * HALF, HALF)
            pooled_ref[pl.ds(mine, HALF), :] = half_ref[y * HALF : (y + 1) * HALF, :]
            pooled_ref[pl.ds(partners, HALF), :] = dot(
                other_ref[at, :].T, in_ref[at, :SAMPLES], 1, 0
            ).astype(BF16)
        products(rows_ref, pooled_ref[:, 2 * OWN : 3 * OWN], (out,))

    return call(
        body,
        [pltpu.VMEM((COLS, SAMPLES), BF16), pltpu.VMEM((2 * RANK + EXT, OWN), BF16)],
        (place, near(arrived), near(other), near(half), near(rows)),
        [IN_SMEM] + [IN_VMEM] * 4,
        cost=pl.CostEstimate(flops=3 << 30, bytes_accessed=4 << 20, transcendentals=0),
    )


def forward_near(pooled, rows):
    def body(pooled_ref, rows_ref, *outs):
        ends = [pooled_ref[:, OWN : 2 * OWN], pooled_ref[:, 3 * OWN :]]
        products(rows_ref, jnp.concatenate(ends, axis=1), outs)

    return call(
        body,
        [pltpu.VMEM((2 * RANK + EXT, OWN), BF16)] * 2,
        (near(pooled), near(rows)),
        cost=pl.CostEstimate(flops=1 << 30, bytes_accessed=2 << 20, transcendentals=0),
    )


def forward_own(pooled, rows):
    def body(pooled_ref, rows_ref, out):
        products(rows_ref, pooled_ref[:, :OWN], (out,))

    return call(
        body,
        [pltpu.VMEM((2 * RANK + EXT, OWN), BF16)],
        (near(pooled), near(rows)),
        cost=pl.CostEstimate(flops=1 << 30, bytes_accessed=1 << 20, transcendentals=0),
    )[0]


def own_samples(parts, labels):
    def body(p0, p1, p2, p3, labels_ref, out):
        def total(rows):
            a, b, c, d = (p[rows, :].astype(F32) for p in (p0, p1, p2, p3))
            return (a + b) + (c + d)

        squeezed = total(slice(0, RANK)).astype(BF16).astype(F32)
        other = total(slice(RANK, 2 * RANK))
        ext = total(slice(2 * RANK, 2 * RANK + EXT))
        logits = ext[0:1] + ext[1:2] + jnp.sum(squeezed * other, axis=0, keepdims=True)
        g = jax.nn.sigmoid(logits) - labels_ref[...].astype(F32)
        out[0:RANK, :] = (g * other).astype(BF16)
        out[RANK : 2 * RANK, :] = (g * squeezed).astype(BF16)
        high = g.astype(BF16).astype(F32)
        at = lax.broadcasted_iota(jnp.int32, (EXT, OWN), 0)
        rows = jnp.where((at == 0) | (at == 2), high, jnp.where(at == 1, g - high, 0.0))
        out[2 * RANK :, :] = rows.astype(BF16)

    return call(body, [pltpu.VMEM((2 * RANK + EXT, OWN), BF16)], (*(near(p) for p in parts), labels))[0]


def by_sample(*blocks):
    return jnp.concatenate([b[...].T for b in blocks], axis=0)


def grad_pooled_of(g, rows_ref):
    tables = [slice(y * EMBED, (y + 1) * EMBED) for y in range(NY)]
    return [dot(g, rows_ref[:, table], 1, 0).astype(BF16) for table in tables]


def by_core(low_core, value, width):
    pairs = value.reshape(-1, NC, width, value.shape[1])
    even, odd = (pairs[:, c].reshape(-1, value.shape[1]) for c in range(NC))
    return jnp.where(low_core, even, odd), jnp.where(low_core, odd, even)


def late_values(place, pooled, arrived):
    def body(place_ref, pooled_ref, in_ref, mine, theirs):
        low_core = place_ref[3] == 0
        half = COLS // NC
        mine[:half, :], theirs[:half, :] = by_core(low_core, pooled_ref[:, LATE:], 32)
        for y in range(NY):
            rows = slice(half + y * 256, half + (y + 1) * 256)
            counts = in_ref[y * 512 : (y + 1) * 512, LATE:SAMPLES]
            mine[rows, :], theirs[rows, :] = by_core(low_core, counts, ROWS)

    return call(
        body,
        [pltpu.VMEM((COLS // NC + NY * 256, SAMPLES - LATE), BF16)] * 2,
        (place, near(pooled), near(arrived)),
        [IN_SMEM] + [IN_VMEM] * 2,
        cost=pl.CostEstimate(flops=1 << 27, bytes_accessed=2 << 20, transcendentals=0),
    )


def put_weights(out, first, j, value):
    for h in range(2):
        at = first + (2 * j + h) * 32
        held = value[:, h * 128 : (h + 1) * 128].reshape(NY * NX, 32, 128)
        out(slice(0, NY * NX), slice(at, at + 32), held)


def put_sums(out, first, value):
    for y in range(NY):
        row = value[:, y * 128 : (y + 1) * 128]
        for x in range(NX):
            out(y * NX + x, slice(first, first + EXT), row)


def put_slab(out, y, value):
    for h in range(2):
        held = value[:, h * 128 : (h + 1) * 128].reshape(NX, ROWS, 128)
        out(slice(y * NX, (y + 1) * NX), slice(h * ROWS, (h + 1) * ROWS), held)


def backward_first(place, block0, block1, pooled, arrived, rows):
    def body(place_ref, b0, b1, pooled_ref, in_ref, rows_ref, mine, theirs):
        low_core = place_ref[3] == 0
        g = by_sample(b0, b1)
        products = grad_pooled_of(g, rows_ref)
        ext = jnp.concatenate([b0[2 * RANK :, :], b1[2 * RANK :, :]], axis=1)

        def writer(ref):
            def write(targets, at, value):
                ref[targets, at, :] = value.astype(ref.dtype)

            return write

        outs = [writer(mine), writer(theirs)]
        for out, part in zip(outs, by_core(low_core, pooled_ref[:, :LATE], 32)):
            for j in range(4):
                put_weights(out, 2 * ROWS, j, dot(part, g[:, j * 256 : (j + 1) * 256], 1, 0))
            put_sums(out, 384, dot(ext, part, 1, 1))
        for y, grad_pooled in enumerate(products):
            counts = in_ref[y * 512 : (y + 1) * 512, :LATE]
            for out, part in zip(outs, by_core(low_core, counts, ROWS)):
                put_slab(out, y, dot(part, grad_pooled, 1, 0))

    return call(
        body,
        [pltpu.VMEM((NY * NX, PACK, 128), F32), pltpu.VMEM((NY * NX, PACK, 128), BF16)],
        (place, *(near(v) for v in (block0, block1, pooled, arrived, rows))),
        [IN_SMEM] + [IN_VMEM] * 5,
        cost=pl.CostEstimate(flops=2 << 30, bytes_accessed=6 << 20, transcendentals=0),
    )


def late_products(block2, block3, rows):
    def body(b2, b3, rows_ref, g_out, out):
        g = by_sample(b2, b3)
        g_out[...] = g
        for y, grad_pooled in enumerate(grad_pooled_of(g, rows_ref)):
            out[:, y * EMBED : (y + 1) * EMBED] = grad_pooled

    return call(
        body,
        [pltpu.VMEM((SAMPLES - LATE, 2 * RANK + EXT), BF16), pltpu.VMEM((SAMPLES - LATE, COLS), BF16)],
        tuple(near(v) for v in (block2, block3, rows)),
        cost=pl.CostEstimate(flops=1 << 30, bytes_accessed=4 << 20, transcendentals=0),
    )


def late_weights(g, blocks, partner_blocks, values, partner_values, first, partner_first):
    def body(g_ref, b2, b3, p2, p3, own_ref, partner_ref, first_ref, other_ref, out):
        half = COLS // NC
        pooled = jnp.concatenate([own_ref[:half, :], partner_ref[:half, :]], axis=1)
        both = jnp.concatenate([g_ref[...], by_sample(p2, p3)], axis=0)

        def write(targets, at, value):
            shifted = slice(at.start + 2 * ROWS, at.stop + 2 * ROWS)
            held = first_ref[targets, shifted, :] + other_ref[targets, shifted, :].astype(F32)
            out[targets, at, :] = (held + value).astype(BF16)

        for j in range(4):
            put_weights(write, 0, j, dot(pooled, both[:, j * 256 : (j + 1) * 256], 1, 0))
        ext = jnp.concatenate([b[2 * RANK :, :] for b in (b2, b3, p2, p3)], axis=1)
        put_sums(write, 256, dot(ext, pooled, 1, 1))

    return call(
        body,
        [pltpu.VMEM((NY * NX, PACK - 2 * ROWS, 128), BF16)],
        tuple(near(v) for v in (g, *blocks, *partner_blocks, values, partner_values, first, partner_first)),
        cost=pl.CostEstimate(flops=1 << 30, bytes_accessed=4 << 20, transcendentals=0),
    )[0]


def late_slab(products, partner_products, values, partner_values, first, partner_first, weights):
    def body(own_products, their_products, own_ref, partner_ref, first_ref, other_ref, weights_ref, out):
        half = COLS // NC
        out[:, 2 * ROWS :, :] = weights_ref[...]

        def write(targets, at, value):
            held = first_ref[targets, at, :] + other_ref[targets, at, :].astype(F32)
            out[targets, at, :] = (held + value).astype(BF16)

        for y in range(NY):
            rows = slice(half + y * 256, half + (y + 1) * 256)
            table = slice(y * EMBED, (y + 1) * EMBED)
            counts = jnp.concatenate([own_ref[rows, :], partner_ref[rows, :]], axis=1)
            both = jnp.concatenate([own_products[:, table], their_products[:, table]], axis=0)
            put_slab(write, y, dot(counts, both, 1, 0))

    return call(
        body,
        [pltpu.VMEM((NY * NX, PACK, 128), BF16)],
        tuple(
            near(v)
            for v in (products, partner_products, values, partner_values, first, partner_first, weights)
        ),
        cost=pl.CostEstimate(flops=1 << 29, bytes_accessed=4 << 20, transcendentals=0),
    )[0]


def finish(shares, own, up_own):
    def body(in_ref, own_ref, up_ref, slab_out, down_out, up_out, bias_out, out_out):
        def total(at):
            held = in_ref[0, at, :].astype(F32)
            for i in range(1, NY * NX):
                held = held + in_ref[i, at, :].astype(F32)
            return held

        slab_out[:, :128] = total(slice(0, ROWS))
        slab_out[:, 128:] = total(slice(ROWS, 2 * ROWS))
        both = [total(slice(128 + j * 32, 160 + j * 32)) for j in range(8)]
        for j in range(4):
            down_out[:, j * 128 : (j + 1) * 128] = both[j].astype(BF16)
        product = jnp.concatenate(both[4:], axis=1)
        w_own, bias_own = own_ref[:, 0:1], own_ref[:, 1:2]
        up_out[...] = (product * w_own).astype(BF16)
        lane = lax.broadcasted_iota(jnp.int32, (32, 128), 1)
        row = lax.broadcasted_iota(jnp.int32, (32, 128), 0)
        last = total(slice(384, 400))
        own = lane.astype(F32) == own_ref[:, 2:3]
        sums = jnp.sum(jnp.where(own, last[0:1] + last[1:2], 0.0), axis=1, keepdims=True)
        out = (1.0 + bias_own) * sums + jnp.sum(product * up_ref[...], axis=1, keepdims=True)
        bias_out[...] = jnp.sum(jnp.where(lane == row, w_own * sums, 0.0), axis=0, keepdims=True)[:, :32]
        out_out[...] = jnp.sum(jnp.where(lane == row, out, 0.0), axis=0, keepdims=True)[:, :32]

    return call(
        body,
        [
            jax.ShapeDtypeStruct((ROWS, EMBED), F32),
            jax.ShapeDtypeStruct((32, RANK), BF16),
            jax.ShapeDtypeStruct((32, RANK), BF16),
            jax.ShapeDtypeStruct((1, 32), F32),
            jax.ShapeDtypeStruct((1, 32), F32),
        ],
        (near(shares), near(own), near(up_own)),
    )


def local(slab, counts, cross_down, cross_up, cross_bias, out_weight, labels):
    place = jnp.stack([lax.axis_index(a) for a in ALL]).astype(jnp.int32)
    w_row, bias_row = out_weight.reshape(1, -1), cross_bias.reshape(1, -1)
    rows = prepare(place, cross_down, cross_up, w_row, bias_row)
    own, up_own = prepare_own(place, cross_up, w_row, bias_row)
    sent = pack_counts(place, counts.T, slab)
    arrived = lax.all_to_all(sent, PLANE, 0, 0, tiled=True).reshape(PEERS * ROWS, SAMPLES + HALF)
    other = shift(arrived[:, SAMPLES:], dc=1)
    half = pool_half(arrived)
    pooled, chunk2 = forward_far(place, arrived, other, half, rows)
    part2 = shift(chunk2, dz=(ORDER[0][2], ORDER[1][2]))
    chunk1, chunk3 = forward_near(pooled, rows)
    part1 = shift(chunk1, dz=(ORDER[0][1], ORDER[1][1]))
    part3 = shift(chunk3, dz=(ORDER[0][3], ORDER[1][3]))
    parts = [part1, part2, part3]
    chunk = forward_own(pooled, rows)
    values, theirs = late_values(place, pooled, arrived)
    partner_values = shift(theirs, dc=1)
    block0 = own_samples([chunk] + parts, labels.reshape(1, OWN))
    blocks = []
    for i in range(1, NZ):
        blocks.append(shift(block0, dz=(-ORDER[0][i], -ORDER[1][i])))
    block1, *late = blocks
    first, theirs = backward_first(place, block0, block1, pooled, arrived, rows)
    partner_first = shift(theirs, dc=1)
    partner_late = []
    for block in late:
        partner_late.append(shift(block, dc=1))
    g, products = late_products(*late, rows)
    partner_products = shift(products, dc=1)
    weights = late_weights(g, late, partner_late, values, partner_values, first, partner_first)
    summed = late_slab(products, partner_products, values, partner_values, first, partner_first, weights)
    shares = lax.all_to_all(summed, ("y", "x"), 0, 0, tiled=True)
    grad_slab, grad_down, grad_up, grad_bias, grad_out = finish(shares, own, up_own)
    return grad_slab, grad_down, grad_up.T, grad_bias.reshape(32), grad_out.reshape(32)


def solution(mesh):
    torus = Mesh(mesh.devices.reshape(NZ, NY, NX, NC), ALL)
    return jax.shard_map(
        local,
        mesh=torus,
        in_specs=(P(ALL, None), P(None, ALL), P(), P(), P(), P(), P(ALL)),
        out_specs=(P(ALL, None), P(ALL, None), P(None, ALL), P(ALL), P(ALL)),
        check_vma=False,
    )
```

```python
import jax
import jax.numpy as jnp
from jax import lax
from jax.experimental import pallas as pl
from jax.experimental.pallas import tpu as pltpu
from jax.sharding import Mesh
from jax.sharding import PartitionSpec as P


ALL = ("z", "y", "x", "c")
PLANE = ("y", "x", "c")
NZ, NY, NX, NC = 4, 4, 4, 2
NK = NX * NC
PEERS = NY * NK
OWN = 128
ROWS = 64
EMBED = 256
RANK = 512
COLS = 1024
SAMPLES = NZ * OWN
EXT = 16
PACK = 400
HALF = EMBED // 2
LATE = SAMPLES // 2
ORDER = ((0, 2, 1, 3), (0, 2, 3, 1))
PLACES = ((0, 2, 1, 3), (0, 3, 1, 2))
F32 = jnp.float32
BF16 = jnp.bfloat16


def dot(a, b, da, db):
    return lax.dot_general(a, b, (((da,), (db,)), ((), ())), preferred_element_type=F32)


def flat(z, y, x, c):
    return (((z % NZ) * NY + y % NY) * NX + x % NX) * NC + c % NC


def shift(value, dz=(0, 0), dc=0):
    pairs = [
        (flat(z, y, x, c), flat(z + dz[c], y, x, c + dc))
        for z in range(NZ)
        for y in range(NY)
        for x in range(NX)
        for c in range(NC)
    ]
    return lax.ppermute(value, ALL, pairs)


def near(value):
    return pltpu.with_memory_space_constraint(value, pltpu.VMEM)


def far(value):
    return pltpu.with_memory_space_constraint(value, pltpu.HBM)


def call(body, outs, args, specs=None, scratch=(), mib=24, cost=None):
    return pl.pallas_call(
        body,
        in_specs=specs or [pl.BlockSpec(memory_space=pltpu.VMEM)] * len(args),
        out_specs=[pl.BlockSpec(memory_space=pltpu.VMEM)] * len(outs),
        out_shape=outs,
        scratch_shapes=list(scratch),
        compiler_params=pltpu.CompilerParams(vmem_limit_bytes=mib << 20),
        cost_estimate=cost,
    )(*args)


IN_SMEM = pl.BlockSpec(memory_space=pltpu.SMEM)
IN_VMEM = pl.BlockSpec(memory_space=pltpu.VMEM)
IN_HBM = pl.BlockSpec(memory_space=pltpu.HBM)


def pack_counts(place, counts_t, slab):
    strip = NK * OWN

    def body(place_ref, counts_ref, slab_ref, out, held, slab_s, sems, slab_sem):
        def copy(y, n):
            z = lax.rem(place_ref[0] + n, NZ)
            start = pl.multiple_of(z * (NY * strip) + y * strip, strip)
            return pltpu.make_async_copy(counts_ref.at[:, pl.ds(start, strip)], held.at[y, n], sems.at[y, n])

        slab_copy = pltpu.make_async_copy(slab_ref, slab_s, slab_sem)
        slab_copy.start()
        for y in range(NY):
            for n in range(NZ):
                copy(y, n).start(priority=n % 2)
        slab_copy.wait()
        for k in range(PEERS):
            half = k % NC
            out[k, :, SAMPLES:] = slab_s[:, half * HALF : (half + 1) * HALF]
        for y in range(NY):
            for n in range(NZ):
                copy(y, n).wait()
                for k in range(NK):
                    to = PLACES[k % NC][n] * OWN
                    out[y * NK + k, :, to : to + OWN] = (
                        held[y, n, :, k * OWN : (k + 1) * OWN].astype(F32).astype(BF16)
                    )

    return call(
        body,
        [pltpu.VMEM((PEERS, ROWS, SAMPLES + HALF), BF16)],
        (place, far(counts_t), far(slab)),
        [IN_SMEM, IN_HBM, IN_HBM],
        [
            pltpu.VMEM((NY, NZ, ROWS, strip), jnp.int32),
            pltpu.VMEM((ROWS, EMBED), BF16),
            pltpu.SemaphoreType.DMA((NY, NZ)),
            pltpu.SemaphoreType.DMA,
        ],
    )[0]


def prepare(place, down, up, w, bias):
    def body(place_ref, down_ref, up_ref, w_ref, bias_ref, rows_out):
        here = pl.ds(pl.multiple_of(place_ref[0] * COLS, COLS), COLS)
        w = w_ref[:, here]
        for part in range(4):
            at = slice(part * 128, (part + 1) * 128)
            rows_out[at, :] = down_ref[here, at].T
        rows_out[RANK : 2 * RANK, :] = (up_ref[:, here].astype(F32) * w).astype(BF16)
        v = w * (1.0 + bias_ref[:, here])
        high = v.astype(BF16).astype(F32)
        at = lax.broadcasted_iota(jnp.int32, (EXT, COLS), 0)
        rows_out[2 * RANK :, :] = jnp.where(at < 2, high, jnp.where(at == 2, v - high, 0.0)).astype(BF16)

    return call(
        body,
        [pltpu.VMEM((2 * RANK + EXT, COLS), BF16)],
        (place, *(near(v) for v in (down, up, w, bias))),
        [IN_SMEM] + [IN_VMEM] * 4,
        cost=pl.CostEstimate(flops=1 << 29, bytes_accessed=6 << 20, transcendentals=0),
    )[0]


def prepare_own(place, up, w, bias):
    def body(place_ref, up_ref, w_ref, bias_ref, own_out, up_out):
        k = place_ref[2] * NC + place_ref[3]
        start = place_ref[0] * COLS + (place_ref[1] * 2 + lax.div(k, 4)) * 128
        strip = pl.ds(pl.multiple_of(start, 128), 128)
        offset = lax.rem(k, 4) * 32
        lane = lax.broadcasted_iota(jnp.int32, (32, 128), 1)
        row = lax.broadcasted_iota(jnp.int32, (32, 128), 0)
        own = lane == row + offset
        w_own = jnp.sum(jnp.where(own, w_ref[:, strip], 0.0), axis=1, keepdims=True)
        bias_own = jnp.sum(jnp.where(own, bias_ref[:, strip], 0.0), axis=1, keepdims=True)
        place_own = (row + place_ref[2] * 32).astype(F32)
        own_out[...] = jnp.where(lane == 0, w_own, jnp.where(lane == 1, bias_own, place_own))
        up_out[...] = dot(jnp.where(own, 1.0, 0.0).astype(BF16), up_ref[:, strip], 1, 1)

    return call(
        body,
        [pltpu.VMEM((32, 128), F32), pltpu.VMEM((32, RANK), F32)],
        (place, *(near(v) for v in (up, w, bias))),
        [IN_SMEM] + [IN_VMEM] * 3,
        cost=pl.CostEstimate(flops=1 << 27, bytes_accessed=1 << 20, transcendentals=0),
    )


def pool_half(arrived):
    def body(in_ref, pooled_ref):
        for y in range(NY):
            at = slice(y * 512, (y + 1) * 512)
            half = slice(y * HALF, (y + 1) * HALF)
            pooled_ref[half, :] = dot(in_ref[at, SAMPLES:].T, in_ref[at, :SAMPLES], 1, 0).astype(BF16)

    return call(
        body,
        [pltpu.VMEM((NY * HALF, SAMPLES), BF16)],
        (near(arrived),),
        cost=pl.CostEstimate(flops=1 << 29, bytes_accessed=2 << 20, transcendentals=0),
    )[0]


def head_of(rows_ref, pooled):
    head = dot(rows_ref[2 * RANK :, :], pooled, 1, 0)
    sums = head[0:1] + head[2:3]
    high = sums.astype(BF16).astype(F32)
    at = lax.broadcasted_iota(jnp.int32, (EXT, pooled.shape[1]), 0)
    return jnp.where(at == 0, high, jnp.where(at == 1, sums - high, 0.0)).astype(BF16)


def products(rows_ref, pooled, outs):
    for part in range(4):
        at = slice(part * 256, (part + 1) * 256)
        product = dot(rows_ref[at, :], pooled, 1, 0).astype(BF16)
        for i, out in enumerate(outs):
            out[at, :] = product[:, i * OWN : (i + 1) * OWN]
    ext = head_of(rows_ref, pooled)
    for i, out in enumerate(outs):
        out[2 * RANK :, :] = ext[:, i * OWN : (i + 1) * OWN]


def forward_far(place, arrived, other, half, rows):
    def body(place_ref, in_ref, other_ref, half_ref, rows_ref, pooled_ref, *outs):
        core = place_ref[3]
        for y in range(NY):
            at = slice(y * 512, (y + 1) * 512)
            mine = pl.multiple_of(y * EMBED + core * HALF, HALF)
            partners = pl.multiple_of(y * EMBED + (1 - core) * HALF, HALF)
            pooled_ref[pl.ds(mine, HALF), :] = half_ref[y * HALF : (y + 1) * HALF, :]
            pooled_ref[pl.ds(partners, HALF), :] = dot(
                other_ref[at, :].T, in_ref[at, :SAMPLES], 1, 0
            ).astype(BF16)
        products(rows_ref, pooled_ref[:, OWN : 3 * OWN], outs)

    return call(
        body,
        [pltpu.VMEM((COLS, SAMPLES), BF16)] + [pltpu.VMEM((2 * RANK + EXT, OWN), BF16)] * 2,
        (place, near(arrived), near(other), near(half), near(rows)),
        [IN_SMEM] + [IN_VMEM] * 4,
        cost=pl.CostEstimate(flops=3 << 30, bytes_accessed=4 << 20, transcendentals=0),
    )


def forward_near(pooled, rows):
    def body(pooled_ref, rows_ref, out):
        products(rows_ref, pooled_ref[:, 3 * OWN :], (out,))

    return call(
        body,
        [pltpu.VMEM((2 * RANK + EXT, OWN), BF16)],
        (near(pooled), near(rows)),
        cost=pl.CostEstimate(flops=1 << 30, bytes_accessed=2 << 20, transcendentals=0),
    )[0]


def forward_own(pooled, rows):
    def body(pooled_ref, rows_ref, out):
        products(rows_ref, pooled_ref[:, :OWN], (out,))

    return call(
        body,
        [pltpu.VMEM((2 * RANK + EXT, OWN), BF16)],
        (near(pooled), near(rows)),
        cost=pl.CostEstimate(flops=1 << 30, bytes_accessed=1 << 20, transcendentals=0),
    )[0]


def own_samples(parts, labels):
    def body(p0, p1, p2, p3, labels_ref, out):
        def total(rows):
            a, b, c, d = (p[rows, :].astype(F32) for p in (p0, p1, p2, p3))
            return (a + b) + (c + d)

        squeezed = total(slice(0, RANK)).astype(BF16).astype(F32)
        other = total(slice(RANK, 2 * RANK))
        ext = total(slice(2 * RANK, 2 * RANK + EXT))
        logits = ext[0:1] + ext[1:2] + jnp.sum(squeezed * other, axis=0, keepdims=True)
        g = jax.nn.sigmoid(logits) - labels_ref[...].astype(F32)
        out[0:RANK, :] = (g * other).astype(BF16)
        out[RANK : 2 * RANK, :] = (g * squeezed).astype(BF16)
        high = g.astype(BF16).astype(F32)
        at = lax.broadcasted_iota(jnp.int32, (EXT, OWN), 0)
        rows = jnp.where((at == 0) | (at == 2), high, jnp.where(at == 1, g - high, 0.0))
        out[2 * RANK :, :] = rows.astype(BF16)

    return call(body, [pltpu.VMEM((2 * RANK + EXT, OWN), BF16)], (*(near(p) for p in parts), labels))[0]


def by_sample(*blocks):
    return jnp.concatenate([b[...].T for b in blocks], axis=0)


def grad_pooled_of(g, rows_ref):
    tables = [slice(y * EMBED, (y + 1) * EMBED) for y in range(NY)]
    return [dot(g, rows_ref[:, table], 1, 0).astype(BF16) for table in tables]


def by_core(low_core, value, width):
    pairs = value.reshape(-1, NC, width, value.shape[1])
    even, odd = (pairs[:, c].reshape(-1, value.shape[1]) for c in range(NC))
    return jnp.where(low_core, even, odd), jnp.where(low_core, odd, even)


def late_values(place, pooled, arrived):
    def body(place_ref, pooled_ref, in_ref, mine, theirs):
        low_core = place_ref[3] == 0
        half = COLS // NC
        mine[:half, :], theirs[:half, :] = by_core(low_core, pooled_ref[:, LATE:], 32)
        for y in range(NY):
            rows = slice(half + y * 256, half + (y + 1) * 256)
            counts = in_ref[y * 512 : (y + 1) * 512, LATE:SAMPLES]
            mine[rows, :], theirs[rows, :] = by_core(low_core, counts, ROWS)

    return call(
        body,
        [pltpu.VMEM((COLS // NC + NY * 256, SAMPLES - LATE), BF16)] * 2,
        (place, near(pooled), near(arrived)),
        [IN_SMEM] + [IN_VMEM] * 2,
        cost=pl.CostEstimate(flops=1 << 27, bytes_accessed=2 << 20, transcendentals=0),
    )


def put_weights(out, first, j, value):
    for h in range(2):
        at = first + (2 * j + h) * 32
        held = value[:, h * 128 : (h + 1) * 128].reshape(NY * NX, 32, 128)
        out(slice(0, NY * NX), slice(at, at + 32), held)


def put_sums(out, first, value):
    for y in range(NY):
        row = value[:, y * 128 : (y + 1) * 128]
        for x in range(NX):
            out(y * NX + x, slice(first, first + EXT), row)


def put_slab(out, y, value):
    for h in range(2):
        held = value[:, h * 128 : (h + 1) * 128].reshape(NX, ROWS, 128)
        out(slice(y * NX, (y + 1) * NX), slice(h * ROWS, (h + 1) * ROWS), held)


def backward_first(place, block0, block1, pooled, arrived, rows):
    def body(place_ref, b0, b1, pooled_ref, in_ref, rows_ref, mine, theirs):
        low_core = place_ref[3] == 0
        g = by_sample(b0, b1)
        products = grad_pooled_of(g, rows_ref)
        ext = jnp.concatenate([b0[2 * RANK :, :], b1[2 * RANK :, :]], axis=1)

        def writer(ref):
            def write(targets, at, value):
                ref[targets, at, :] = value.astype(ref.dtype)

            return write

        outs = [writer(mine), writer(theirs)]
        for out, part in zip(outs, by_core(low_core, pooled_ref[:, :LATE], 32)):
            for j in range(4):
                put_weights(out, 2 * ROWS, j, dot(part, g[:, j * 256 : (j + 1) * 256], 1, 0))
            put_sums(out, 384, dot(ext, part, 1, 1))
        for y, grad_pooled in enumerate(products):
            counts = in_ref[y * 512 : (y + 1) * 512, :LATE]
            for out, part in zip(outs, by_core(low_core, counts, ROWS)):
                put_slab(out, y, dot(part, grad_pooled, 1, 0))

    return call(
        body,
        [pltpu.VMEM((NY * NX, PACK, 128), F32), pltpu.VMEM((NY * NX, PACK, 128), BF16)],
        (place, *(near(v) for v in (block0, block1, pooled, arrived, rows))),
        [IN_SMEM] + [IN_VMEM] * 5,
        cost=pl.CostEstimate(flops=2 << 30, bytes_accessed=6 << 20, transcendentals=0),
    )


def late_products(block2, block3, rows):
    def body(b2, b3, rows_ref, g_out, out):
        g = by_sample(b2, b3)
        g_out[...] = g
        for y, grad_pooled in enumerate(grad_pooled_of(g, rows_ref)):
            out[:, y * EMBED : (y + 1) * EMBED] = grad_pooled

    return call(
        body,
        [pltpu.VMEM((SAMPLES - LATE, 2 * RANK + EXT), BF16), pltpu.VMEM((SAMPLES - LATE, COLS), BF16)],
        tuple(near(v) for v in (block2, block3, rows)),
        cost=pl.CostEstimate(flops=1 << 30, bytes_accessed=4 << 20, transcendentals=0),
    )


def late_weights(g, blocks, partner_blocks, values, partner_values, first, partner_first):
    def body(g_ref, b2, b3, p2, p3, own_ref, partner_ref, first_ref, other_ref, out):
        half = COLS // NC
        pooled = jnp.concatenate([own_ref[:half, :], partner_ref[:half, :]], axis=1)
        both = jnp.concatenate([g_ref[...], by_sample(p2, p3)], axis=0)

        def write(targets, at, value):
            shifted = slice(at.start + 2 * ROWS, at.stop + 2 * ROWS)
            held = first_ref[targets, shifted, :] + other_ref[targets, shifted, :].astype(F32)
            out[targets, at, :] = (held + value).astype(BF16)

        for j in range(4):
            put_weights(write, 0, j, dot(pooled, both[:, j * 256 : (j + 1) * 256], 1, 0))
        ext = jnp.concatenate([b[2 * RANK :, :] for b in (b2, b3, p2, p3)], axis=1)
        put_sums(write, 256, dot(ext, pooled, 1, 1))

    return call(
        body,
        [pltpu.VMEM((NY * NX, PACK - 2 * ROWS, 128), BF16)],
        tuple(near(v) for v in (g, *blocks, *partner_blocks, values, partner_values, first, partner_first)),
        cost=pl.CostEstimate(flops=1 << 30, bytes_accessed=4 << 20, transcendentals=0),
    )[0]


def late_slab(products, partner_products, values, partner_values, first, partner_first, weights):
    def body(own_products, their_products, own_ref, partner_ref, first_ref, other_ref, weights_ref, out):
        half = COLS // NC
        out[:, 2 * ROWS :, :] = weights_ref[...]

        def write(targets, at, value):
            held = first_ref[targets, at, :] + other_ref[targets, at, :].astype(F32)
            out[targets, at, :] = (held + value).astype(BF16)

        for y in range(NY):
            rows = slice(half + y * 256, half + (y + 1) * 256)
            table = slice(y * EMBED, (y + 1) * EMBED)
            counts = jnp.concatenate([own_ref[rows, :], partner_ref[rows, :]], axis=1)
            both = jnp.concatenate([own_products[:, table], their_products[:, table]], axis=0)
            put_slab(write, y, dot(counts, both, 1, 0))

    return call(
        body,
        [pltpu.VMEM((NY * NX, PACK, 128), BF16)],
        tuple(
            near(v)
            for v in (products, partner_products, values, partner_values, first, partner_first, weights)
        ),
        cost=pl.CostEstimate(flops=1 << 29, bytes_accessed=4 << 20, transcendentals=0),
    )[0]


def finish(shares, own, up_own):
    def body(in_ref, own_ref, up_ref, slab_out, down_out, up_out, bias_out, out_out):
        def total(at):
            held = in_ref[0, at, :].astype(F32)
            for i in range(1, NY * NX):
                held = held + in_ref[i, at, :].astype(F32)
            return held

        slab_out[:, :128] = total(slice(0, ROWS))
        slab_out[:, 128:] = total(slice(ROWS, 2 * ROWS))
        both = [total(slice(128 + j * 32, 160 + j * 32)) for j in range(8)]
        for j in range(4):
            down_out[:, j * 128 : (j + 1) * 128] = both[j].astype(BF16)
        product = jnp.concatenate(both[4:], axis=1)
        w_own, bias_own = own_ref[:, 0:1], own_ref[:, 1:2]
        up_out[...] = (product * w_own).astype(BF16)
        lane = lax.broadcasted_iota(jnp.int32, (32, 128), 1)
        row = lax.broadcasted_iota(jnp.int32, (32, 128), 0)
        last = total(slice(384, 400))
        own = lane.astype(F32) == own_ref[:, 2:3]
        sums = jnp.sum(jnp.where(own, last[0:1] + last[1:2], 0.0), axis=1, keepdims=True)
        out = (1.0 + bias_own) * sums + jnp.sum(product * up_ref[...], axis=1, keepdims=True)
        bias_out[...] = jnp.sum(jnp.where(lane == row, w_own * sums, 0.0), axis=0, keepdims=True)[:, :32]
        out_out[...] = jnp.sum(jnp.where(lane == row, out, 0.0), axis=0, keepdims=True)[:, :32]

    return call(
        body,
        [
            jax.ShapeDtypeStruct((ROWS, EMBED), F32),
            jax.ShapeDtypeStruct((32, RANK), BF16),
            jax.ShapeDtypeStruct((32, RANK), BF16),
            jax.ShapeDtypeStruct((1, 32), F32),
            jax.ShapeDtypeStruct((1, 32), F32),
        ],
        (near(shares), near(own), near(up_own)),
    )


def local(slab, counts, cross_down, cross_up, cross_bias, out_weight, labels):
    place = jnp.stack([lax.axis_index(a) for a in ALL]).astype(jnp.int32)
    w_row, bias_row = out_weight.reshape(1, -1), cross_bias.reshape(1, -1)
    rows = prepare(place, cross_down, cross_up, w_row, bias_row)
    own, up_own = prepare_own(place, cross_up, w_row, bias_row)
    sent = pack_counts(place, counts.T, slab)
    arrived = lax.all_to_all(sent, PLANE, 0, 0, tiled=True).reshape(PEERS * ROWS, SAMPLES + HALF)
    other = shift(arrived[:, SAMPLES:], dc=1)
    half = pool_half(arrived)
    pooled, chunk1, chunk2 = forward_far(place, arrived, other, half, rows)
    part2 = shift(chunk2, dz=(ORDER[0][2], ORDER[1][2]))
    part1 = shift(chunk1, dz=(ORDER[0][1], ORDER[1][1]))
    chunk3 = forward_near(pooled, rows)
    part3 = shift(chunk3, dz=(ORDER[0][3], ORDER[1][3]))
    parts = [part1, part2, part3]
    chunk = forward_own(pooled, rows)
    values, theirs = late_values(place, pooled, arrived)
    partner_values = shift(theirs, dc=1)
    block0 = own_samples([chunk] + parts, labels.reshape(1, OWN))
    blocks = []
    for i in range(1, NZ):
        blocks.append(shift(block0, dz=(-ORDER[0][i], -ORDER[1][i])))
    block1, *late = blocks
    first, theirs = backward_first(place, block0, block1, pooled, arrived, rows)
    partner_first = shift(theirs, dc=1)
    partner_late = []
    for block in late:
        partner_late.append(shift(block, dc=1))
    g, products = late_products(*late, rows)
    partner_products = shift(products, dc=1)
    weights = late_weights(g, late, partner_late, values, partner_values, first, partner_first)
    summed = late_slab(products, partner_products, values, partner_values, first, partner_first, weights)
    shares = lax.all_to_all(summed, ("y", "x"), 0, 0, tiled=True)
    grad_slab, grad_down, grad_up, grad_bias, grad_out = finish(shares, own, up_own)
    return grad_slab, grad_down, grad_up.T, grad_bias.reshape(32), grad_out.reshape(32)


def solution(mesh):
    torus = Mesh(mesh.devices.reshape(NZ, NY, NX, NC), ALL)
    return jax.shard_map(
        local,
        mesh=torus,
        in_specs=(P(ALL, None), P(None, ALL), P(), P(), P(), P(), P(ALL)),
        out_specs=(P(ALL, None), P(ALL, None), P(None, ALL), P(ALL), P(ALL)),
        check_vma=False,
    )
```

```python
import jax
import jax.numpy as jnp
from jax import lax
from jax.experimental import pallas as pl
from jax.experimental.pallas import tpu as pltpu
from jax.sharding import Mesh
from jax.sharding import PartitionSpec as P


ALL = ("z", "y", "x", "c")
PLANE = ("y", "x", "c")
NZ, NY, NX, NC = 4, 4, 4, 2
NK = NX * NC
PEERS = NY * NK
OWN = 128
ROWS = 64
EMBED = 256
RANK = 512
COLS = 1024
SAMPLES = NZ * OWN
EXT = 16
PACK = 400
HALF = EMBED // 2
LATE = SAMPLES // 2
ORDER = ((0, 2, 1, 3), (0, 2, 3, 1))
PLACES = ((0, 2, 1, 3), (0, 3, 1, 2))
F32 = jnp.float32
BF16 = jnp.bfloat16


def dot(a, b, da, db):
    return lax.dot_general(a, b, (((da,), (db,)), ((), ())), preferred_element_type=F32)


def flat(z, y, x, c):
    return (((z % NZ) * NY + y % NY) * NX + x % NX) * NC + c % NC


def shift(value, dz=(0, 0), dc=0):
    pairs = [
        (flat(z, y, x, c), flat(z + dz[c], y, x, c + dc))
        for z in range(NZ)
        for y in range(NY)
        for x in range(NX)
        for c in range(NC)
    ]
    return lax.ppermute(value, ALL, pairs)


def near(value):
    return pltpu.with_memory_space_constraint(value, pltpu.VMEM)


def far(value):
    return pltpu.with_memory_space_constraint(value, pltpu.HBM)


def call(body, outs, args, specs=None, scratch=(), mib=24, cost=None):
    return pl.pallas_call(
        body,
        in_specs=specs or [pl.BlockSpec(memory_space=pltpu.VMEM)] * len(args),
        out_specs=[pl.BlockSpec(memory_space=pltpu.VMEM)] * len(outs),
        out_shape=outs,
        scratch_shapes=list(scratch),
        compiler_params=pltpu.CompilerParams(vmem_limit_bytes=mib << 20),
        cost_estimate=cost,
    )(*args)


IN_SMEM = pl.BlockSpec(memory_space=pltpu.SMEM)
IN_VMEM = pl.BlockSpec(memory_space=pltpu.VMEM)
IN_HBM = pl.BlockSpec(memory_space=pltpu.HBM)


def pack_counts(place, counts_t, slab):
    strip = NK * OWN

    def body(place_ref, counts_ref, slab_ref, out, held, slab_s, sems, slab_sem):
        def copy(y, n):
            z = lax.rem(place_ref[0] + n, NZ)
            start = pl.multiple_of(z * (NY * strip) + y * strip, strip)
            return pltpu.make_async_copy(counts_ref.at[:, pl.ds(start, strip)], held.at[y, n], sems.at[y, n])

        slab_copy = pltpu.make_async_copy(slab_ref, slab_s, slab_sem)
        for y in range(NY):
            for n in range(NZ):
                copy(y, n).start(priority=n % 2)
        slab_copy.start()
        slab_copy.wait()
        for k in range(PEERS):
            half = k % NC
            out[k, :, SAMPLES:] = slab_s[:, half * HALF : (half + 1) * HALF]
        for y in range(NY):
            for n in range(NZ):
                copy(y, n).wait()
                for k in range(NK):
                    to = PLACES[k % NC][n] * OWN
                    out[y * NK + k, :, to : to + OWN] = (
                        held[y, n, :, k * OWN : (k + 1) * OWN].astype(F32).astype(BF16)
                    )

    return call(
        body,
        [pltpu.VMEM((PEERS, ROWS, SAMPLES + HALF), BF16)],
        (place, far(counts_t), far(slab)),
        [IN_SMEM, IN_HBM, IN_HBM],
        [
            pltpu.VMEM((NY, NZ, ROWS, strip), jnp.int32),
            pltpu.VMEM((ROWS, EMBED), BF16),
            pltpu.SemaphoreType.DMA((NY, NZ)),
            pltpu.SemaphoreType.DMA,
        ],
    )[0]


def prepare(place, down, up, w, bias):
    def body(place_ref, down_ref, up_ref, w_ref, bias_ref, rows_out):
        here = pl.ds(pl.multiple_of(place_ref[0] * COLS, COLS), COLS)
        w = w_ref[:, here]
        for part in range(4):
            at = slice(part * 128, (part + 1) * 128)
            rows_out[at, :] = down_ref[here, at].T
        rows_out[RANK : 2 * RANK, :] = (up_ref[:, here].astype(F32) * w).astype(BF16)
        v = w * (1.0 + bias_ref[:, here])
        high = v.astype(BF16).astype(F32)
        at = lax.broadcasted_iota(jnp.int32, (EXT, COLS), 0)
        rows_out[2 * RANK :, :] = jnp.where(at < 2, high, jnp.where(at == 2, v - high, 0.0)).astype(BF16)

    return call(
        body,
        [pltpu.VMEM((2 * RANK + EXT, COLS), BF16)],
        (place, *(near(v) for v in (down, up, w, bias))),
        [IN_SMEM] + [IN_VMEM] * 4,
        cost=pl.CostEstimate(flops=1 << 29, bytes_accessed=6 << 20, transcendentals=0),
    )[0]


def prepare_own(place, up, w, bias):
    def body(place_ref, up_ref, w_ref, bias_ref, own_out, up_out):
        k = place_ref[2] * NC + place_ref[3]
        start = place_ref[0] * COLS + (place_ref[1] * 2 + lax.div(k, 4)) * 128
        strip = pl.ds(pl.multiple_of(start, 128), 128)
        offset = lax.rem(k, 4) * 32
        lane = lax.broadcasted_iota(jnp.int32, (32, 128), 1)
        row = lax.broadcasted_iota(jnp.int32, (32, 128), 0)
        own = lane == row + offset
        w_own = jnp.sum(jnp.where(own, w_ref[:, strip], 0.0), axis=1, keepdims=True)
        bias_own = jnp.sum(jnp.where(own, bias_ref[:, strip], 0.0), axis=1, keepdims=True)
        place_own = (row + place_ref[2] * 32).astype(F32)
        own_out[...] = jnp.where(lane == 0, w_own, jnp.where(lane == 1, bias_own, place_own))
        up_out[...] = dot(jnp.where(own, 1.0, 0.0).astype(BF16), up_ref[:, strip], 1, 1)

    return call(
        body,
        [pltpu.VMEM((32, 128), F32), pltpu.VMEM((32, RANK), F32)],
        (place, *(near(v) for v in (up, w, bias))),
        [IN_SMEM] + [IN_VMEM] * 3,
        cost=pl.CostEstimate(flops=1 << 27, bytes_accessed=1 << 20, transcendentals=0),
    )


def pool_half(arrived):
    def body(in_ref, pooled_ref):
        for y in range(NY):
            at = slice(y * 512, (y + 1) * 512)
            half = slice(y * HALF, (y + 1) * HALF)
            pooled_ref[half, :] = dot(in_ref[at, SAMPLES:].T, in_ref[at, :SAMPLES], 1, 0).astype(BF16)

    return call(
        body,
        [pltpu.VMEM((NY * HALF, SAMPLES), BF16)],
        (near(arrived),),
        cost=pl.CostEstimate(flops=1 << 29, bytes_accessed=2 << 20, transcendentals=0),
    )[0]


def head_of(rows_ref, pooled):
    head = dot(rows_ref[2 * RANK :, :], pooled, 1, 0)
    sums = head[0:1] + head[2:3]
    high = sums.astype(BF16).astype(F32)
    at = lax.broadcasted_iota(jnp.int32, (EXT, pooled.shape[1]), 0)
    return jnp.where(at == 0, high, jnp.where(at == 1, sums - high, 0.0)).astype(BF16)


def products(rows_ref, pooled, outs):
    for part in range(4):
        at = slice(part * 256, (part + 1) * 256)
        product = dot(rows_ref[at, :], pooled, 1, 0).astype(BF16)
        for i, out in enumerate(outs):
            out[at, :] = product[:, i * OWN : (i + 1) * OWN]
    ext = head_of(rows_ref, pooled)
    for i, out in enumerate(outs):
        out[2 * RANK :, :] = ext[:, i * OWN : (i + 1) * OWN]


def forward_far(place, arrived, other, half, rows):
    def body(place_ref, in_ref, other_ref, half_ref, rows_ref, pooled_ref, out):
        core = place_ref[3]
        for y in range(NY):
            at = slice(y * 512, (y + 1) * 512)
            mine = pl.multiple_of(y * EMBED + core * HALF, HALF)
            partners = pl.multiple_of(y * EMBED + (1 - core) * HALF, HALF)
            pooled_ref[pl.ds(mine, HALF), :] = half_ref[y * HALF : (y + 1) * HALF, :]
            pooled_ref[pl.ds(partners, HALF), :] = dot(
                other_ref[at, :].T, in_ref[at, :SAMPLES], 1, 0
            ).astype(BF16)
        products(rows_ref, pooled_ref[:, 2 * OWN : 3 * OWN], (out,))

    return call(
        body,
        [pltpu.VMEM((COLS, SAMPLES), BF16), pltpu.VMEM((2 * RANK + EXT, OWN), BF16)],
        (place, near(arrived), near(other), near(half), near(rows)),
        [IN_SMEM] + [IN_VMEM] * 4,
        cost=pl.CostEstimate(flops=3 << 30, bytes_accessed=4 << 20, transcendentals=0),
    )


def forward_near(pooled, rows):
    def body(pooled_ref, rows_ref, *outs):
        ends = [pooled_ref[:, OWN : 2 * OWN], pooled_ref[:, 3 * OWN :]]
        products(rows_ref, jnp.concatenate(ends, axis=1), outs)

    return call(
        body,
        [pltpu.VMEM((2 * RANK + EXT, OWN), BF16)] * 2,
        (near(pooled), near(rows)),
        cost=pl.CostEstimate(flops=1 << 30, bytes_accessed=2 << 20, transcendentals=0),
    )


def forward_own(pooled, rows):
    def body(pooled_ref, rows_ref, out):
        products(rows_ref, pooled_ref[:, :OWN], (out,))

    return call(
        body,
        [pltpu.VMEM((2 * RANK + EXT, OWN), BF16)],
        (near(pooled), near(rows)),
        cost=pl.CostEstimate(flops=1 << 30, bytes_accessed=1 << 20, transcendentals=0),
    )[0]


def own_samples(parts, labels):
    def body(p0, p1, p2, p3, labels_ref, out):
        def total(rows):
            a, b, c, d = (p[rows, :].astype(F32) for p in (p0, p1, p2, p3))
            return (a + b) + (c + d)

        squeezed = total(slice(0, RANK)).astype(BF16).astype(F32)
        other = total(slice(RANK, 2 * RANK))
        ext = total(slice(2 * RANK, 2 * RANK + EXT))
        logits = ext[0:1] + ext[1:2] + jnp.sum(squeezed * other, axis=0, keepdims=True)
        g = jax.nn.sigmoid(logits) - labels_ref[...].astype(F32)
        out[0:RANK, :] = (g * other).astype(BF16)
        out[RANK : 2 * RANK, :] = (g * squeezed).astype(BF16)
        high = g.astype(BF16).astype(F32)
        at = lax.broadcasted_iota(jnp.int32, (EXT, OWN), 0)
        rows = jnp.where((at == 0) | (at == 2), high, jnp.where(at == 1, g - high, 0.0))
        out[2 * RANK :, :] = rows.astype(BF16)

    return call(body, [pltpu.VMEM((2 * RANK + EXT, OWN), BF16)], (*(near(p) for p in parts), labels))[0]


def by_sample(*blocks):
    return jnp.concatenate([b[...].T for b in blocks], axis=0)


def grad_pooled_of(g, rows_ref):
    tables = [slice(y * EMBED, (y + 1) * EMBED) for y in range(NY)]
    return [dot(g, rows_ref[:, table], 1, 0).astype(BF16) for table in tables]


def by_core(low_core, value, width):
    pairs = value.reshape(-1, NC, width, value.shape[1])
    even, odd = (pairs[:, c].reshape(-1, value.shape[1]) for c in range(NC))
    return jnp.where(low_core, even, odd), jnp.where(low_core, odd, even)


def late_values(place, pooled, arrived):
    def body(place_ref, pooled_ref, in_ref, mine, theirs):
        low_core = place_ref[3] == 0
        half = COLS // NC
        mine[:half, :], theirs[:half, :] = by_core(low_core, pooled_ref[:, LATE:], 32)
        for y in range(NY):
            rows = slice(half + y * 256, half + (y + 1) * 256)
            counts = in_ref[y * 512 : (y + 1) * 512, LATE:SAMPLES]
            mine[rows, :], theirs[rows, :] = by_core(low_core, counts, ROWS)

    return call(
        body,
        [pltpu.VMEM((COLS // NC + NY * 256, SAMPLES - LATE), BF16)] * 2,
        (place, near(pooled), near(arrived)),
        [IN_SMEM] + [IN_VMEM] * 2,
        cost=pl.CostEstimate(flops=1 << 27, bytes_accessed=2 << 20, transcendentals=0),
    )


def put_weights(out, first, j, value):
    for h in range(2):
        at = first + (2 * j + h) * 32
        held = value[:, h * 128 : (h + 1) * 128].reshape(NY * NX, 32, 128)
        out(slice(0, NY * NX), slice(at, at + 32), held)


def put_sums(out, first, value):
    for y in range(NY):
        row = value[:, y * 128 : (y + 1) * 128]
        for x in range(NX):
            out(y * NX + x, slice(first, first + EXT), row)


def put_slab(out, y, value):
    for h in range(2):
        held = value[:, h * 128 : (h + 1) * 128].reshape(NX, ROWS, 128)
        out(slice(y * NX, (y + 1) * NX), slice(h * ROWS, (h + 1) * ROWS), held)


def backward_first(place, block0, block1, pooled, arrived, rows):
    def body(place_ref, b0, b1, pooled_ref, in_ref, rows_ref, mine, theirs):
        low_core = place_ref[3] == 0
        g = by_sample(b0, b1)
        products = grad_pooled_of(g, rows_ref)
        ext = jnp.concatenate([b0[2 * RANK :, :], b1[2 * RANK :, :]], axis=1)

        def writer(ref):
            def write(targets, at, value):
                ref[targets, at, :] = value.astype(ref.dtype)

            return write

        outs = [writer(mine), writer(theirs)]
        for out, part in zip(outs, by_core(low_core, pooled_ref[:, :LATE], 32)):
            for j in range(4):
                put_weights(out, 2 * ROWS, j, dot(part, g[:, j * 256 : (j + 1) * 256], 1, 0))
            put_sums(out, 384, dot(ext, part, 1, 1))
        for y, grad_pooled in enumerate(products):
            counts = in_ref[y * 512 : (y + 1) * 512, :LATE]
            for out, part in zip(outs, by_core(low_core, counts, ROWS)):
                put_slab(out, y, dot(part, grad_pooled, 1, 0))

    return call(
        body,
        [pltpu.VMEM((NY * NX, PACK, 128), F32), pltpu.VMEM((NY * NX, PACK, 128), BF16)],
        (place, *(near(v) for v in (block0, block1, pooled, arrived, rows))),
        [IN_SMEM] + [IN_VMEM] * 5,
        cost=pl.CostEstimate(flops=2 << 30, bytes_accessed=6 << 20, transcendentals=0),
    )


def late_products(block2, block3, rows):
    def body(b2, b3, rows_ref, g_out, out):
        g = by_sample(b2, b3)
        g_out[...] = g
        for y, grad_pooled in enumerate(grad_pooled_of(g, rows_ref)):
            out[:, y * EMBED : (y + 1) * EMBED] = grad_pooled

    return call(
        body,
        [pltpu.VMEM((SAMPLES - LATE, 2 * RANK + EXT), BF16), pltpu.VMEM((SAMPLES - LATE, COLS), BF16)],
        tuple(near(v) for v in (block2, block3, rows)),
        cost=pl.CostEstimate(flops=1 << 30, bytes_accessed=4 << 20, transcendentals=0),
    )


def late_weights(g, blocks, partner_blocks, values, partner_values, first, partner_first):
    def body(g_ref, b2, b3, p2, p3, own_ref, partner_ref, first_ref, other_ref, out):
        half = COLS // NC
        pooled = jnp.concatenate([own_ref[:half, :], partner_ref[:half, :]], axis=1)
        both = jnp.concatenate([g_ref[...], by_sample(p2, p3)], axis=0)

        def write(targets, at, value):
            shifted = slice(at.start + 2 * ROWS, at.stop + 2 * ROWS)
            held = first_ref[targets, shifted, :] + other_ref[targets, shifted, :].astype(F32)
            out[targets, at, :] = (held + value).astype(BF16)

        for j in range(4):
            put_weights(write, 0, j, dot(pooled, both[:, j * 256 : (j + 1) * 256], 1, 0))
        ext = jnp.concatenate([b[2 * RANK :, :] for b in (b2, b3, p2, p3)], axis=1)
        put_sums(write, 256, dot(ext, pooled, 1, 1))

    return call(
        body,
        [pltpu.VMEM((NY * NX, PACK - 2 * ROWS, 128), BF16)],
        tuple(near(v) for v in (g, *blocks, *partner_blocks, values, partner_values, first, partner_first)),
        cost=pl.CostEstimate(flops=1 << 30, bytes_accessed=4 << 20, transcendentals=0),
    )[0]


def late_slab(products, partner_products, values, partner_values, first, partner_first, weights):
    def body(own_products, their_products, own_ref, partner_ref, first_ref, other_ref, weights_ref, out):
        half = COLS // NC
        out[:, 2 * ROWS :, :] = weights_ref[...]

        def write(targets, at, value):
            held = first_ref[targets, at, :] + other_ref[targets, at, :].astype(F32)
            out[targets, at, :] = (held + value).astype(BF16)

        for y in range(NY):
            rows = slice(half + y * 256, half + (y + 1) * 256)
            table = slice(y * EMBED, (y + 1) * EMBED)
            counts = jnp.concatenate([own_ref[rows, :], partner_ref[rows, :]], axis=1)
            both = jnp.concatenate([own_products[:, table], their_products[:, table]], axis=0)
            put_slab(write, y, dot(counts, both, 1, 0))

    return call(
        body,
        [pltpu.VMEM((NY * NX, PACK, 128), BF16)],
        tuple(
            near(v)
            for v in (products, partner_products, values, partner_values, first, partner_first, weights)
        ),
        cost=pl.CostEstimate(flops=1 << 29, bytes_accessed=4 << 20, transcendentals=0),
    )[0]


def finish(shares, own, up_own):
    def body(in_ref, own_ref, up_ref, slab_out, down_out, up_out, bias_out, out_out):
        def total(at):
            held = [(in_ref[i, at, :] + in_ref[i + 1, at, :]).astype(F32) for i in range(0, NY * NX, 2)]
            while len(held) > 1:
                held = [a + b for a, b in zip(held[::2], held[1::2])]
            return held[0]

        slab_out[:, :128] = total(slice(0, ROWS))
        slab_out[:, 128:] = total(slice(ROWS, 2 * ROWS))
        both = [total(slice(128 + j * 32, 160 + j * 32)) for j in range(8)]
        for j in range(4):
            down_out[:, j * 128 : (j + 1) * 128] = both[j].astype(BF16)
        product = jnp.concatenate(both[4:], axis=1)
        w_own, bias_own = own_ref[:, 0:1], own_ref[:, 1:2]
        up_out[...] = (product * w_own).astype(BF16)
        lane = lax.broadcasted_iota(jnp.int32, (32, 128), 1)
        row = lax.broadcasted_iota(jnp.int32, (32, 128), 0)
        last = total(slice(384, 400))
        own = lane.astype(F32) == own_ref[:, 2:3]
        sums = jnp.sum(jnp.where(own, last[0:1] + last[1:2], 0.0), axis=1, keepdims=True)
        out = (1.0 + bias_own) * sums + jnp.sum(product * up_ref[...], axis=1, keepdims=True)
        bias_out[...] = jnp.sum(jnp.where(lane == row, w_own * sums, 0.0), axis=0, keepdims=True)[:, :32]
        out_out[...] = jnp.sum(jnp.where(lane == row, out, 0.0), axis=0, keepdims=True)[:, :32]

    return call(
        body,
        [
            jax.ShapeDtypeStruct((ROWS, EMBED), F32),
            jax.ShapeDtypeStruct((32, RANK), BF16),
            jax.ShapeDtypeStruct((32, RANK), BF16),
            jax.ShapeDtypeStruct((1, 32), F32),
            jax.ShapeDtypeStruct((1, 32), F32),
        ],
        (near(shares), near(own), near(up_own)),
    )


def local(slab, counts, cross_down, cross_up, cross_bias, out_weight, labels):
    place = jnp.stack([lax.axis_index(a) for a in ALL]).astype(jnp.int32)
    w_row, bias_row = out_weight.reshape(1, -1), cross_bias.reshape(1, -1)
    rows = prepare(place, cross_down, cross_up, w_row, bias_row)
    own, up_own = prepare_own(place, cross_up, w_row, bias_row)
    sent = pack_counts(place, counts.T, slab)
    arrived = lax.all_to_all(sent, PLANE, 0, 0, tiled=True).reshape(PEERS * ROWS, SAMPLES + HALF)
    other = shift(arrived[:, SAMPLES:], dc=1)
    half = pool_half(arrived)
    pooled, chunk2 = forward_far(place, arrived, other, half, rows)
    part2 = shift(chunk2, dz=(ORDER[0][2], ORDER[1][2]))
    chunk1, chunk3 = forward_near(pooled, rows)
    part1 = shift(chunk1, dz=(ORDER[0][1], ORDER[1][1]))
    part3 = shift(chunk3, dz=(ORDER[0][3], ORDER[1][3]))
    parts = [part1, part2, part3]
    chunk = forward_own(pooled, rows)
    values, theirs = late_values(place, pooled, arrived)
    partner_values = shift(theirs, dc=1)
    block0 = own_samples([chunk] + parts, labels.reshape(1, OWN))
    blocks = []
    for i in range(1, NZ):
        blocks.append(shift(block0, dz=(-ORDER[0][i], -ORDER[1][i])))
    block1, *late = blocks
    first, theirs = backward_first(place, block0, block1, pooled, arrived, rows)
    partner_first = shift(theirs, dc=1)
    partner_late = []
    for block in late:
        partner_late.append(shift(block, dc=1))
    g, products = late_products(*late, rows)
    partner_products = shift(products, dc=1)
    weights = late_weights(g, late, partner_late, values, partner_values, first, partner_first)
    summed = late_slab(products, partner_products, values, partner_values, first, partner_first, weights)
    shares = lax.all_to_all(summed, ("y", "x"), 0, 0, tiled=True)
    grad_slab, grad_down, grad_up, grad_bias, grad_out = finish(shares, own, up_own)
    return grad_slab, grad_down, grad_up.T, grad_bias.reshape(32), grad_out.reshape(32)


def solution(mesh):
    torus = Mesh(mesh.devices.reshape(NZ, NY, NX, NC), ALL)
    return jax.shard_map(
        local,
        mesh=torus,
        in_specs=(P(ALL, None), P(None, ALL), P(), P(), P(), P(), P(ALL)),
        out_specs=(P(ALL, None), P(ALL, None), P(None, ALL), P(ALL), P(ALL)),
        check_vma=False,
    )
```
